32 devices in a mesh: seq: 4 (over z), fsdp: 8 (over y, x, core).
Axes of the slice: x: 2, y: 2, z: 4, core: 2. Of those that a mesh axis runs over, the one named last changes fastest.
Arguments:
- layer_input: bfloat16 [16, 512, 768], P('fsdp', 'seq'), may hold values from -20 to 20
- cotangent: bfloat16 [16, 512, 768], P('fsdp', 'seq'), may hold values from -6 to 6
- lengths: int32 [16], P('fsdp'), may hold values from 64 to 512, as said below
- project_weight: float32 [768, 2304], P('fsdp'), may hold values from -0.0625 to 0.0625
- output_weight: float32 [768, 768], P('fsdp'), may hold values from -2.5 to 2.5
- up_weight: float32 [768, 3072], P('fsdp'), may hold values from -0.21875 to 0.21875
- down_weight: float32 [3072, 768], P('fsdp'), may hold values from -0.109375 to 0.109375
- norm_gains: float32 [2, 768], P(None, 'fsdp'), may hold values from 0.5 to 1.5
- biases: float32 [6, 768], P(None, 'fsdp'), may hold values from -3 to 3
- hidden_bias: float32 [3072], P('fsdp'), may hold values from -3 to 3
- first_project: float32 [768, 2304], P('fsdp'), may hold values from -28 to 28
- first_output: float32 [768, 768], P('fsdp'), may hold values from -28 to 28
- first_up: float32 [768, 3072], P('fsdp'), may hold values from -28 to 28
- first_down: float32 [3072, 768], P('fsdp'), may hold values from -28 to 28
- first_gains: float32 [2, 768], P(None, 'fsdp'), may hold values from -28 to 28
- first_biases: float32 [6, 768], P(None, 'fsdp'), may hold values from -28 to 28
- first_hidden: float32 [3072], P('fsdp'), may hold values from -28 to 28
- second_project: float32 [768, 2304], P('fsdp'), may hold values from 1.6384 to 16.384
- second_output: float32 [768, 768], P('fsdp'), may hold values from 1.6384 to 16.384
- second_up: float32 [768, 3072], P('fsdp'), may hold values from 1.6384 to 16.384
- second_down: float32 [3072, 768], P('fsdp'), may hold values from 1.6384 to 16.384
- second_gains: float32 [2, 768], P(None, 'fsdp'), may hold values from 1.6384 to 16.384
- second_biases: float32 [6, 768], P(None, 'fsdp'), may hold values from 1.6384 to 16.384
- second_hidden: float32 [3072], P('fsdp'), may hold values from 1.6384 to 16.384
Outputs:
- block_output: bfloat16 [16, 512, 768], P('fsdp', 'seq')
- input_gradient: bfloat16 [16, 512, 768], P('fsdp', 'seq')
- project_gradient: float32 [768, 2304], P('fsdp')
- output_gradient: float32 [768, 768], P('fsdp')
- up_gradient: float32 [768, 3072], P('fsdp')
- down_gradient: float32 [3072, 768], P('fsdp')
- gains_gradient: float32 [2, 768], P(None, 'fsdp')
- biases_gradient: float32 [6, 768], P(None, 'fsdp')
- hidden_gradient: float32 [3072], P('fsdp')
- project_new: float32 [768, 2304], P('fsdp')
- output_new: float32 [768, 768], P('fsdp')
- up_new: float32 [768, 3072], P('fsdp')
- down_new: float32 [3072, 768], P('fsdp')
- gains_new: float32 [2, 768], P(None, 'fsdp')
- biases_new: float32 [6, 768], P(None, 'fsdp')
- hidden_new: float32 [3072], P('fsdp')
- first_project_new: float32 [768, 2304], P('fsdp')
- first_output_new: float32 [768, 768], P('fsdp')
- first_up_new: float32 [768, 3072], P('fsdp')
- first_down_new: float32 [3072, 768], P('fsdp')
- first_gains_new: float32 [2, 768], P(None, 'fsdp')
- first_biases_new: float32 [6, 768], P(None, 'fsdp')
- first_hidden_new: float32 [3072], P('fsdp')
- second_project_new: float32 [768, 2304], P('fsdp')
- second_output_new: float32 [768, 768], P('fsdp')
- second_up_new: float32 [768, 3072], P('fsdp')
- second_down_new: float32 [3072, 768], P('fsdp')
- second_gains_new: float32 [2, 768], P(None, 'fsdp')
- second_biases_new: float32 [6, 768], P(None, 'fsdp')
- second_hidden_new: float32 [3072], P('fsdp')
The draws below stay inside these ranges and needn't reach their ends.
Inputs may be any that keep to these rules, and one draw needn't show every extreme that they name: Positions at and after lengths[s] of sequence s are padding keys; some sequence has all 512 positions real.
All inputs are finite; a program needn't handle non-finite values.
Results may differ from the reference program's by a relative error of at most 0.023.
The reference program's roundings to bfloat16 on the way count: a program that leaves them out, or rounds other values in their place, can miss the bound.
Values may be sent and summed in bfloat16 or wider, within the bound.
No kernel may reach another device: no remote copies, remote signals or barrier semaphores. Data moves between devices by JAX's collectives and lax.ppermute only.
A program may use at most 128 MiB of HBM per device.

```python
import math
import jax
import jax.numpy as jnp
from jax import lax

D = 768
HD = 64
FF = 3072
L = 512
ADAM_STEP = 3
SEQS = 16
TOKENS = 8192


def draw_layer_input(key, part):
    return jnp.clip(jax.random.normal(key, (SEQS, L, D), jnp.float32), -5.0, 5.0).astype(jnp.bfloat16)


def draw_project_weight(key, part):
    values = jax.random.uniform(key, (D, 3 * D), jnp.float32, -0.0625, 0.0625)
    return values


def draw_lengths(key, part):
    values = jax.random.randint(key, (SEQS,), L // 8, L + 1)
    return values.at[0].set(L).at[SEQS - 1].set(L // 8)


def level_of(own_key, shape, cuts, least, high):
    level, own = 1.0, jax.random.fold_in(own_key, 6)
    for axis_at, parts in cuts:
        steps = jnp.exp(jax.random.uniform(jax.random.fold_in(own, axis_at), (parts,), jnp.float32, least / len(cuts), high / len(cuts)))
        level = level * jnp.repeat(steps, shape[axis_at] // parts).reshape([-1 if axis == axis_at else 1 for axis in range(len(shape))])
    return level


def gaussian(own_key, shape, scale, reach, cuts=(), kind=jnp.bfloat16):
    array = jax.random.normal(own_key, shape, jnp.float32) * scale
    if len(cuts) > 0:
        array = level_of(own_key, shape, cuts, -0.22, 0.18) * array
    return jnp.clip(array, min=-reach, max=reach).astype(kind)


def setup_inputs(seed: int = 0) -> dict:
    splits = jax.random.split(jax.random.key(seed), 25)
    return {
        "layer_input": draw_layer_input(jax.random.fold_in(splits[24], 71), 0),
        "cotangent": gaussian(splits[1], (SEQS, L, D), 1.0, 6.0, ((0, 8), (1, 4))),
        "lengths": draw_lengths(jax.random.fold_in(splits[24], 71), 0),
        "project_weight": draw_project_weight(jax.random.fold_in(splits[24], 71), 0),
        "output_weight": gaussian(splits[4], (D, D), (max(D * 4 // L, 1)) ** -0.5, 2.5, ((0, 8),), jnp.float32),
        "up_weight": gaussian(splits[5], (D, FF), D ** -0.5, 0.21875, ((0, 8),), jnp.float32),
        "down_weight": gaussian(splits[6], (FF, D), FF ** -0.5, 0.109375, ((0, 8),), jnp.float32),
        "norm_gains": jnp.clip(1.0 + 0.1 * jax.random.normal(splits[7], (2, D), jnp.float32), 0.5, 1.5),
        "biases": gaussian(splits[8], (6, D), 0.5, 3.0, ((1, 8),), jnp.float32),
        "hidden_bias": gaussian(splits[9], (FF,), 0.5, 3.0, ((0, 8),), jnp.float32),
        "first_project": gaussian(splits[10], (D, 3 * D), (0.05 * TOKENS ** 0.5), 28.0, ((0, 8),), jnp.float32),
        "first_output": gaussian(splits[11], (D, D), (0.05 * TOKENS ** 0.5), 28.0, ((0, 8),), jnp.float32),
        "first_up": gaussian(splits[12], (D, FF), (0.05 * TOKENS ** 0.5), 28.0, ((0, 8),), jnp.float32),
        "first_down": gaussian(splits[13], (FF, D), (0.05 * TOKENS ** 0.5), 28.0, ((0, 8),), jnp.float32),
        "first_gains": gaussian(splits[14], (2, D), (0.05 * TOKENS ** 0.5), 28.0, ((1, 8),), jnp.float32),
        "first_biases": gaussian(splits[15], (6, D), (0.05 * TOKENS ** 0.5), 28.0, ((1, 8),), jnp.float32),
        "first_hidden": gaussian(splits[16], (FF,), (0.05 * TOKENS ** 0.5), 28.0, ((0, 8),), jnp.float32),
        "second_project": jnp.clip(jnp.exp(math.log(16.384) - 2.3025852 * jax.random.uniform(splits[17], (D, 3 * D), jnp.float32) ** level_of(splits[17], (D, 3 * D), ((0, 8),), -0.2, 0.2)), 1.6384, 16.384),
        "second_output": jnp.clip(jnp.exp(math.log(16.384) - 2.3025852 * jax.random.uniform(splits[18], (D, D), jnp.float32) ** level_of(splits[18], (D, D), ((0, 8),), -0.2, 0.2)), 1.6384, 16.384),
        "second_up": jnp.clip(jnp.exp(math.log(16.384) - 2.3025852 * jax.random.uniform(splits[19], (D, FF), jnp.float32) ** level_of(splits[19], (D, FF), ((0, 8),), -0.2, 0.2)), 1.6384, 16.384),
        "second_down": jnp.clip(jnp.exp(math.log(16.384) - 2.3025852 * jax.random.uniform(splits[20], (FF, D), jnp.float32) ** level_of(splits[20], (FF, D), ((0, 8),), -0.2, 0.2)), 1.6384, 16.384),
        "second_gains": jnp.clip(jnp.exp(math.log(16.384) - 2.3025852 * jax.random.uniform(splits[21], (2, D), jnp.float32) ** level_of(splits[21], (2, D), ((1, 8),), -0.2, 0.2)), 1.6384, 16.384),
        "second_biases": jnp.clip(jnp.exp(math.log(16.384) - 2.3025852 * jax.random.uniform(splits[22], (6, D), jnp.float32) ** level_of(splits[22], (6, D), ((1, 8),), -0.2, 0.2)), 1.6384, 16.384),
        "second_hidden": jnp.clip(jnp.exp(math.log(16.384) - 2.3025852 * jax.random.uniform(splits[23], (FF,), jnp.float32) ** level_of(splits[23], (FF,), ((0, 8),), -0.2, 0.2)), 1.6384, 16.384),
    }


beta_one = 0.9
beta_two = 0.999
learn_rate = 0.01
decay_rate = 0.01
adam_eps = 1e-08
norm_eps = 1e-05
half_root = 0.7071067811865476
gauss_peak = 0.3989422804014327

def layer_norm(summed, gain, shift):
    centred = summed - lax.optimization_barrier(jnp.mean(summed, axis=-1, keepdims=True))
    spread = lax.optimization_barrier(jnp.mean(centred * centred, axis=-1, keepdims=True))
    recip = lax.rsqrt(spread + norm_eps)
    normed = centred * recip
    return (normed * gain + shift, normed, recip)

def norm_back(upstream, normed, recip, gain):
    scaled = upstream * gain
    return recip * (scaled - lax.optimization_barrier(jnp.mean(scaled, axis=-1, keepdims=True)) - normed * lax.optimization_barrier(jnp.mean(scaled * normed, axis=-1, keepdims=True)))

def gelu_exact(pre_act):
    return 0.5 * pre_act * (1.0 + lax.erf(pre_act * half_root))

def gelu_slope(pre_act):
    return 0.5 * (1.0 + lax.erf(pre_act * half_root)) + pre_act * jnp.exp(-0.5 * pre_act * pre_act) * gauss_peak

def to_half(values):
    return lax.optimization_barrier(values.astype(jnp.bfloat16)).astype(jnp.float32)

def score_block(query_block, key_block, length):
    scores = jnp.einsum('qhd,khd->hqk', query_block.astype(jnp.float32), key_block.astype(jnp.float32)) * HD ** (-0.5)
    allowed = jnp.arange(key_block.shape[0])[None, None, :] < length
    return (scores, allowed)

def attend_forward(query_block, key_block, value_block, length):
    scores, allowed = score_block(query_block, key_block, length)
    masked = jnp.where(allowed, scores, -jnp.inf)
    row_max = lax.optimization_barrier(jnp.max(masked, axis=-1, keepdims=True))
    lifted = jnp.exp(masked - row_max)
    row_total = lax.optimization_barrier(jnp.sum(lifted, axis=-1, keepdims=True))
    weights16 = to_half(lifted / row_total)
    context = jnp.einsum('hqk,khd->qhd', weights16, value_block.astype(jnp.float32))
    token_count = query_block.shape[0]
    return (context.reshape(token_count, -1).astype(jnp.bfloat16), (row_max + jnp.log(row_total))[:, :, 0])

def attend_backward(query_block, key_block, value_block, context16, log_total, dcontext16, length):
    token_count = query_block.shape[0]
    scores, allowed = score_block(query_block, key_block, length)
    attention = jnp.where(allowed, jnp.exp(scores - log_total[:, :, None]), 0.0)
    weights16 = to_half(attention)
    upstream = dcontext16.astype(jnp.float32).reshape(token_count, -1, HD)
    kept = context16.astype(jnp.float32).reshape(token_count, -1, HD)
    value_grad = jnp.einsum('hqk,qhd->khd', weights16, upstream)
    prob_grad = jnp.einsum('qhd,khd->hqk', upstream, value_block.astype(jnp.float32))
    offset = lax.optimization_barrier(jnp.sum(upstream * kept, axis=-1))
    score_grad = attention * (prob_grad - jnp.transpose(offset)[:, :, None])
    score16 = to_half(score_grad * HD ** (-0.5))
    query_grad = jnp.einsum('hqk,khd->qhd', score16, key_block.astype(jnp.float32))
    key_grad = jnp.einsum('hqk,qhd->khd', score16, query_block.astype(jnp.float32))
    stacked = jnp.stack([query_grad.reshape(token_count, -1), key_grad.reshape(token_count, -1), value_grad.reshape(token_count, -1)], axis=1)
    return stacked.astype(jnp.bfloat16)

def sequence_pass(params16, tokens16, upstream16, length):
    project16, output16, up16, down16, gains16, biases16, hidden16 = params16
    gain_rows = gains16.astype(jnp.float32)
    bias_rows = biases16.astype(jnp.float32)
    hidden_row = hidden16.astype(jnp.float32)
    token_count, model_width = tokens16.shape
    shift = jnp.concatenate([bias_rows[0], jnp.zeros_like(bias_rows[0]), bias_rows[1]])
    packed = (jnp.dot(tokens16, project16, preferred_element_type=jnp.float32) + shift).astype(jnp.bfloat16)
    packed = packed.reshape(token_count, 3, -1, HD)
    query_block, key_block, value_block = (packed[:, 0], packed[:, 1], packed[:, 2])
    context16, log_total = attend_forward(query_block, key_block, value_block, length)
    inner_sum = tokens16.astype(jnp.float32) + jnp.dot(context16, output16, preferred_element_type=jnp.float32) + bias_rows[2]
    after_attend, norm_one, recip_one = layer_norm(inner_sum, gain_rows[0], bias_rows[3])
    after_attend16 = after_attend.astype(jnp.bfloat16)
    pre_act = jnp.dot(after_attend16, up16, preferred_element_type=jnp.float32) + hidden_row
    activated16 = gelu_exact(pre_act).astype(jnp.bfloat16)
    outer_sum = after_attend + jnp.dot(activated16, down16, preferred_element_type=jnp.float32) + bias_rows[4]
    final, norm_two, recip_two = layer_norm(outer_sum, gain_rows[1], bias_rows[5])
    upstream = upstream16.astype(jnp.float32)
    grad_outer = norm_back(upstream, norm_two, recip_two, gain_rows[1])
    grad_outer16 = grad_outer.astype(jnp.bfloat16)
    grad_pre = jnp.dot(grad_outer16, down16.T, preferred_element_type=jnp.float32) * gelu_slope(pre_act)
    grad_pre16 = grad_pre.astype(jnp.bfloat16)
    grad_middle = grad_outer + jnp.dot(grad_pre16, up16.T, preferred_element_type=jnp.float32)
    grad_inner = norm_back(grad_middle, norm_one, recip_one, gain_rows[0])
    grad_inner16 = grad_inner.astype(jnp.bfloat16)
    grad_context16 = jnp.dot(grad_inner16, output16.T, preferred_element_type=jnp.float32).astype(jnp.bfloat16)
    packed_grad = attend_backward(query_block, key_block, value_block, context16, log_total, grad_context16, length)
    packed_grad = packed_grad.reshape(token_count, 3 * model_width)
    input_grad = (grad_inner + jnp.dot(packed_grad, project16.T, preferred_element_type=jnp.float32)).astype(jnp.bfloat16)
    project_grad = jnp.dot(tokens16.T, packed_grad, preferred_element_type=jnp.float32)
    output_grad = jnp.dot(context16.T, grad_inner16, preferred_element_type=jnp.float32)
    up_grad = jnp.dot(after_attend16.T, grad_pre16, preferred_element_type=jnp.float32)
    down_grad = jnp.dot(activated16.T, grad_outer16, preferred_element_type=jnp.float32)
    gains_grad = jnp.stack([lax.optimization_barrier(jnp.sum(grad_middle * norm_one, axis=0)), lax.optimization_barrier(jnp.sum(upstream * norm_two, axis=0))])
    biases_grad = jnp.stack([lax.optimization_barrier(jnp.sum(packed_grad[:, :model_width].astype(jnp.float32), axis=0)), lax.optimization_barrier(jnp.sum(packed_grad[:, 2 * model_width:].astype(jnp.float32), axis=0)), lax.optimization_barrier(jnp.sum(grad_inner, axis=0)), lax.optimization_barrier(jnp.sum(grad_middle, axis=0)), lax.optimization_barrier(jnp.sum(grad_outer, axis=0)), lax.optimization_barrier(jnp.sum(upstream, axis=0))])
    hidden_grad = lax.optimization_barrier(jnp.sum(grad_pre, axis=0))
    grads = (project_grad, output_grad, up_grad, down_grad, gains_grad, biases_grad, hidden_grad)
    return (final.astype(jnp.bfloat16), input_grad, grads)

def adam_step(master, first, second, gradient, with_decay):
    first_new = beta_one * first + (1.0 - beta_one) * gradient
    second_new = beta_two * second + (1.0 - beta_two) * gradient * gradient
    first_hat = first_new / (1.0 - beta_one ** ADAM_STEP)
    second_hat = second_new / (1.0 - beta_two ** ADAM_STEP)
    change = first_hat / (jnp.sqrt(second_hat) + adam_eps)
    if with_decay:
        change = change + decay_rate * master
    return (master - learn_rate * change, first_new, second_new)

def reference(layer_input, cotangent, lengths, project_weight, output_weight, up_weight, down_weight, norm_gains, biases, hidden_bias, first_project, first_output, first_up, first_down, first_gains, first_biases, first_hidden, second_project, second_output, second_up, second_down, second_gains, second_biases, second_hidden):
    masters = (project_weight, output_weight, up_weight, down_weight, norm_gains, biases, hidden_bias)
    firsts = (first_project, first_output, first_up, first_down, first_gains, first_biases, first_hidden)
    seconds = (second_project, second_output, second_up, second_down, second_gains, second_biases, second_hidden)
    params16 = tuple((master.astype(jnp.bfloat16) for master in masters))
    empty_grads = tuple((jnp.zeros(master.shape, jnp.float32) for master in masters))

    def advance(running, inputs):
        tokens16, upstream16, length = inputs
        final, input_grad, grads = sequence_pass(params16, tokens16, upstream16, length)
        return (tuple((held + added for held, added in zip(running, grads))), (final, input_grad))
    totals, (block_output, input_gradient) = lax.scan(advance, empty_grads, (layer_input, cotangent, lengths))
    decay_flags = (True, True, True, True, False, False, False)
    results = [adam_step(masters[number], firsts[number], seconds[number], totals[number], decay_flags[number]) for number in range(7)]
    new_masters = tuple((outcome[0] for outcome in results))
    new_firsts = tuple((outcome[1] for outcome in results))
    new_seconds = tuple((outcome[2] for outcome in results))
    return (block_output, input_gradient) + tuple(totals) + new_masters + new_firsts + new_seconds
```

```python
import jax
import jax.numpy as jnp
from jax import lax
from jax.experimental import pallas as pl
from jax.experimental.pallas import tpu as pltpu
from jax.sharding import PartitionSpec as P

HD = 64
ADAM_STEP = 3


beta_one = 0.9
beta_two = 0.999
learn_rate = 0.01
decay_rate = 0.01
adam_eps = 1e-08
norm_eps = 1e-05
half_root = 0.7071067811865476
gauss_peak = 0.3989422804014327

bf16 = jnp.bfloat16
f32 = jnp.float32


def layer_norm(summed, gain, shift):
    centred = summed - jnp.mean(summed, axis=-1, keepdims=True)
    spread = jnp.mean(centred * centred, axis=-1, keepdims=True)
    recip = lax.rsqrt(spread + norm_eps)
    normed = centred * recip
    return (normed * gain + shift, normed, recip)


def norm_back(upstream, normed, recip, gain):
    scaled = upstream * gain
    return recip * (
        scaled
        - jnp.mean(scaled, axis=-1, keepdims=True)
        - normed * jnp.mean(scaled * normed, axis=-1, keepdims=True)
    )


def gelu_exact(pre_act):
    return 0.5 * pre_act * (1.0 + lax.erf(pre_act * half_root))


def gelu_slope(pre_act):
    return (
        0.5 * (1.0 + lax.erf(pre_act * half_root))
        + pre_act * jnp.exp(-0.5 * pre_act * pre_act) * gauss_peak
    )


def dot(left, right):
    return jnp.dot(left, right, preferred_element_type=f32)


def contract_last(left, right):
    return lax.dot_general(left, right, (((1,), (1,)), ((), ())), preferred_element_type=f32)


def contract_first(left, right):
    return lax.dot_general(left, right, (((0,), (0,)), ((), ())), preferred_element_type=f32)


def pick(array, index, axis=0):
    return lax.dynamic_index_in_dim(array, index, axis, keepdims=False)


def after(value, *others):
    return lax.optimization_barrier((value,) + others)[0] if others else value


def round_up(value, unit):
    return -(-value // unit) * unit


def adam_step(master, first, second, gradient, with_decay):
    first_new = beta_one * first + (1.0 - beta_one) * gradient
    second_new = beta_two * second + (1.0 - beta_two) * gradient * gradient
    first_hat = first_new / (1.0 - beta_one**ADAM_STEP)
    second_hat = second_new / (1.0 - beta_two**ADAM_STEP)
    change = first_hat / (jnp.sqrt(second_hat) + adam_eps)
    if with_decay:
        change = change + decay_rate * master
    return (master - learn_rate * change, first_new, second_new)


LANES = 128


def keep_rows(limits_ref, group_at, planes, slice_len):
    rows = lax.broadcasted_iota(jnp.int32, (slice_len, 1), 0)
    return jnp.concatenate(
        [rows < limits_ref[group_at, step] for step in range(planes)], axis=0
    )


def head_mask(shape, place):
    lane = lax.broadcasted_iota(jnp.int32, shape, 1)
    return (lane >= place * HD) & (lane < (place + 1) * HD)


def forward_kernel(limits_ref, query_ref, key_ref, value_ref, context_ref, log_ref):
    planes = limits_ref.shape[1]
    length = query_ref.shape[0]
    keep = keep_rows(limits_ref, pl.program_id(0), planes, length // planes)
    query = query_ref[...] * jnp.asarray(HD**-0.5, bf16)
    key = key_ref[...]
    value = value_ref[...]
    total = None
    for place in range(LANES // HD):
        own = head_mask(query.shape, place)
        zero = jnp.zeros_like(query)
        scores = contract_last(key, jnp.where(own, query, zero))
        scores = jnp.where(keep, scores, -jnp.inf)
        row_max = jnp.max(scores, axis=0, keepdims=True)
        lifted = jnp.exp(scores - row_max)
        row_total = jnp.sum(lifted, axis=0, keepdims=True)
        weights16 = (lifted * (1.0 / row_total)).astype(bf16)
        part = contract_first(jnp.where(own, value, zero), weights16)
        total = part if total is None else total + part
        log_ref[0, place : place + 1, :] = row_max + jnp.log(row_total)
    context_ref[...] = jnp.transpose(total).astype(bf16)


def backward_kernel(
    limits_ref,
    query_ref,
    key_ref,
    value_ref,
    context_ref,
    log_ref,
    upstream_ref,
    grads_ref,
):
    planes = limits_ref.shape[1]
    length = query_ref.shape[0]
    keep = keep_rows(limits_ref, pl.program_id(0), planes, length // planes)
    scale = HD**-0.5
    query = query_ref[...] * jnp.asarray(scale, bf16)
    key = key_ref[...]
    value = value_ref[...]
    upstream = upstream_ref[...]
    offsets = jnp.transpose(upstream.astype(f32) * context_ref[...].astype(f32))
    zero = jnp.zeros_like(query)
    query_grad, key_grad, value_grad = None, None, None
    for place in range(LANES // HD):
        own = head_mask(query.shape, place)
        own_query = jnp.where(own, query, zero)
        own_upstream = jnp.where(own, upstream, zero)
        scores = contract_last(key, own_query)
        attention = jnp.exp(scores - log_ref[0, place : place + 1, :])
        attention = jnp.where(keep, attention, 0.0)
        part = dot(attention.astype(bf16), own_upstream)
        value_grad = part if value_grad is None else value_grad + part
        prob_grad = contract_last(value, own_upstream)
        offset = jnp.sum(offsets[place * HD : (place + 1) * HD], axis=0, keepdims=True)
        score16 = (attention * (prob_grad - offset) * scale).astype(bf16)
        part = dot(score16, own_query)
        key_grad = part if key_grad is None else key_grad + part
        part = contract_first(jnp.where(own, key, zero), score16)
        query_grad = part if query_grad is None else query_grad + part
    width = grads_ref.shape[1] // 3
    start = pl.multiple_of(pl.program_id(1) * LANES, LANES)
    grads_ref[:, pl.ds(start, LANES)] = jnp.transpose(query_grad).astype(bf16)
    grads_ref[:, pl.ds(width + start, LANES)] = (key_grad * (1.0 / scale)).astype(bf16)
    grads_ref[:, pl.ds(2 * width + start, LANES)] = value_grad.astype(bf16)


def attend_forward(packed, limits, width):
    group, planes = limits.shape
    length = packed.shape[0] // group
    pairs = width // LANES
    places = LANES // HD

    def block(offset):
        return pl.BlockSpec((length, LANES), lambda g, j, limits: (g, offset + j))

    return pl.pallas_call(
        forward_kernel,
        out_shape=(
            jax.ShapeDtypeStruct((packed.shape[0], width), bf16),
            jax.ShapeDtypeStruct((group * pairs, places, length), f32),
        ),
        grid_spec=pltpu.PrefetchScalarGridSpec(
            num_scalar_prefetch=1,
            grid=(group, pairs),
            in_specs=[block(0), block(pairs), block(2 * pairs)],
            out_specs=[
                block(0),
                pl.BlockSpec((1, places, length), lambda g, j, limits: (g * pairs + j, 0, 0)),
            ],
        ),
        cost_estimate=pl.CostEstimate(
            flops=4 * packed.shape[0] * length * width,
            bytes_accessed=packed.size * 3,
            transcendentals=packed.shape[0] * length * width // HD,
        ),
        name="attend_forward",
    )(limits, packed, packed, packed)


def attend_backward(packed, context16, log_total, upstream16, limits, width):
    group, planes = limits.shape
    length = packed.shape[0] // group
    pairs = width // LANES
    places = LANES // HD

    def block(offset):
        return pl.BlockSpec((length, LANES), lambda g, j, limits: (g, offset + j))

    return pl.pallas_call(
        backward_kernel,
        out_shape=jax.ShapeDtypeStruct(packed.shape, bf16),
        grid_spec=pltpu.PrefetchScalarGridSpec(
            num_scalar_prefetch=1,
            grid=(group, pairs),
            in_specs=[
                block(0),
                block(pairs),
                block(2 * pairs),
                block(0),
                pl.BlockSpec((1, places, length), lambda g, j, limits: (g * pairs + j, 0, 0)),
                block(0),
            ],
            out_specs=pl.BlockSpec((length, packed.shape[1]), lambda g, j, limits: (g, 0)),
        ),
        cost_estimate=pl.CostEstimate(
            flops=10 * packed.shape[0] * length * width,
            bytes_accessed=packed.size * 6,
            transcendentals=packed.shape[0] * length * width // HD,
        ),
        name="attend_backward",
    )(limits, packed, packed, packed, context16, log_total, upstream16)


def make_shards(planes, members):
    chips = members // 2
    bits = [1 << bit for bit in range(chips.bit_length() - 1)]
    plane_bits = [1 << bit for bit in range(planes.bit_length() - 1)]
    axes = ("seq", "fsdp")

    def swap(value, mask):
        return lax.ppermute(value, "fsdp", [(i, i ^ mask) for i in range(members)])

    def partner(value):
        return swap(value, 1)

    def along(value, step):
        return lax.ppermute(value, "seq", [(i, (i + step) % planes) for i in range(planes)])

    def across(value, mask):
        return lax.ppermute(value, "seq", [(i, i ^ mask) for i in range(planes)])

    def gather_chips(own, chip, first=(), later=()):
        rows, width = own.shape
        half = rows // 2
        direct = {}
        sent = after(own, *first)
        for bit in bits:
            direct[bit] = swap(sent, 2 * bit)
        halves = []
        for lower, order in ((0, bits), (half, bits[::-1])):
            held = {0: own[lower : lower + half]}
            for bit in order:
                far = [rel for rel in held if rel]
                fresh = {bit: direct[bit][lower : lower + half]}
                if far:
                    batch = held[far[0]] if len(far) == 1 else jnp.concatenate([held[r] for r in far])
                    moved = swap(after(batch, *later), 2 * bit)
                    for place, rel in enumerate(far):
                        fresh[rel | bit] = moved[place * half : (place + 1) * half]
                held.update(fresh)
            halves.append(held)
        whole = jnp.zeros((chips, rows, width), own.dtype)
        last = ()
        for rel in range(chips):
            if rel == 0 or rel in direct:
                piece = own if rel == 0 else direct[rel]
                whole = lax.dynamic_update_slice(whole, piece[None], (chip ^ rel, 0, 0))
            else:
                for side in (0, 1):
                    last += (halves[side][rel],)
                    whole = lax.dynamic_update_slice(
                        whole, halves[side][rel][None], (chip ^ rel, side * half, 0)
                    )
        return whole, tuple(direct.values()), last

    def scatter_chips(terms, chip, holds=()):
        half = terms.shape[1] // 2
        outs = []
        for lower, order in ((0, bits[::-1]), (half, bits)):
            block = terms[:, lower : lower + half].reshape((2,) * len(bits) + (half, terms.shape[2]))
            left = bits[::-1]
            for turn, bit in enumerate(order):
                axis = left.index(bit)
                left = [other for other in left if other != bit]
                mine = (chip // bit) % 2
                sent = pick(block, 1 - mine, axis).astype(bf16)
                kept = pick(block, mine, axis)
                if turn < len(holds):
                    sent = after(sent, *holds[turn])
                block = kept.astype(f32) + swap(sent, 2 * bit).astype(f32)
            outs.append(block)
        return jnp.concatenate(outs, axis=0)

    def reduce_planes(term, plane):
        rows, width = term.shape
        parts = term.reshape(planes, rows // planes, width)
        total = pick(parts, plane)
        for step in range(1, planes):
            sent = pick(parts, (plane + step) % planes).astype(bf16)
            total = total + along(sent, step).astype(f32)
        total = total.astype(bf16)
        whole = jnp.zeros((planes,) + total.shape, bf16)
        whole = lax.dynamic_update_slice(whole, total[None], (plane, 0, 0))
        for step in range(1, planes):
            moved = along(total, step)
            whole = lax.dynamic_update_slice(whole, moved[None], ((plane - step) % planes, 0, 0))
        return whole.reshape(rows, width)

    def reduce_pairs(term, plane, hold=()):
        rows, width = term.shape
        block = term.reshape((2,) * len(plane_bits) + (rows // planes, width))
        left = plane_bits[::-1]
        for bit in plane_bits:
            axis = left.index(bit)
            left = [other for other in left if other != bit]
            mine = (plane // bit) % 2
            sent = after(pick(block, 1 - mine, axis).astype(bf16), *hold)
            hold = ()
            block = pick(block, mine, axis).astype(f32) + across(sent, bit).astype(f32)
        block = block.astype(bf16)
        for turn, bit in enumerate(plane_bits[::-1]):
            other = across(block, bit)
            first = (plane // bit) % 2 == 0
            block = jnp.stack(
                [jnp.where(first, block, other), jnp.where(first, other, block)], axis=turn
            )
        return block.reshape(rows, width)

    def shards(
        layer_input,
        cotangent,
        lengths,
        project_weight,
        output_weight,
        up_weight,
        down_weight,
        norm_gains,
        biases,
        hidden_bias,
        *moments,
    ):
        masters = (
            project_weight,
            output_weight,
            up_weight,
            down_weight,
            norm_gains,
            biases,
            hidden_bias,
        )
        firsts, seconds = moments[:7], moments[7:]
        seqs_here, slice_len, width = layer_input.shape
        own_rows = project_weight.shape[0]
        hidden_width = up_weight.shape[1]
        hidden_half = hidden_width // 2
        hidden_block = hidden_width // members
        half_width = width // 2
        group = 2 * seqs_here // planes
        turns = seqs_here // group
        plane = lax.axis_index("seq")
        member = lax.axis_index("fsdp")
        chip, core = member // 2, member % 2
        home = plane * group // seqs_here

        def home_of(plane_at):
            return plane_at * group // seqs_here

        def to_sequences(array, first=(), later=()):
            array = after(array, *first)
            blocks = []
            for step in range(planes):
                target = (plane + step) % planes
                block = lax.dynamic_slice_in_dim(array, (target * group) % seqs_here, group, 0)
                if step:
                    pairs = []
                    for source in range(planes):
                        there = (source + step) % planes
                        for one in range(chips):
                            at = 2 * one + home_of(there)
                            pairs.append((source * members + at, there * members + at))
                    block = lax.ppermute(block, axes, pairs)
                blocks.append(block)
            mine = jnp.stack(blocks, axis=1).reshape(group * planes * slice_len, width)
            return jnp.where(core == home, mine, partner(after(mine, *later)))

        def from_sequences(array, hold=()):
            blocks = after(array, *hold).reshape(group, planes, slice_len, width)
            arrived = [blocks[:, 0]]
            for step in range(1, planes):
                pairs = []
                for source in range(planes):
                    there = (source - step) % planes
                    for one in range(chips):
                        at = 2 * one + home_of(source)
                        pairs.append((source * members + at, there * members + at))
                arrived.append(lax.ppermute(blocks[:, step], axes, pairs))
            slots = []
            for turn in range(turns):
                step_at = (core * turns + turn - plane) % planes
                value = arrived[0]
                for step in range(1, planes):
                    value = jnp.where(step_at == step, arrived[step], value)
                slots.append(value)
            return jnp.concatenate(slots, axis=0)

        def by_core(low, high):
            return jnp.where(core == 0, low, high)

        def split_columns(array, block):
            pieces = [
                array[:, start : start + block] for start in range(0, array.shape[1], block)
            ]
            return jnp.concatenate(pieces[::2], axis=1), jnp.concatenate(pieces[1::2], axis=1)

        def join_columns(low, high, block):
            pieces = []
            for start in range(0, low.shape[1], block):
                pieces += [low[:, start : start + block], high[:, start : start + block]]
            return jnp.concatenate(pieces, axis=1)

        tokens16 = to_sequences(layer_input)
        project_low, project_high = split_columns(project_weight, half_width)
        up_low, up_high = split_columns(up_weight, hidden_block)
        low_cols = jnp.concatenate([project_low, up_low], axis=1).astype(bf16)
        high_cols = jnp.concatenate([project_high, up_high], axis=1).astype(bf16)
        kept_cols = by_core(low_cols, high_cols)
        swapped = partner(by_core(high_cols, low_cols))
        both = jnp.concatenate(
            [by_core(kept_cols, swapped), by_core(swapped, kept_cols)], axis=0
        )
        cut = 3 * half_width
        project16, project_direct, project_last = gather_chips(both[:, :cut], chip)

        small = jnp.concatenate([norm_gains, biases], axis=0).astype(bf16)
        small = lax.dynamic_update_slice(
            jnp.zeros((small.shape[0], width), bf16), small, (0, member * own_rows)
        )
        hidden_small = lax.dynamic_update_slice(
            jnp.zeros((hidden_half,), bf16), hidden_bias.astype(bf16), (chip * hidden_block,)
        ).reshape(-1, width)
        small = jnp.concatenate([small, hidden_small], axis=0)
        fill = round_up(own_rows + small.shape[0], 32) - own_rows - small.shape[0]
        pack = jnp.concatenate(
            [output_weight.astype(bf16), small, jnp.zeros((fill, width), bf16)], axis=0
        )
        packs, pack_direct, pack_last = gather_chips(pack, chip, project_direct)
        other_packs = partner(packs)

        home_lengths = jnp.where(core == home, lengths, partner(lengths))
        length = lax.dynamic_slice_in_dim(home_lengths, (plane * group) % seqs_here, group, 0)
        starts = (plane - jnp.arange(planes)) % planes * slice_len
        limits = length[:, None] - starts[None, :]

        project16 = project16.reshape(width, cut)
        even, odd = by_core(packs, other_packs), by_core(other_packs, packs)
        pair = jnp.stack([even, odd], axis=1)
        output16 = lax.dynamic_slice_in_dim(pair, core * (chips // 2), chips // 2, 0)
        output16 = output16[:, :, :own_rows].reshape(half_width, width)
        table = jnp.sum(
            packs[:, own_rows : own_rows + 8].astype(f32)
            + other_packs[:, own_rows : own_rows + 8].astype(f32),
            axis=0,
        )
        gain_rows, bias_rows = table[:2], table[2:]
        hidden_row = jnp.sum(
            packs[:, own_rows + 8 : own_rows + 8 + hidden_half // width].astype(f32), axis=0
        ).reshape(-1)

        own_bias = by_core(bias_rows[:2, :half_width], bias_rows[:2, half_width:])
        shift = jnp.concatenate([own_bias[0], jnp.zeros_like(own_bias[0]), own_bias[1]])
        packed = (dot(tokens16, project16) + shift).astype(bf16)
        context16, log_total = attend_forward(packed, limits, half_width)

        up16, up_direct, up_last = gather_chips(
            both[:, cut:], chip, project_last, (context16,)
        )
        up16 = up16.reshape(width, hidden_half)
        inner_part = dot(context16, output16)
        inner_sum = tokens16.astype(f32) + (inner_part + partner(inner_part)) + bias_rows[2]
        after_attend, norm_one, recip_one = layer_norm(inner_sum, gain_rows[0], bias_rows[3])
        after_attend16 = after_attend.astype(bf16)
        upstream16 = to_sequences(cotangent, (packed,), (inner_part,))
        pre_act = dot(after_attend16, up16) + hidden_row
        activated16 = gelu_exact(pre_act).astype(bf16)
        down16, down_direct, down_last = gather_chips(
            down_weight.astype(bf16), chip, (context16,), (activated16,)
        )
        down16 = down16.reshape(hidden_half, width)
        outer_part = dot(activated16, down16)
        outer_sum = after_attend + (outer_part + partner(outer_part)) + bias_rows[4]
        final, norm_two, recip_two = layer_norm(outer_sum, gain_rows[1], bias_rows[5])

        upstream = upstream16.astype(f32)
        grad_outer = norm_back(upstream, norm_two, recip_two, gain_rows[1])
        grad_outer16 = grad_outer.astype(bf16)
        down_term = contract_first(activated16, grad_outer16).astype(bf16)
        grad_pre = contract_last(grad_outer16, down16) * gelu_slope(pre_act)
        grad_pre16 = grad_pre.astype(bf16)
        middle_part = contract_last(grad_pre16, up16)
        grad_middle = grad_outer + (middle_part + partner(middle_part))
        up_term = contract_first(after_attend16, grad_pre16).astype(bf16)
        block_output = from_sequences(final.astype(bf16), (middle_part,))
        grad_inner = norm_back(grad_middle, norm_one, recip_one, gain_rows[0])
        grad_inner16 = grad_inner.astype(bf16)
        grad_context16 = contract_last(grad_inner16, output16).astype(bf16)
        down_sum = scatter_chips(
            down_term.reshape(chips, -1, width), chip, ((), (grad_context16,))
        )
        output_term = contract_first(context16, grad_inner16).astype(bf16)
        packed_grad = attend_backward(
            packed, context16, log_total, grad_context16, limits, half_width
        )
        up_sum = scatter_chips(
            up_term.reshape(chips, -1, hidden_half), chip, ((), (packed_grad,))
        )
        project_term = contract_first(tokens16, packed_grad).astype(bf16)
        input_part = contract_last(packed_grad, project16)
        input_sum = grad_inner + (input_part + partner(input_part))
        input_gradient = from_sequences(input_sum.astype(bf16))

        packed_sum = jnp.sum(packed_grad.astype(f32), axis=0)
        edge = jnp.stack([packed_sum[:half_width], packed_sum[2 * half_width :]])
        blank = jnp.zeros_like(edge)
        edge = by_core(
            jnp.concatenate([edge, blank], axis=1), jnp.concatenate([blank, edge], axis=1)
        ).astype(bf16)
        edge = jnp.concatenate([edge, jnp.zeros((14, width), bf16)], axis=0)
        mine_rows = output_term.reshape(chips // 2, 2, own_rows, width)
        kept_rows = pick(mine_rows, core, 1)
        sent_rows = pick(mine_rows, 1 - core, 1).reshape(-1, width)
        other_rows = partner(jnp.concatenate([sent_rows, edge], axis=0))
        edge = (edge[:2] + other_rows[-16:-14]).astype(bf16)
        other_rows = other_rows[:-16].reshape(kept_rows.shape)
        ordered = jnp.concatenate(
            [by_core(kept_rows, other_rows), by_core(other_rows, kept_rows)], axis=0
        )
        wide_terms = jnp.stack(
            [
                jnp.sum(grad_middle * norm_one, axis=0),
                jnp.sum(upstream * norm_two, axis=0),
                jnp.sum(grad_inner, axis=0),
                jnp.sum(grad_middle, axis=0),
                jnp.sum(grad_outer, axis=0),
                jnp.sum(upstream, axis=0),
            ]
        ).astype(bf16)
        hidden_term = jnp.sum(grad_pre, axis=0).astype(bf16).reshape(-1, width)
        tail = jnp.concatenate([edge, wide_terms, hidden_term], axis=0)
        fill = round_up(own_rows + tail.shape[0], 32) - own_rows - tail.shape[0]
        tail = jnp.concatenate([tail, jnp.zeros((fill, width), bf16)], axis=0)
        tail = jnp.broadcast_to(tail[None], (chips,) + tail.shape)
        output_rows = jnp.concatenate([ordered, tail], axis=1)
        project_sum = scatter_chips(project_term.reshape(chips, -1, cut), chip)
        output_sum = scatter_chips(output_rows, chip)

        def full_columns(term, block):
            parts = term.reshape(2, own_rows, -1)
            kept = pick(parts, core)
            other = partner(pick(parts, 1 - core))
            return join_columns(by_core(kept, other), by_core(other, kept), block).astype(f32)

        down_total = reduce_pairs(down_sum, plane, (packed_grad,)).astype(f32)
        up_total = full_columns(reduce_pairs(up_sum, plane), hidden_block)
        output_all = reduce_planes(output_sum, plane).astype(f32)
        project_total = full_columns(reduce_planes(project_sum, plane), half_width)
        output_total = output_all[:own_rows]
        own_table = lax.dynamic_slice(
            output_all[own_rows : own_rows + 8], (0, member * own_rows), (8, own_rows)
        )
        hidden_total = lax.dynamic_slice(
            output_all[own_rows + 8 : own_rows + 8 + hidden_half // width].reshape(-1),
            (chip * hidden_block,),
            (hidden_block,),
        )
        gains_total = own_table[2:4]
        biases_total = jnp.concatenate([own_table[:2], own_table[4:]], axis=0)
        totals = (
            project_total,
            output_total,
            up_total,
            down_total,
            gains_total,
            biases_total,
            hidden_total,
        )
        decay_flags = (True, True, True, True, False, False, False)
        results = [
            adam_step(masters[n], firsts[n], seconds[n], totals[n], decay_flags[n])
            for n in range(7)
        ]
        return (
            (block_output, input_gradient)
            + totals
            + tuple(outcome[0] for outcome in results)
            + tuple(outcome[1] for outcome in results)
            + tuple(outcome[2] for outcome in results)
        )

    return shards


def solution(mesh):
    tokens = P("fsdp", "seq", None)
    rows = P("fsdp", None)
    columns = P(None, "fsdp")
    flat = P("fsdp")
    params = (rows, rows, rows, rows, columns, columns, flat)
    return jax.shard_map(
        make_shards(mesh.shape["seq"], mesh.shape["fsdp"]),
        mesh=mesh,
        in_specs=(tokens, tokens, flat) + params * 3,
        out_specs=(tokens, tokens) + params * 4,
        check_vma=False,
    )
```

```python
import jax
import jax.numpy as jnp
from jax import lax
from jax.experimental import pallas as pl
from jax.experimental.pallas import tpu as pltpu
from jax.sharding import PartitionSpec as P


HD = 64
ADAM_STEP = 3


beta_one = 0.9
beta_two = 0.999
learn_rate = 0.01
decay_rate = 0.01
adam_eps = 1e-08
norm_eps = 1e-05
half_root = 0.7071067811865476
gauss_peak = 0.3989422804014327

bf16 = jnp.bfloat16
f32 = jnp.float32


def layer_norm(summed, gain, shift):
    centred = summed - jnp.mean(summed, axis=-1, keepdims=True)
    spread = jnp.mean(centred * centred, axis=-1, keepdims=True)
    recip = lax.rsqrt(spread + norm_eps)
    normed = centred * recip
    return (normed * gain + shift, normed, recip)


def norm_back(upstream, normed, recip, gain):
    scaled = upstream * gain
    return recip * (
        scaled
        - jnp.mean(scaled, axis=-1, keepdims=True)
        - normed * jnp.mean(scaled * normed, axis=-1, keepdims=True)
    )


def gelu_exact(pre_act):
    return 0.5 * pre_act * (1.0 + lax.erf(pre_act * half_root))


def gelu_slope(pre_act):
    return (
        0.5 * (1.0 + lax.erf(pre_act * half_root))
        + pre_act * jnp.exp(-0.5 * pre_act * pre_act) * gauss_peak
    )


def dot(left, right):
    return jnp.dot(left, right, preferred_element_type=f32)


def contract_last(left, right):
    return lax.dot_general(left, right, (((1,), (1,)), ((), ())), preferred_element_type=f32)


def contract_first(left, right):
    return lax.dot_general(left, right, (((0,), (0,)), ((), ())), preferred_element_type=f32)


def pick(array, index, axis=0):
    return lax.dynamic_index_in_dim(array, index, axis, keepdims=False)


def after(value, *others):
    return lax.optimization_barrier((value,) + others)[0] if others else value


def round_up(value, unit):
    return -(-value // unit) * unit


def adam_step(master, first, second, gradient, with_decay):
    first_new = beta_one * first + (1.0 - beta_one) * gradient
    second_new = beta_two * second + (1.0 - beta_two) * gradient * gradient
    first_hat = first_new / (1.0 - beta_one**ADAM_STEP)
    second_hat = second_new / (1.0 - beta_two**ADAM_STEP)
    change = first_hat / (jnp.sqrt(second_hat) + adam_eps)
    if with_decay:
        change = change + decay_rate * master
    return (master - learn_rate * change, first_new, second_new)


LANES = 128


def keep_rows(limits_ref, group_at, planes, slice_len):
    rows = lax.broadcasted_iota(jnp.int32, (slice_len, 1), 0)
    return jnp.concatenate(
        [rows < limits_ref[group_at, step] for step in range(planes)], axis=0
    )


def head_mask(shape, place):
    lane = lax.broadcasted_iota(jnp.int32, shape, 1)
    return (lane >= place * HD) & (lane < (place + 1) * HD)


def forward_kernel(limits_ref, query_ref, key_ref, value_ref, context_ref, log_ref):
    planes = limits_ref.shape[1]
    length = query_ref.shape[0]
    keep = keep_rows(limits_ref, pl.program_id(0), planes, length // planes)
    query = query_ref[...] * jnp.asarray(HD**-0.5, bf16)
    key = key_ref[...]
    value = value_ref[...]
    total = None
    for place in range(LANES // HD):
        own = head_mask(query.shape, place)
        zero = jnp.zeros_like(query)
        scores = contract_last(key, jnp.where(own, query, zero))
        scores = jnp.where(keep, scores, -jnp.inf)
        row_max = jnp.max(scores, axis=0, keepdims=True)
        lifted = jnp.exp(scores - row_max)
        row_total = jnp.sum(lifted, axis=0, keepdims=True)
        weights16 = (lifted * (1.0 / row_total)).astype(bf16)
        part = contract_first(jnp.where(own, value, zero), weights16)
        total = part if total is None else total + part
        log_ref[0, place : place + 1, :] = row_max + jnp.log(row_total)
    context_ref[...] = jnp.transpose(total).astype(bf16)


def backward_kernel(
    limits_ref,
    query_ref,
    key_ref,
    value_ref,
    context_ref,
    log_ref,
    upstream_ref,
    grads_ref,
):
    planes = limits_ref.shape[1]
    length = query_ref.shape[0]
    keep = keep_rows(limits_ref, pl.program_id(0), planes, length // planes)
    scale = HD**-0.5
    query = query_ref[...] * jnp.asarray(scale, bf16)
    key = key_ref[...]
    value = value_ref[...]
    upstream = upstream_ref[...]
    offsets = jnp.transpose(upstream.astype(f32) * context_ref[...].astype(f32))
    zero = jnp.zeros_like(query)
    query_grad, key_grad, value_grad = None, None, None
    for place in range(LANES // HD):
        own = head_mask(query.shape, place)
        own_query = jnp.where(own, query, zero)
        own_upstream = jnp.where(own, upstream, zero)
        scores = contract_last(key, own_query)
        attention = jnp.exp(scores - log_ref[0, place : place + 1, :])
        attention = jnp.where(keep, attention, 0.0)
        part = dot(attention.astype(bf16), own_upstream)
        value_grad = part if value_grad is None else value_grad + part
        prob_grad = contract_last(value, own_upstream)
        offset = jnp.sum(offsets[place * HD : (place + 1) * HD], axis=0, keepdims=True)
        score16 = (attention * (prob_grad - offset) * scale).astype(bf16)
        part = dot(score16, own_query)
        key_grad = part if key_grad is None else key_grad + part
        part = contract_first(jnp.where(own, key, zero), score16)
        query_grad = part if query_grad is None else query_grad + part
    width = grads_ref.shape[1] // 3
    start = pl.multiple_of(pl.program_id(1) * LANES, LANES)
    grads_ref[:, pl.ds(start, LANES)] = jnp.transpose(query_grad).astype(bf16)
    grads_ref[:, pl.ds(width + start, LANES)] = (key_grad * (1.0 / scale)).astype(bf16)
    grads_ref[:, pl.ds(2 * width + start, LANES)] = value_grad.astype(bf16)


def attend_forward(packed, limits, width):
    group, _ = limits.shape
    length = packed.shape[0] // group
    pairs = width // LANES
    places = LANES // HD

    def block(offset):
        return pl.BlockSpec((length, LANES), lambda g, j, limits: (g, offset + j))

    return pl.pallas_call(
        forward_kernel,
        out_shape=(
            jax.ShapeDtypeStruct((packed.shape[0], width), bf16),
            jax.ShapeDtypeStruct((group * pairs, places, length), f32),
        ),
        grid_spec=pltpu.PrefetchScalarGridSpec(
            num_scalar_prefetch=1,
            grid=(group, pairs),
            in_specs=[block(0), block(pairs), block(2 * pairs)],
            out_specs=[
                block(0),
                pl.BlockSpec((1, places, length), lambda g, j, limits: (g * pairs + j, 0, 0)),
            ],
        ),
        cost_estimate=pl.CostEstimate(
            flops=4 * packed.shape[0] * length * width,
            bytes_accessed=packed.size * 3,
            transcendentals=packed.shape[0] * length * width // HD,
        ),
        name="attend_forward",
    )(limits, packed, packed, packed)


def attend_backward(packed, context16, log_total, upstream16, limits, width):
    group, _ = limits.shape
    length = packed.shape[0] // group
    pairs = width // LANES
    places = LANES // HD

    def block(offset):
        return pl.BlockSpec((length, LANES), lambda g, j, limits: (g, offset + j))

    return pl.pallas_call(
        backward_kernel,
        out_shape=jax.ShapeDtypeStruct(packed.shape, bf16),
        grid_spec=pltpu.PrefetchScalarGridSpec(
            num_scalar_prefetch=1,
            grid=(group, pairs),
            in_specs=[
                block(0),
                block(pairs),
                block(2 * pairs),
                block(0),
                pl.BlockSpec((1, places, length), lambda g, j, limits: (g * pairs + j, 0, 0)),
                block(0),
            ],
            out_specs=pl.BlockSpec((length, packed.shape[1]), lambda g, j, limits: (g, 0)),
        ),
        cost_estimate=pl.CostEstimate(
            flops=10 * packed.shape[0] * length * width,
            bytes_accessed=packed.size * 6,
            transcendentals=packed.shape[0] * length * width // HD,
        ),
        name="attend_backward",
    )(limits, packed, packed, packed, context16, log_total, upstream16)


def make_shards(planes, members):
    chips = members // 2
    bits = [1 << bit for bit in range(chips.bit_length() - 1)]
    plane_bits = [1 << bit for bit in range(planes.bit_length() - 1)]
    axes = ("seq", "fsdp")

    def swap(value, mask):
        return lax.ppermute(value, "fsdp", [(i, i ^ mask) for i in range(members)])

    def partner(value):
        return swap(value, 1)

    def along(value, step):
        return lax.ppermute(value, "seq", [(i, (i + step) % planes) for i in range(planes)])

    def across(value, mask):
        return lax.ppermute(value, "seq", [(i, i ^ mask) for i in range(planes)])

    def gather_chips(own, first=(), later=()):
        rows = own.shape[0]
        half = max(rows // 32 * 16, 1)
        direct = {}
        sent = after(own, *first)
        for bit in bits:
            direct[bit] = swap(sent, 2 * bit)
        pieces = [(0, 0, own)] + [(bit, 0, direct[bit]) for bit in bits]
        last = ()
        for lower, upper, order in ((0, half, bits), (half, rows, bits[::-1])):
            held = {0: own[lower:upper]}
            for bit in order:
                far = [rel for rel in held if rel]
                fresh = {bit: direct[bit][lower:upper]}
                if far:
                    batch = held[far[0]] if len(far) == 1 else jnp.concatenate([held[r] for r in far])
                    moved = swap(after(batch, *later), 2 * bit)
                    size = upper - lower
                    for place, rel in enumerate(far):
                        fresh[rel | bit] = moved[place * size : (place + 1) * size]
                        pieces.append((rel | bit, lower, fresh[rel | bit]))
                        last += (fresh[rel | bit],)
                held.update(fresh)
        return pieces, tuple(direct.values()), last

    def assemble(pieces, chip, rows):
        width = pieces[0][2].shape[1]
        whole = jnp.zeros((chips, rows, width), pieces[0][2].dtype)
        for rel, lower, piece in pieces:
            used = min(piece.shape[0], rows - lower)
            if used > 0:
                whole = lax.dynamic_update_slice(
                    whole, piece[None, :used], (chip ^ rel, lower, 0)
                )
        return whole

    def scatter_chips(terms, chip, holds=()):
        half = terms.shape[1] // 2
        outs = []
        for lower, order in ((0, bits[::-1]), (half, bits)):
            block = terms[:, lower : lower + half].reshape((2,) * len(bits) + (half, terms.shape[2]))
            left = bits[::-1]
            for turn, bit in enumerate(order):
                axis = left.index(bit)
                left = [other for other in left if other != bit]
                mine = (chip // bit) % 2
                sent = pick(block, 1 - mine, axis).astype(bf16)
                kept = pick(block, mine, axis)
                if turn < len(holds):
                    sent = after(sent, *holds[turn])
                block = kept.astype(f32) + swap(sent, 2 * bit).astype(f32)
            outs.append(block)
        return jnp.concatenate(outs, axis=0)

    def reduce_planes(term, plane):
        rows, width = term.shape
        parts = term.reshape(planes, rows // planes, width)
        total = pick(parts, plane)
        for step in range(1, planes):
            sent = pick(parts, (plane + step) % planes).astype(bf16)
            total = total + along(sent, step).astype(f32)
        total = total.astype(bf16)
        whole = jnp.zeros((planes,) + total.shape, bf16)
        whole = lax.dynamic_update_slice(whole, total[None], (plane, 0, 0))
        for step in range(1, planes):
            moved = along(total, step)
            whole = lax.dynamic_update_slice(whole, moved[None], ((plane - step) % planes, 0, 0))
        return whole.reshape(rows, width)

    def reduce_pairs(term, plane, hold=()):
        rows, width = term.shape
        block = term.reshape((2,) * len(plane_bits) + (rows // planes, width))
        left = plane_bits[::-1]
        for bit in plane_bits:
            axis = left.index(bit)
            left = [other for other in left if other != bit]
            mine = (plane // bit) % 2
            sent = after(pick(block, 1 - mine, axis).astype(bf16), *hold)
            hold = ()
            block = pick(block, mine, axis).astype(f32) + across(sent, bit).astype(f32)
        block = block.astype(bf16)
        for turn, bit in enumerate(plane_bits[::-1]):
            other = across(block, bit)
            first = (plane // bit) % 2 == 0
            block = jnp.stack(
                [jnp.where(first, block, other), jnp.where(first, other, block)], axis=turn
            )
        return block.reshape(rows, width)

    def shards(
        layer_input,
        cotangent,
        lengths,
        project_weight,
        output_weight,
        up_weight,
        down_weight,
        norm_gains,
        biases,
        hidden_bias,
        *moments,
    ):
        masters = (
            project_weight,
            output_weight,
            up_weight,
            down_weight,
            norm_gains,
            biases,
            hidden_bias,
        )
        firsts, seconds = moments[:7], moments[7:]
        seqs_here, slice_len, width = layer_input.shape
        own_rows = project_weight.shape[0]
        hidden_width = up_weight.shape[1]
        hidden_half = hidden_width // 2
        hidden_block = hidden_width // members
        half_width = width // 2
        group = 2 * seqs_here // planes
        turns = seqs_here // group
        plane = lax.axis_index("seq")
        member = lax.axis_index("fsdp")
        chip, core = member // 2, member % 2
        home = plane * group // seqs_here

        def home_of(plane_at):
            return plane_at * group // seqs_here

        def to_sequences(array, first=(), later=()):
            array = after(array, *first)
            blocks = []
            for step in range(planes):
                target = (plane + step) % planes
                block = lax.dynamic_slice_in_dim(array, (target * group) % seqs_here, group, 0)
                if step:
                    pairs = []
                    for source in range(planes):
                        there = (source + step) % planes
                        for one in range(chips):
                            at = 2 * one + home_of(there)
                            pairs.append((source * members + at, there * members + at))
                    block = lax.ppermute(block, axes, pairs)
                blocks.append(block)
            mine = jnp.stack(blocks, axis=1).reshape(group * planes * slice_len, width)
            return jnp.where(core == home, mine, partner(after(mine, *later)))

        def from_sequences(array, hold=()):
            blocks = after(array, *hold).reshape(group, planes, slice_len, width)
            arrived = [blocks[:, 0]]
            for step in range(1, planes):
                pairs = []
                for source in range(planes):
                    there = (source - step) % planes
                    for one in range(chips):
                        at = 2 * one + home_of(source)
                        pairs.append((source * members + at, there * members + at))
                arrived.append(lax.ppermute(blocks[:, step], axes, pairs))
            slots = []
            for turn in range(turns):
                step_at = (core * turns + turn - plane) % planes
                value = arrived[0]
                for step in range(1, planes):
                    value = jnp.where(step_at == step, arrived[step], value)
                slots.append(value)
            return jnp.concatenate(slots, axis=0)

        def by_core(low, high):
            return jnp.where(core == 0, low, high)

        def split_columns(array, block):
            pieces = [
                array[:, start : start + block] for start in range(0, array.shape[1], block)
            ]
            return jnp.concatenate(pieces[::2], axis=1), jnp.concatenate(pieces[1::2], axis=1)

        def join_columns(low, high, block):
            pieces = []
            for start in range(0, low.shape[1], block):
                pieces += [low[:, start : start + block], high[:, start : start + block]]
            return jnp.concatenate(pieces, axis=1)

        tokens16 = to_sequences(layer_input)
        project_low, project_high = split_columns(project_weight, half_width)
        up_low, up_high = split_columns(up_weight, hidden_block)
        low_cols = jnp.concatenate([project_low, up_low], axis=1).astype(bf16)
        high_cols = jnp.concatenate([project_high, up_high], axis=1).astype(bf16)
        table = jnp.concatenate([norm_gains, biases], axis=0).astype(bf16)
        tables = table.shape[0]
        table = lax.dynamic_update_slice(
            jnp.zeros((tables, width), bf16), table, (0, member * own_rows)
        )
        kept_cols = by_core(low_cols, high_cols)
        cut = 3 * half_width
        spare = jnp.pad(table, ((0, 16 - tables), (0, low_cols.shape[1] - width)))
        swapped = partner(jnp.concatenate([by_core(high_cols, low_cols), spare], axis=0))
        other_table = swapped[own_rows : own_rows + tables, :width]
        swapped = swapped[:own_rows]
        both = jnp.concatenate(
            [by_core(kept_cols, swapped), by_core(swapped, kept_cols)], axis=0
        )
        hidden_small = lax.dynamic_update_slice(
            jnp.zeros((hidden_half,), bf16), hidden_bias.astype(bf16), (chip * hidden_block,)
        ).reshape(-1, width)
        small = jnp.concatenate([table + other_table, hidden_small], axis=0)
        chip_rows = 2 * own_rows
        fill = round_up(chip_rows + small.shape[0], 16) - chip_rows - small.shape[0]
        small = jnp.pad(small, ((0, fill), (0, cut - width)))
        pieces, project_direct, project_last = gather_chips(
            jnp.concatenate([both[:, :cut], small], axis=0)
        )
        project16 = assemble(pieces, chip, chip_rows).reshape(width, cut)
        smalls = 0.0
        for _, lower, piece in pieces:
            if lower + piece.shape[0] > chip_rows:
                smalls = smalls + piece[max(chip_rows - lower, 0) :, :width].astype(f32)
        gain_rows, bias_rows = smalls[:2], smalls[2:tables]
        hidden_row = smalls[tables : tables + hidden_half // width].reshape(-1)

        pieces, _, _ = gather_chips(output_weight.astype(bf16), project_direct)
        packs = assemble(pieces, chip, own_rows)
        other_packs = partner(packs)
        even, odd = by_core(packs, other_packs), by_core(other_packs, packs)
        pair = jnp.stack([even, odd], axis=1)
        output16 = lax.dynamic_slice_in_dim(pair, core * (chips // 2), chips // 2, 0)
        output16 = output16.reshape(half_width, width)

        home_lengths = jnp.where(core == home, lengths, partner(lengths))
        length = lax.dynamic_slice_in_dim(home_lengths, (plane * group) % seqs_here, group, 0)
        starts = (plane - jnp.arange(planes)) % planes * slice_len
        limits = length[:, None] - starts[None, :]

        own_bias = by_core(bias_rows[:2, :half_width], bias_rows[:2, half_width:])
        shift = jnp.concatenate([own_bias[0], jnp.zeros_like(own_bias[0]), own_bias[1]])
        packed = (dot(tokens16, project16) + shift).astype(bf16)
        context16, log_total = attend_forward(packed, limits, half_width)

        pieces, _, _ = gather_chips(both[:, cut:], project_last, (context16,))
        up16 = assemble(pieces, chip, chip_rows).reshape(width, hidden_half)
        inner_part = dot(context16, output16)
        inner_sum = tokens16.astype(f32) + (inner_part + partner(inner_part)) + bias_rows[2]
        after_attend, norm_one, recip_one = layer_norm(inner_sum, gain_rows[0], bias_rows[3])
        after_attend16 = after_attend.astype(bf16)
        upstream16 = to_sequences(cotangent, (packed,), (inner_part,))
        pre_act = dot(after_attend16, up16) + hidden_row
        activated16 = gelu_exact(pre_act).astype(bf16)
        pieces, _, _ = gather_chips(down_weight.astype(bf16), (context16,), (activated16,))
        down16 = assemble(pieces, chip, down_weight.shape[0]).reshape(hidden_half, width)
        outer_part = dot(activated16, down16)
        outer_sum = after_attend + (outer_part + partner(outer_part)) + bias_rows[4]
        final, norm_two, recip_two = layer_norm(outer_sum, gain_rows[1], bias_rows[5])

        upstream = upstream16.astype(f32)
        grad_outer = norm_back(upstream, norm_two, recip_two, gain_rows[1])
        grad_outer16 = grad_outer.astype(bf16)
        down_term = contract_first(activated16, grad_outer16).astype(bf16)
        grad_pre = contract_last(grad_outer16, down16) * gelu_slope(pre_act)
        grad_pre16 = grad_pre.astype(bf16)
        middle_part = contract_last(grad_pre16, up16)
        grad_middle = grad_outer + (middle_part + partner(middle_part))
        up_term = contract_first(after_attend16, grad_pre16).astype(bf16)
        block_output = from_sequences(final.astype(bf16), (middle_part,))
        grad_inner = norm_back(grad_middle, norm_one, recip_one, gain_rows[0])
        grad_inner16 = grad_inner.astype(bf16)
        grad_context16 = contract_last(grad_inner16, output16).astype(bf16)
        down_sum = scatter_chips(down_term.reshape(chips, -1, width), chip, ((), (grad_context16,)))
        output_term = contract_first(context16, grad_inner16).astype(bf16)
        packed_grad = attend_backward(
            packed, context16, log_total, grad_context16, limits, half_width
        )
        up_sum = scatter_chips(up_term.reshape(chips, -1, hidden_half), chip, ((), (packed_grad,)))
        project_term = contract_first(tokens16, packed_grad).astype(bf16)
        input_part = contract_last(packed_grad, project16)
        other_part = partner(input_part)
        input_sum = (grad_inner + (input_part + other_part)).astype(bf16)
        input_gradient = from_sequences(input_sum)

        packed_sum = jnp.sum(packed_grad.astype(f32), axis=0)
        edge = jnp.stack([packed_sum[:half_width], packed_sum[2 * half_width :]])
        blank = jnp.zeros_like(edge)
        edge = by_core(
            jnp.concatenate([edge, blank], axis=1), jnp.concatenate([blank, edge], axis=1)
        ).astype(bf16)
        edge = jnp.concatenate([edge, jnp.zeros((14, width), bf16)], axis=0)
        mine_rows = output_term.reshape(chips // 2, 2, own_rows, width)
        kept_rows = pick(mine_rows, core, 1)
        sent_rows = pick(mine_rows, 1 - core, 1).reshape(-1, width)
        other_rows = partner(jnp.concatenate([sent_rows, edge], axis=0))
        edge = (edge[:2] + other_rows[-16:-14]).astype(bf16)
        other_rows = other_rows[:-16].reshape(kept_rows.shape)
        ordered = jnp.concatenate(
            [by_core(kept_rows, other_rows), by_core(other_rows, kept_rows)], axis=0
        )
        wide_terms = jnp.stack(
            [
                jnp.sum(grad_middle * norm_one, axis=0),
                jnp.sum(upstream * norm_two, axis=0),
                jnp.sum(grad_inner, axis=0),
                jnp.sum(grad_middle, axis=0),
                jnp.sum(grad_outer, axis=0),
                jnp.sum(upstream, axis=0),
            ]
        ).astype(bf16)
        hidden_term = jnp.sum(grad_pre, axis=0).astype(bf16).reshape(-1, width)
        tail = jnp.concatenate([edge, wide_terms, hidden_term], axis=0)
        fill = round_up(own_rows + tail.shape[0], 32) - own_rows - tail.shape[0]
        tail = jnp.concatenate([tail, jnp.zeros((fill, width), bf16)], axis=0)
        tail = jnp.broadcast_to(tail[None], (chips,) + tail.shape)
        output_rows = jnp.concatenate([ordered, tail], axis=1)
        project_sum = scatter_chips(project_term.reshape(chips, -1, cut), chip)
        output_sum = scatter_chips(output_rows, chip)

        def full_columns(term, block):
            parts = term.reshape(2, own_rows, -1)
            kept = pick(parts, core)
            other = partner(pick(parts, 1 - core))
            return join_columns(by_core(kept, other), by_core(other, kept), block).astype(f32)

        down_total = reduce_pairs(down_sum, plane, (packed_grad,)).astype(f32)
        up_total = full_columns(reduce_pairs(up_sum, plane), hidden_block)
        output_all = reduce_pairs(output_sum, plane).astype(f32)
        project_total = full_columns(reduce_planes(project_sum, plane), half_width)
        output_total = output_all[:own_rows]
        own_table = lax.dynamic_slice(
            output_all[own_rows : own_rows + 8], (0, member * own_rows), (8, own_rows)
        )
        hidden_total = lax.dynamic_slice(
            output_all[own_rows + 8 : own_rows + 8 + hidden_half // width].reshape(-1),
            (chip * hidden_block,),
            (hidden_block,),
        )
        gains_total = own_table[2:4]
        biases_total = jnp.concatenate([own_table[:2], own_table[4:]], axis=0)
        totals = (
            project_total,
            output_total,
            up_total,
            down_total,
            gains_total,
            biases_total,
            hidden_total,
        )
        decay_flags = (True, True, True, True, False, False, False)
        results = [
            adam_step(masters[n], firsts[n], seconds[n], totals[n], decay_flags[n])
            for n in range(7)
        ]
        return (
            (block_output, input_gradient)
            + totals
            + tuple(outcome[0] for outcome in results)
            + tuple(outcome[1] for outcome in results)
            + tuple(outcome[2] for outcome in results)
        )

    return shards


def solution(mesh):
    tokens = P("fsdp", "seq", None)
    rows = P("fsdp", None)
    columns = P(None, "fsdp")
    flat = P("fsdp")
    params = (rows, rows, rows, rows, columns, columns, flat)
    shards = make_shards(mesh.shape["seq"], mesh.shape["fsdp"])

    return jax.shard_map(
        shards,
        mesh=mesh,
        in_specs=(tokens, tokens, flat) + params * 3,
        out_specs=(tokens, tokens) + params * 4,
        check_vma=False,
    )
```

```python
import jax
import jax.numpy as jnp
from jax import lax
from jax.experimental import pallas as pl
from jax.experimental.pallas import tpu as pltpu
from jax.sharding import PartitionSpec as P


HD = 64
ADAM_STEP = 3


beta_one = 0.9
beta_two = 0.999
learn_rate = 0.01
decay_rate = 0.01
adam_eps = 1e-08
norm_eps = 1e-05
half_root = 0.7071067811865476
gauss_peak = 0.3989422804014327

bf16 = jnp.bfloat16
f32 = jnp.float32


def layer_norm(summed, gain, shift):
    centred = summed - jnp.mean(summed, axis=-1, keepdims=True)
    spread = jnp.mean(centred * centred, axis=-1, keepdims=True)
    recip = lax.rsqrt(spread + norm_eps)
    normed = centred * recip
    return (normed * gain + shift, normed, recip)


def norm_back(upstream, normed, recip, gain):
    scaled = upstream * gain
    return recip * (
        scaled
        - jnp.mean(scaled, axis=-1, keepdims=True)
        - normed * jnp.mean(scaled * normed, axis=-1, keepdims=True)
    )


def gelu_exact(pre_act):
    return 0.5 * pre_act * (1.0 + lax.erf(pre_act * half_root))


def gelu_slope(pre_act):
    return (
        0.5 * (1.0 + lax.erf(pre_act * half_root))
        + pre_act * jnp.exp(-0.5 * pre_act * pre_act) * gauss_peak
    )


def dot(left, right):
    return jnp.dot(left, right, preferred_element_type=f32)


def contract_last(left, right):
    return lax.dot_general(left, right, (((1,), (1,)), ((), ())), preferred_element_type=f32)


def contract_first(left, right):
    return lax.dot_general(left, right, (((0,), (0,)), ((), ())), preferred_element_type=f32)


def pick(array, index, axis=0):
    return lax.dynamic_index_in_dim(array, index, axis, keepdims=False)


def after(value, *others):
    return lax.optimization_barrier((value,) + others)[0] if others else value


def round_up(value, unit):
    return -(-value // unit) * unit


def adam_step(master, first, second, gradient, with_decay):
    first_new = beta_one * first + (1.0 - beta_one) * gradient
    second_new = beta_two * second + (1.0 - beta_two) * gradient * gradient
    first_hat = first_new / (1.0 - beta_one**ADAM_STEP)
    second_hat = second_new / (1.0 - beta_two**ADAM_STEP)
    change = first_hat / (jnp.sqrt(second_hat) + adam_eps)
    if with_decay:
        change = change + decay_rate * master
    return (master - learn_rate * change, first_new, second_new)


LANES = 128


def keep_rows(limits_ref, group_at, planes, slice_len):
    rows = lax.broadcasted_iota(jnp.int32, (slice_len, 1), 0)
    return jnp.concatenate(
        [rows < limits_ref[group_at, step] for step in range(planes)], axis=0
    )


def head_mask(shape, place):
    lane = lax.broadcasted_iota(jnp.int32, shape, 1)
    return (lane >= place * HD) & (lane < (place + 1) * HD)


def forward_kernel(limits_ref, query_ref, key_ref, value_ref, context_ref, log_ref):
    planes = limits_ref.shape[1]
    length = query_ref.shape[0]
    keep = keep_rows(limits_ref, pl.program_id(0), planes, length // planes)
    query = query_ref[...] * jnp.asarray(HD**-0.5, bf16)
    key = key_ref[...]
    value = value_ref[...]
    total = None
    for place in range(LANES // HD):
        own = head_mask(query.shape, place)
        zero = jnp.zeros_like(query)
        scores = contract_last(key, jnp.where(own, query, zero))
        scores = jnp.where(keep, scores, -jnp.inf)
        row_max = jnp.max(scores, axis=0, keepdims=True)
        lifted = jnp.exp(scores - row_max)
        row_total = jnp.sum(lifted, axis=0, keepdims=True)
        weights16 = (lifted * (1.0 / row_total)).astype(bf16)
        part = contract_first(jnp.where(own, value, zero), weights16)
        total = part if total is None else total + part
        log_ref[0, place : place + 1, :] = row_max + jnp.log(row_total)
    context_ref[...] = jnp.transpose(total).astype(bf16)


def backward_kernel(
    limits_ref,
    query_ref,
    key_ref,
    value_ref,
    context_ref,
    log_ref,
    upstream_ref,
    grads_ref,
):
    planes = limits_ref.shape[1]
    length = query_ref.shape[0]
    keep = keep_rows(limits_ref, pl.program_id(0), planes, length // planes)
    scale = HD**-0.5
    query = query_ref[...] * jnp.asarray(scale, bf16)
    key = key_ref[...]
    value = value_ref[...]
    upstream = upstream_ref[...]
    offsets = jnp.transpose(upstream.astype(f32) * context_ref[...].astype(f32))
    zero = jnp.zeros_like(query)
    query_grad, key_grad, value_grad = None, None, None
    for place in range(LANES // HD):
        own = head_mask(query.shape, place)
        own_query = jnp.where(own, query, zero)
        own_upstream = jnp.where(own, upstream, zero)
        scores = contract_last(key, own_query)
        attention = jnp.exp(scores - log_ref[0, place : place + 1, :])
        attention = jnp.where(keep, attention, 0.0)
        part = dot(attention.astype(bf16), own_upstream)
        value_grad = part if value_grad is None else value_grad + part
        prob_grad = contract_last(value, own_upstream)
        offset = jnp.sum(offsets[place * HD : (place + 1) * HD], axis=0, keepdims=True)
        score16 = (attention * (prob_grad - offset) * scale).astype(bf16)
        part = dot(score16, own_query)
        key_grad = part if key_grad is None else key_grad + part
        part = contract_first(jnp.where(own, key, zero), score16)
        query_grad = part if query_grad is None else query_grad + part
    width = grads_ref.shape[1] // 3
    start = pl.multiple_of(pl.program_id(1) * LANES, LANES)
    grads_ref[:, pl.ds(start, LANES)] = jnp.transpose(query_grad).astype(bf16)
    grads_ref[:, pl.ds(width + start, LANES)] = (key_grad * (1.0 / scale)).astype(bf16)
    grads_ref[:, pl.ds(2 * width + start, LANES)] = value_grad.astype(bf16)


def attend_forward(packed, limits, width):
    group, _ = limits.shape
    length = packed.shape[0] // group
    pairs = width // LANES
    places = LANES // HD

    def block(offset):
        return pl.BlockSpec((length, LANES), lambda g, j, limits: (g, offset + j))

    return pl.pallas_call(
        forward_kernel,
        out_shape=(
            jax.ShapeDtypeStruct((packed.shape[0], width), bf16),
            jax.ShapeDtypeStruct((group * pairs, places, length), f32),
        ),
        grid_spec=pltpu.PrefetchScalarGridSpec(
            num_scalar_prefetch=1,
            grid=(group, pairs),
            in_specs=[block(0), block(pairs), block(2 * pairs)],
            out_specs=[
                block(0),
                pl.BlockSpec((1, places, length), lambda g, j, limits: (g * pairs + j, 0, 0)),
            ],
        ),
        cost_estimate=pl.CostEstimate(
            flops=4 * packed.shape[0] * length * width,
            bytes_accessed=packed.size * 3,
            transcendentals=packed.shape[0] * length * width // HD,
        ),
        name="attend_forward",
    )(limits, packed, packed, packed)


def attend_backward(packed, context16, log_total, upstream16, limits, width):
    group, _ = limits.shape
    length = packed.shape[0] // group
    pairs = width // LANES
    places = LANES // HD

    def block(offset):
        return pl.BlockSpec((length, LANES), lambda g, j, limits: (g, offset + j))

    return pl.pallas_call(
        backward_kernel,
        out_shape=jax.ShapeDtypeStruct(packed.shape, bf16),
        grid_spec=pltpu.PrefetchScalarGridSpec(
            num_scalar_prefetch=1,
            grid=(group, pairs),
            in_specs=[
                block(0),
                block(pairs),
                block(2 * pairs),
                block(0),
                pl.BlockSpec((1, places, length), lambda g, j, limits: (g * pairs + j, 0, 0)),
                block(0),
            ],
            out_specs=pl.BlockSpec((length, packed.shape[1]), lambda g, j, limits: (g, 0)),
        ),
        cost_estimate=pl.CostEstimate(
            flops=10 * packed.shape[0] * length * width,
            bytes_accessed=packed.size * 6,
            transcendentals=packed.shape[0] * length * width // HD,
        ),
        name="attend_backward",
    )(limits, packed, packed, packed, context16, log_total, upstream16)


def make_shards(planes, members):
    chips = members // 2
    bits = [1 << bit for bit in range(chips.bit_length() - 1)]
    axes = ("seq", "fsdp")

    def swap(value, mask):
        return lax.ppermute(value, "fsdp", [(i, i ^ mask) for i in range(members)])

    def partner(value):
        return swap(value, 1)

    def along(value, step):
        return lax.ppermute(value, "seq", [(i, (i + step) % planes) for i in range(planes)])

    def gather_chips(own, first=(), later=()):
        rows = own.shape[0]
        half = max(rows // 32 * 16, 1)
        direct = {}
        sent = after(own, *first)
        for bit in bits:
            direct[bit] = swap(sent, 2 * bit)
        pieces = [(0, 0, own)] + [(bit, 0, direct[bit]) for bit in bits]
        last = ()
        for lower, upper, order in ((0, half, bits), (half, rows, bits[::-1])):
            held = {0: own[lower:upper]}
            for bit in order:
                far = [rel for rel in held if rel]
                fresh = {bit: direct[bit][lower:upper]}
                if far:
                    batch = held[far[0]] if len(far) == 1 else jnp.concatenate([held[r] for r in far])
                    moved = swap(after(batch, *later), 2 * bit)
                    size = upper - lower
                    for place, rel in enumerate(far):
                        fresh[rel | bit] = moved[place * size : (place + 1) * size]
                        pieces.append((rel | bit, lower, fresh[rel | bit]))
                        last += (fresh[rel | bit],)
                held.update(fresh)
        return pieces, tuple(direct.values()), last

    def assemble(pieces, chip, rows):
        width = pieces[0][2].shape[1]
        whole = jnp.zeros((chips, rows, width), pieces[0][2].dtype)
        for rel, lower, piece in pieces:
            used = min(piece.shape[0], rows - lower)
            if used > 0:
                whole = lax.dynamic_update_slice(
                    whole, piece[None, :used], (chip ^ rel, lower, 0)
                )
        return whole

    def total_of(terms):
        whole = terms[0].astype(f32)
        for term in terms[1:]:
            whole = whole + term.astype(f32)
        return whole

    def scatter_chips(sides, chip, holds=()):
        outs = []
        for block, order in zip(sides, (bits[::-1], bits)):
            terms = [block.reshape((2,) * len(bits) + block.shape[1:])]
            left = bits[::-1]
            for turn, bit in enumerate(order):
                axis = left.index(bit)
                left = [other for other in left if other != bit]
                mine = (chip // bit) % 2
                sent = total_of([pick(term, 1 - mine, axis) for term in terms]).astype(bf16)
                if turn < len(holds):
                    sent = after(sent, *holds[turn])
                terms = [pick(term, mine, axis) for term in terms]
                terms.append(swap(sent, 2 * bit))
            outs.append(terms)
        return outs

    def reduce_planes(sides, plane, hold=()):
        def quarter(index):
            return jnp.concatenate(
                [total_of([pick(term, index) for term in terms]) for terms in sides], axis=0
            )

        arrived = []
        for step in range(1, planes):
            sent = quarter((plane + step) % planes).astype(bf16)
            arrived.append(along(after(sent, *hold), step))
        total = total_of([quarter(plane)] + arrived).astype(bf16)
        whole = jnp.zeros((planes,) + total.shape, bf16)
        whole = lax.dynamic_update_slice(whole, total[None], (plane, 0, 0))
        for step in range(1, planes):
            moved = along(total, step)
            whole = lax.dynamic_update_slice(whole, moved[None], ((plane - step) % planes, 0, 0))
        return whole

    def shards(
        layer_input,
        cotangent,
        lengths,
        project_weight,
        output_weight,
        up_weight,
        down_weight,
        norm_gains,
        biases,
        hidden_bias,
        *moments,
    ):
        masters = (
            project_weight,
            output_weight,
            up_weight,
            down_weight,
            norm_gains,
            biases,
            hidden_bias,
        )
        firsts, seconds = moments[:7], moments[7:]
        seqs_here, slice_len, width = layer_input.shape
        own_rows = project_weight.shape[0]
        hidden_width = up_weight.shape[1]
        hidden_half = hidden_width // 2
        hidden_block = hidden_width // members
        half_width = width // 2
        group = 2 * seqs_here // planes
        turns = seqs_here // group
        plane = lax.axis_index("seq")
        member = lax.axis_index("fsdp")
        chip, core = member // 2, member % 2
        home = plane * group // seqs_here

        def home_of(plane_at):
            return plane_at * group // seqs_here

        def to_sequences(array, first=(), later=()):
            array = after(array, *first)
            blocks = []
            for step in range(planes):
                target = (plane + step) % planes
                block = lax.dynamic_slice_in_dim(array, (target * group) % seqs_here, group, 0)
                if step:
                    pairs = []
                    for source in range(planes):
                        there = (source + step) % planes
                        for one in range(chips):
                            at = 2 * one + home_of(there)
                            pairs.append((source * members + at, there * members + at))
                    block = lax.ppermute(block, axes, pairs)
                blocks.append(block)
            mine = jnp.stack(blocks, axis=1).reshape(group * planes * slice_len, width)
            return jnp.where(core == home, mine, partner(after(mine, *later)))

        def from_sequences(array, hold=()):
            blocks = after(array, *hold).reshape(group, planes, slice_len, width)
            arrived = [blocks[:, 0]]
            for step in range(1, planes):
                pairs = []
                for source in range(planes):
                    there = (source - step) % planes
                    for one in range(chips):
                        at = 2 * one + home_of(source)
                        pairs.append((source * members + at, there * members + at))
                arrived.append(lax.ppermute(blocks[:, step], axes, pairs))
            slots = []
            for turn in range(turns):
                step_at = (core * turns + turn - plane) % planes
                value = arrived[0]
                for step in range(1, planes):
                    value = jnp.where(step_at == step, arrived[step], value)
                slots.append(value)
            return jnp.concatenate(slots, axis=0)

        def by_core(low, high):
            return jnp.where(core == 0, low, high)

        def split_columns(array, block):
            pieces = [
                array[:, start : start + block] for start in range(0, array.shape[1], block)
            ]
            return jnp.concatenate(pieces[::2], axis=1), jnp.concatenate(pieces[1::2], axis=1)

        def join_columns(low, high, block):
            pieces = []
            for start in range(0, low.shape[1], block):
                pieces += [low[:, start : start + block], high[:, start : start + block]]
            return jnp.concatenate(pieces, axis=1)

        tokens16 = to_sequences(layer_input)
        project_low, project_high = split_columns(project_weight, half_width)
        up_low, up_high = split_columns(up_weight, hidden_block)
        output_low, output_high = split_columns(output_weight, half_width)
        low_cols = jnp.concatenate([project_low, output_low, up_low], axis=1).astype(bf16)
        high_cols = jnp.concatenate([project_high, output_high, up_high], axis=1).astype(bf16)
        table = jnp.concatenate([norm_gains, biases], axis=0).astype(bf16)
        tables = table.shape[0]
        table = lax.dynamic_update_slice(
            jnp.zeros((tables, width), bf16), table, (0, member * own_rows)
        )
        kept_cols = by_core(low_cols, high_cols)
        cut = 4 * half_width
        spare = jnp.pad(table, ((0, 16 - tables), (0, low_cols.shape[1] - width)))
        swapped = partner(jnp.concatenate([by_core(high_cols, low_cols), spare], axis=0))
        other_table = swapped[own_rows : own_rows + tables, :width]
        swapped = swapped[:own_rows]
        both = jnp.concatenate(
            [by_core(kept_cols, swapped), by_core(swapped, kept_cols)], axis=0
        )
        hidden_small = lax.dynamic_update_slice(
            jnp.zeros((hidden_half,), bf16), hidden_bias.astype(bf16), (chip * hidden_block,)
        ).reshape(-1, width)
        small = jnp.concatenate([table + other_table, hidden_small], axis=0)
        chip_rows = 2 * own_rows
        fill = round_up(chip_rows + small.shape[0], 16) - chip_rows - small.shape[0]
        small = jnp.pad(small, ((0, fill), (0, cut - width)))
        pieces, _, project_last = gather_chips(jnp.concatenate([both[:, :cut], small], axis=0))
        attend16 = assemble(pieces, chip, chip_rows).reshape(width, cut)
        project16 = attend16[:, : 3 * half_width]
        output_own = attend16[:, 3 * half_width :]
        output_other = partner(output_own)
        output16 = jnp.concatenate(
            [by_core(output_own, output_other), by_core(output_other, output_own)], axis=1
        )
        output16 = lax.dynamic_slice_in_dim(output16, core * half_width, half_width, 0)
        smalls = 0.0
        for _, lower, piece in pieces:
            if lower + piece.shape[0] > chip_rows:
                smalls = smalls + piece[max(chip_rows - lower, 0) :, :width].astype(f32)
        gain_rows, bias_rows = smalls[:2], smalls[2:tables]
        hidden_row = smalls[tables : tables + hidden_half // width].reshape(-1)

        home_lengths = jnp.where(core == home, lengths, partner(lengths))
        length = lax.dynamic_slice_in_dim(home_lengths, (plane * group) % seqs_here, group, 0)
        starts = (plane - jnp.arange(planes)) % planes * slice_len
        limits = length[:, None] - starts[None, :]

        own_bias = by_core(bias_rows[:2, :half_width], bias_rows[:2, half_width:])
        shift = jnp.concatenate([own_bias[0], jnp.zeros_like(own_bias[0]), own_bias[1]])
        packed = (dot(tokens16, project16) + shift).astype(bf16)
        context16, log_total = attend_forward(packed, limits, half_width)

        pieces, _, _ = gather_chips(both[:, cut:], project_last, (context16,))
        up16 = assemble(pieces, chip, chip_rows).reshape(width, hidden_half)
        inner_part = dot(context16, output16)
        other_context16 = partner(context16)
        inner_sum = tokens16.astype(f32) + (inner_part + partner(inner_part)) + bias_rows[2]
        after_attend, norm_one, recip_one = layer_norm(inner_sum, gain_rows[0], bias_rows[3])
        after_attend16 = after_attend.astype(bf16)
        upstream16 = to_sequences(cotangent, (), (inner_part,))
        pre_act = dot(after_attend16, up16) + hidden_row
        activated16 = gelu_exact(pre_act).astype(bf16)
        pieces, _, _ = gather_chips(down_weight.astype(bf16), (packed,), (context16,))
        down16 = assemble(pieces, chip, down_weight.shape[0]).reshape(hidden_half, width)
        outer_part = dot(activated16, down16)
        outer_sum = after_attend + (outer_part + partner(outer_part)) + bias_rows[4]
        final, norm_two, recip_two = layer_norm(outer_sum, gain_rows[1], bias_rows[5])

        upstream = upstream16.astype(f32)
        grad_outer = norm_back(upstream, norm_two, recip_two, gain_rows[1])
        grad_outer16 = grad_outer.astype(bf16)
        down_term = contract_first(activated16, grad_outer16).astype(bf16)
        grad_pre = contract_last(grad_outer16, down16) * gelu_slope(pre_act)
        grad_pre16 = grad_pre.astype(bf16)
        middle_part = contract_last(grad_pre16, up16)
        grad_middle = grad_outer + (middle_part + partner(middle_part))
        up_term = contract_first(after_attend16, grad_pre16).astype(bf16)
        block_output = from_sequences(final.astype(bf16), (middle_part,))
        grad_inner = norm_back(grad_middle, norm_one, recip_one, gain_rows[0])
        grad_inner16 = grad_inner.astype(bf16)
        grad_context16 = contract_last(grad_inner16, output16).astype(bf16)
        down_blocks = down_term.reshape(chips, planes, -1, width)
        down_sides = scatter_chips(
            (down_blocks[..., :half_width], down_blocks[..., half_width:]), chip, ((), (up_term,))
        )
        down_whole = reduce_planes(down_sides, plane, (grad_context16,))
        context_full = jnp.concatenate(
            [by_core(context16, other_context16), by_core(other_context16, context16)], axis=1
        )
        grad_half = by_core(grad_inner16[:, :half_width], grad_inner16[:, half_width:])
        output_term = contract_first(context_full, grad_half).astype(bf16)
        packed_grad = attend_backward(
            packed, context16, log_total, grad_context16, limits, half_width
        )
        up_blocks = up_term.reshape(chips, planes, -1, hidden_half)
        up_sides = scatter_chips(
            (up_blocks[..., : hidden_half // 2], up_blocks[..., hidden_half // 2 :]),
            chip,
            ((), (packed_grad,)),
        )
        up_whole = reduce_planes(up_sides, plane)
        project_term = contract_first(tokens16, packed_grad).astype(bf16)
        input_part = contract_last(packed_grad, project16)
        other_part = partner(input_part)
        input_sum = (grad_inner + (input_part + other_part)).astype(bf16)
        input_gradient = from_sequences(input_sum)

        packed_sum = jnp.sum(packed_grad.astype(f32), axis=0)
        edge = jnp.stack([packed_sum[:half_width], packed_sum[2 * half_width :]])
        blank = jnp.zeros_like(edge)
        edge = by_core(
            jnp.concatenate([edge, blank], axis=1), jnp.concatenate([blank, edge], axis=1)
        )
        wide_terms = jnp.stack(
            [
                jnp.sum(grad_middle * norm_one, axis=0),
                jnp.sum(upstream * norm_two, axis=0),
                jnp.sum(grad_inner, axis=0),
                jnp.sum(grad_middle, axis=0),
                jnp.sum(grad_outer, axis=0),
                jnp.sum(upstream, axis=0),
            ]
        )
        hidden_term = jnp.sum(grad_pre, axis=0).reshape(-1, width)
        small_terms = jnp.concatenate([edge, wide_terms, hidden_term], axis=0).astype(bf16)
        small_rows = round_up(small_terms.shape[0], 16)
        small_terms = jnp.pad(small_terms, ((0, small_rows - small_terms.shape[0]), (0, 0)))
        small_terms = jnp.concatenate(
            [small_terms[None], jnp.zeros((planes - 1, small_rows, width), bf16)], axis=0
        )
        small_terms = jnp.broadcast_to(small_terms[None], (chips,) + small_terms.shape)
        project_blocks = project_term.reshape(chips, planes, -1, 3 * half_width)
        output_blocks = output_term.reshape(chips, planes, -1, half_width)
        attend_sides = scatter_chips(
            (
                jnp.concatenate([project_blocks[..., :width], small_terms], axis=2),
                jnp.concatenate([project_blocks[..., width:], output_blocks], axis=3),
            ),
            chip,
        )
        attend_whole = reduce_planes(attend_sides, plane)

        def rows_of(whole, start, count):
            return whole[:, start : start + count].reshape(planes * count, -1)

        def swap_halves(term, extra):
            parts = term.reshape(2, own_rows, -1)
            sent = pick(parts, 1 - core)
            if extra is not None:
                sent = jnp.concatenate([sent, extra], axis=0)
            other = partner(sent)
            kept = pick(parts, core)
            rest = other[own_rows:]
            other = other[:own_rows]
            return by_core(kept, other), by_core(other, kept), rest

        quarter = down_whole.shape[1] // 2
        down_total = jnp.concatenate(
            [rows_of(down_whole, 0, quarter), rows_of(down_whole, quarter, quarter)], axis=1
        ).astype(f32)
        quarter = up_whole.shape[1] // 2
        up_term = jnp.concatenate(
            [rows_of(up_whole, 0, quarter), rows_of(up_whole, quarter, quarter)], axis=1
        )
        low, high, _ = swap_halves(up_term, None)
        up_total = join_columns(low, high, hidden_block).astype(f32)
        quarter = (attend_whole.shape[1] - small_rows) // 2
        attend_term = jnp.concatenate(
            [
                rows_of(attend_whole, 0, quarter),
                rows_of(attend_whole, quarter + small_rows, quarter),
            ],
            axis=1,
        )
        own_small = attend_whole[0, quarter : quarter + small_rows]
        low, high, other_small = swap_halves(
            attend_term, jnp.pad(own_small, ((0, 0), (0, cut - width)))
        )
        project_total = join_columns(
            low[:, : 3 * half_width], high[:, : 3 * half_width], half_width
        ).astype(f32)
        output_total = jnp.concatenate(
            [low[:, 3 * half_width :], high[:, 3 * half_width :]], axis=1
        ).astype(f32)
        own_small = own_small.astype(f32)
        table_total = jnp.concatenate(
            [own_small[:2] + other_small[:2, :width].astype(f32), own_small[2:8]], axis=0
        )
        own_table = lax.dynamic_slice(table_total, (0, member * own_rows), (8, own_rows))
        hidden_total = lax.dynamic_slice(
            own_small[8 : 8 + hidden_half // width].reshape(-1),
            (chip * hidden_block,),
            (hidden_block,),
        )
        gains_total = own_table[2:4]
        biases_total = jnp.concatenate([own_table[:2], own_table[4:]], axis=0)
        totals = (
            project_total,
            output_total,
            up_total,
            down_total,
            gains_total,
            biases_total,
            hidden_total,
        )
        decay_flags = (True, True, True, True, False, False, False)
        results = []
        for n in range(7):
            results.append(adam_step(masters[n], firsts[n], seconds[n], totals[n], decay_flags[n]))
        return (
            (block_output, input_gradient)
            + totals
            + tuple(outcome[0] for outcome in results)
            + tuple(outcome[1] for outcome in results)
            + tuple(outcome[2] for outcome in results)
        )

    return shards


def solution(mesh):
    tokens = P("fsdp", "seq", None)
    rows = P("fsdp", None)
    columns = P(None, "fsdp")
    flat = P("fsdp")
    params = (rows, rows, rows, rows, columns, columns, flat)
    shards = make_shards(mesh.shape["seq"], mesh.shape["fsdp"])

    return jax.shard_map(
        shards,
        mesh=mesh,
        in_specs=(tokens, tokens, flat) + params * 3,
        out_specs=(tokens, tokens) + params * 4,
        check_vma=False,
    )
```

```python
import jax
import jax.numpy as jnp
from jax import lax
from jax.experimental import pallas as pl
from jax.experimental.pallas import tpu as pltpu
from jax.sharding import PartitionSpec as P


HD = 64
ADAM_STEP = 3


beta_one = 0.9
beta_two = 0.999
learn_rate = 0.01
decay_rate = 0.01
adam_eps = 1e-08
norm_eps = 1e-05
half_root = 0.7071067811865476
gauss_peak = 0.3989422804014327

bf16 = jnp.bfloat16
f32 = jnp.float32


def layer_norm(summed, gain, shift):
    centred = summed - jnp.mean(summed, axis=-1, keepdims=True)
    spread = jnp.mean(centred * centred, axis=-1, keepdims=True)
    recip = lax.rsqrt(spread + norm_eps)
    normed = centred * recip
    return (normed * gain + shift, normed, recip)


def norm_back(upstream, normed, recip, gain):
    scaled = upstream * gain
    return recip * (
        scaled
        - jnp.mean(scaled, axis=-1, keepdims=True)
        - normed * jnp.mean(scaled * normed, axis=-1, keepdims=True)
    )


def gelu_exact(pre_act):
    return 0.5 * pre_act * (1.0 + lax.erf(pre_act * half_root))


def gelu_slope(pre_act):
    return (
        0.5 * (1.0 + lax.erf(pre_act * half_root))
        + pre_act * jnp.exp(-0.5 * pre_act * pre_act) * gauss_peak
    )


def dot(left, right):
    return jnp.dot(left, right, preferred_element_type=f32)


def contract_last(left, right):
    return lax.dot_general(left, right, (((1,), (1,)), ((), ())), preferred_element_type=f32)


def contract_first(left, right):
    return lax.dot_general(left, right, (((0,), (0,)), ((), ())), preferred_element_type=f32)


def pick(array, index, axis=0):
    return lax.dynamic_index_in_dim(array, index, axis, keepdims=False)


def after(value, *others):
    return lax.optimization_barrier((value,) + others)[0] if others else value


def round_up(value, unit):
    return -(-value // unit) * unit


def adam_step(master, first, second, gradient, with_decay):
    first_new = beta_one * first + (1.0 - beta_one) * gradient
    second_new = beta_two * second + (1.0 - beta_two) * gradient * gradient
    first_hat = first_new / (1.0 - beta_one**ADAM_STEP)
    second_hat = second_new / (1.0 - beta_two**ADAM_STEP)
    change = first_hat / (jnp.sqrt(second_hat) + adam_eps)
    if with_decay:
        change = change + decay_rate * master
    return (master - learn_rate * change, first_new, second_new)


LANES = 128


def keep_rows(limits_ref, group_at, planes, slice_len):
    rows = lax.broadcasted_iota(jnp.int32, (slice_len, 1), 0)
    return jnp.concatenate(
        [rows < limits_ref[group_at, step] for step in range(planes)], axis=0
    )


def head_mask(shape, place):
    lane = lax.broadcasted_iota(jnp.int32, shape, 1)
    return (lane >= place * HD) & (lane < (place + 1) * HD)


def forward_kernel(limits_ref, query_ref, key_ref, value_ref, context_ref, log_ref):
    planes = limits_ref.shape[1]
    length = query_ref.shape[0]
    keep = keep_rows(limits_ref, pl.program_id(0), planes, length // planes)
    query = query_ref[...] * jnp.asarray(HD**-0.5, bf16)
    key = key_ref[...]
    value = value_ref[...]
    total = None
    for place in range(LANES // HD):
        own = head_mask(query.shape, place)
        zero = jnp.zeros_like(query)
        scores = contract_last(key, jnp.where(own, query, zero))
        scores = jnp.where(keep, scores, -jnp.inf)
        row_max = jnp.max(scores, axis=0, keepdims=True)
        lifted = jnp.exp(scores - row_max)
        row_total = jnp.sum(lifted, axis=0, keepdims=True)
        weights16 = (lifted * (1.0 / row_total)).astype(bf16)
        part = contract_first(jnp.where(own, value, zero), weights16)
        total = part if total is None else total + part
        log_ref[0, place : place + 1, :] = row_max + jnp.log(row_total)
    context_ref[...] = jnp.transpose(total).astype(bf16)


def backward_kernel(
    limits_ref,
    query_ref,
    key_ref,
    value_ref,
    context_ref,
    log_ref,
    upstream_ref,
    grads_ref,
):
    planes = limits_ref.shape[1]
    length = query_ref.shape[0]
    keep = keep_rows(limits_ref, pl.program_id(0), planes, length // planes)
    scale = HD**-0.5
    query = query_ref[...] * jnp.asarray(scale, bf16)
    key = key_ref[...]
    value = value_ref[...]
    upstream = upstream_ref[...]
    offsets = jnp.transpose(upstream.astype(f32) * context_ref[...].astype(f32))
    zero = jnp.zeros_like(query)
    query_grad, key_grad, value_grad = None, None, None
    for place in range(LANES // HD):
        own = head_mask(query.shape, place)
        own_query = jnp.where(own, query, zero)
        own_upstream = jnp.where(own, upstream, zero)
        scores = contract_last(key, own_query)
        attention = jnp.exp(scores - log_ref[0, place : place + 1, :])
        attention = jnp.where(keep, attention, 0.0)
        part = dot(attention.astype(bf16), own_upstream)
        value_grad = part if value_grad is None else value_grad + part
        prob_grad = contract_last(value, own_upstream)
        offset = jnp.sum(offsets[place * HD : (place + 1) * HD], axis=0, keepdims=True)
        score16 = (attention * (prob_grad - offset) * scale).astype(bf16)
        part = dot(score16, own_query)
        key_grad = part if key_grad is None else key_grad + part
        part = contract_first(jnp.where(own, key, zero), score16)
        query_grad = part if query_grad is None else query_grad + part
    width = grads_ref.shape[1] // 3
    start = pl.multiple_of(pl.program_id(1) * LANES, LANES)
    grads_ref[:, pl.ds(start, LANES)] = jnp.transpose(query_grad).astype(bf16)
    grads_ref[:, pl.ds(width + start, LANES)] = (key_grad * (1.0 / scale)).astype(bf16)
    grads_ref[:, pl.ds(2 * width + start, LANES)] = value_grad.astype(bf16)


def attend_forward(packed, limits, width):
    group, _ = limits.shape
    length = packed.shape[0] // group
    pairs = width // LANES
    places = LANES // HD

    def block(offset):
        return pl.BlockSpec((length, LANES), lambda g, j, limits: (g, offset + j))

    return pl.pallas_call(
        forward_kernel,
        out_shape=(
            jax.ShapeDtypeStruct((packed.shape[0], width), bf16),
            jax.ShapeDtypeStruct((group * pairs, places, length), f32),
        ),
        grid_spec=pltpu.PrefetchScalarGridSpec(
            num_scalar_prefetch=1,
            grid=(group, pairs),
            in_specs=[block(0), block(pairs), block(2 * pairs)],
            out_specs=[
                block(0),
                pl.BlockSpec((1, places, length), lambda g, j, limits: (g * pairs + j, 0, 0)),
            ],
        ),
        cost_estimate=pl.CostEstimate(
            flops=4 * packed.shape[0] * length * width,
            bytes_accessed=packed.size * 3,
            transcendentals=packed.shape[0] * length * width // HD,
        ),
        name="attend_forward",
    )(limits, packed, packed, packed)


def attend_backward(packed, context16, log_total, upstream16, limits, width):
    group, _ = limits.shape
    length = packed.shape[0] // group
    pairs = width // LANES
    places = LANES // HD

    def block(offset):
        return pl.BlockSpec((length, LANES), lambda g, j, limits: (g, offset + j))

    return pl.pallas_call(
        backward_kernel,
        out_shape=jax.ShapeDtypeStruct(packed.shape, bf16),
        grid_spec=pltpu.PrefetchScalarGridSpec(
            num_scalar_prefetch=1,
            grid=(group, pairs),
            in_specs=[
                block(0),
                block(pairs),
                block(2 * pairs),
                block(0),
                pl.BlockSpec((1, places, length), lambda g, j, limits: (g * pairs + j, 0, 0)),
                block(0),
            ],
            out_specs=pl.BlockSpec((length, packed.shape[1]), lambda g, j, limits: (g, 0)),
        ),
        cost_estimate=pl.CostEstimate(
            flops=10 * packed.shape[0] * length * width,
            bytes_accessed=packed.size * 6,
            transcendentals=packed.shape[0] * length * width // HD,
        ),
        name="attend_backward",
    )(limits, packed, packed, packed, context16, log_total, upstream16)


def make_shards(planes, members):
    chips = members // 2
    bits = [1 << bit for bit in range(chips.bit_length() - 1)]
    axes = ("seq", "fsdp")

    def swap(value, mask):
        return lax.ppermute(value, "fsdp", [(i, i ^ mask) for i in range(members)])

    def partner(value):
        return swap(value, 1)

    def along(value, step):
        return lax.ppermute(value, "seq", [(i, (i + step) % planes) for i in range(planes)])

    def gather_chips(own, first=(), later=()):
        rows = own.shape[0]
        half = max(rows // 32 * 16, 1)
        direct = {}
        sent = after(own, *first)
        for bit in bits:
            direct[bit] = swap(sent, 2 * bit)
        pieces = [(0, 0, own)] + [(bit, 0, direct[bit]) for bit in bits]
        last = ()
        for lower, upper, order in ((0, half, bits), (half, rows, bits[::-1])):
            held = {0: own[lower:upper]}
            for bit in order:
                far = [rel for rel in held if rel]
                fresh = {bit: direct[bit][lower:upper]}
                if far:
                    batch = held[far[0]] if len(far) == 1 else jnp.concatenate([held[r] for r in far])
                    moved = swap(after(batch, *later), 2 * bit)
                    size = upper - lower
                    for place, rel in enumerate(far):
                        fresh[rel | bit] = moved[place * size : (place + 1) * size]
                        pieces.append((rel | bit, lower, fresh[rel | bit]))
                        last += (fresh[rel | bit],)
                held.update(fresh)
        return pieces, tuple(direct.values()), last

    def assemble(pieces, chip, rows):
        width = pieces[0][2].shape[1]
        whole = jnp.zeros((chips, rows, width), pieces[0][2].dtype)
        for rel, lower, piece in pieces:
            used = min(piece.shape[0], rows - lower)
            if used > 0:
                whole = lax.dynamic_update_slice(
                    whole, piece[None, :used], (chip ^ rel, lower, 0)
                )
        return whole

    def total_of(terms):
        whole = terms[0].astype(f32)
        for term in terms[1:]:
            whole = whole + term.astype(f32)
        return whole

    def scatter_chips(sides, chip, holds=()):
        outs = []
        for block, order in zip(sides, (bits[::-1], bits)):
            terms = [block.reshape((2,) * len(bits) + block.shape[1:])]
            left = bits[::-1]
            for turn, bit in enumerate(order):
                axis = left.index(bit)
                left = [other for other in left if other != bit]
                mine = (chip // bit) % 2
                sent = total_of([pick(term, 1 - mine, axis) for term in terms]).astype(bf16)
                if turn < len(holds):
                    sent = after(sent, *holds[turn])
                terms = [pick(term, mine, axis) for term in terms]
                terms.append(swap(sent, 2 * bit))
            outs.append(terms)
        return outs

    def reduce_planes(sides, plane, hold=()):
        def quarter(index):
            return jnp.concatenate(
                [total_of([pick(term, index) for term in terms]) for terms in sides], axis=0
            )

        arrived = []
        for step in range(1, planes):
            sent = quarter((plane + step) % planes).astype(bf16)
            arrived.append(along(after(sent, *hold), step))
        total = total_of([quarter(plane)] + arrived).astype(bf16)
        whole = jnp.zeros((planes,) + total.shape, bf16)
        whole = lax.dynamic_update_slice(whole, total[None], (plane, 0, 0))
        for step in range(1, planes):
            moved = along(total, step)
            whole = lax.dynamic_update_slice(whole, moved[None], ((plane - step) % planes, 0, 0))
        return whole

    def reduce_line(sides, plane, hold=()):
        if planes != 4:
            whole = reduce_planes(sides, plane, hold)
            count = whole.shape[1] // len(sides)
            return jnp.concatenate(
                [
                    whole[:, start : start + count].reshape(planes * count, -1)
                    for start in range(0, whole.shape[1], count)
                ],
                axis=1,
            )

        def line(value, pairs):
            return lax.ppermute(value, "seq", pairs)

        def flat(terms):
            return total_of([term.reshape(-1, term.shape[-1]) for term in terms])

        own = jnp.concatenate([flat(terms) for terms in sides], axis=1).astype(bf16)
        own = after(own, *hold)
        own = total_of([own, line(own, [(0, 1), (3, 2)])]).astype(bf16)
        own = total_of([own, line(own, [(1, 2), (2, 1)])]).astype(bf16)
        other = line(own, [(1, 0), (2, 3)])
        return jnp.where((plane == 1) | (plane == 2), own, other)

    def shards(
        layer_input,
        cotangent,
        lengths,
        project_weight,
        output_weight,
        up_weight,
        down_weight,
        norm_gains,
        biases,
        hidden_bias,
        *moments,
    ):
        masters = (
            project_weight,
            output_weight,
            up_weight,
            down_weight,
            norm_gains,
            biases,
            hidden_bias,
        )
        firsts, seconds = moments[:7], moments[7:]
        seqs_here, slice_len, width = layer_input.shape
        own_rows = project_weight.shape[0]
        hidden_width = up_weight.shape[1]
        hidden_half = hidden_width // 2
        hidden_block = hidden_width // members
        half_width = width // 2
        group = 2 * seqs_here // planes
        turns = seqs_here // group
        plane = lax.axis_index("seq")
        member = lax.axis_index("fsdp")
        chip, core = member // 2, member % 2
        home = plane * group // seqs_here

        def home_of(plane_at):
            return plane_at * group // seqs_here

        def to_sequences(array, first=(), later=()):
            array = after(array, *first)
            blocks = []
            for step in range(planes):
                target = (plane + step) % planes
                block = lax.dynamic_slice_in_dim(array, (target * group) % seqs_here, group, 0)
                if step:
                    pairs = []
                    for source in range(planes):
                        there = (source + step) % planes
                        for one in range(chips):
                            at = 2 * one + home_of(there)
                            pairs.append((source * members + at, there * members + at))
                    block = lax.ppermute(block, axes, pairs)
                blocks.append(block)
            mine = jnp.stack(blocks, axis=1).reshape(group * planes * slice_len, width)
            return jnp.where(core == home, mine, partner(after(mine, *later)))

        def from_sequences(array, hold=()):
            blocks = after(array, *hold).reshape(group, planes, slice_len, width)
            arrived = [blocks[:, 0]]
            for step in range(1, planes):
                pairs = []
                for source in range(planes):
                    there = (source - step) % planes
                    for one in range(chips):
                        at = 2 * one + home_of(source)
                        pairs.append((source * members + at, there * members + at))
                arrived.append(lax.ppermute(blocks[:, step], axes, pairs))
            slots = []
            for turn in range(turns):
                step_at = (core * turns + turn - plane) % planes
                value = arrived[0]
                for step in range(1, planes):
                    value = jnp.where(step_at == step, arrived[step], value)
                slots.append(value)
            return jnp.concatenate(slots, axis=0)

        def by_core(low, high):
            return jnp.where(core == 0, low, high)

        def split_columns(array, block):
            pieces = [
                array[:, start : start + block] for start in range(0, array.shape[1], block)
            ]
            return jnp.concatenate(pieces[::2], axis=1), jnp.concatenate(pieces[1::2], axis=1)

        def join_columns(low, high, block):
            pieces = []
            for start in range(0, low.shape[1], block):
                pieces += [low[:, start : start + block], high[:, start : start + block]]
            return jnp.concatenate(pieces, axis=1)

        tokens16 = to_sequences(layer_input)
        project_low, project_high = split_columns(project_weight, half_width)
        up_low, up_high = split_columns(up_weight, hidden_block)
        output_low, output_high = split_columns(output_weight, half_width)
        low_cols = jnp.concatenate([project_low, output_low, up_low], axis=1).astype(bf16)
        high_cols = jnp.concatenate([project_high, output_high, up_high], axis=1).astype(bf16)
        table = jnp.concatenate([norm_gains, biases], axis=0).astype(bf16)
        tables = table.shape[0]
        table = lax.dynamic_update_slice(
            jnp.zeros((tables, width), bf16), table, (0, member * own_rows)
        )
        kept_cols = by_core(low_cols, high_cols)
        cut = 4 * half_width
        spare = jnp.pad(table, ((0, 16 - tables), (0, low_cols.shape[1] - width)))
        swapped = partner(jnp.concatenate([by_core(high_cols, low_cols), spare], axis=0))
        other_table = swapped[own_rows : own_rows + tables, :width]
        swapped = swapped[:own_rows]
        both = jnp.concatenate([by_core(kept_cols, swapped), by_core(swapped, kept_cols)], axis=0)
        hidden_small = lax.dynamic_update_slice(
            jnp.zeros((hidden_half,), bf16), hidden_bias.astype(bf16), (chip * hidden_block,)
        ).reshape(-1, width)
        small = jnp.concatenate([table + other_table, hidden_small], axis=0)
        chip_rows = 2 * own_rows
        fill = round_up(chip_rows + small.shape[0], 16) - chip_rows - small.shape[0]
        small = jnp.pad(small, ((0, fill), (0, cut - width)))
        pieces, _, project_last = gather_chips(jnp.concatenate([both[:, :cut], small], axis=0))
        attend16 = assemble(pieces, chip, chip_rows).reshape(width, cut)
        project16 = attend16[:, : 3 * half_width]
        output_own = attend16[:, 3 * half_width :]
        output_other = partner(output_own)
        output16 = jnp.concatenate(
            [by_core(output_own, output_other), by_core(output_other, output_own)], axis=1
        )
        output16 = lax.dynamic_slice_in_dim(output16, core * half_width, half_width, 0)
        smalls = 0.0
        for _, lower, piece in pieces:
            if lower + piece.shape[0] > chip_rows:
                smalls = smalls + piece[max(chip_rows - lower, 0) :, :width].astype(f32)
        gain_rows, bias_rows = smalls[:2], smalls[2:tables]
        hidden_row = smalls[tables : tables + hidden_half // width].reshape(-1)

        home_lengths = jnp.where(core == home, lengths, partner(lengths))
        length = lax.dynamic_slice_in_dim(home_lengths, (plane * group) % seqs_here, group, 0)
        starts = (plane - jnp.arange(planes)) % planes * slice_len
        limits = length[:, None] - starts[None, :]

        own_bias = by_core(bias_rows[:2, :half_width], bias_rows[:2, half_width:])
        shift = jnp.concatenate([own_bias[0], jnp.zeros_like(own_bias[0]), own_bias[1]])
        packed = (dot(tokens16, project16) + shift).astype(bf16)
        context16, log_total = attend_forward(packed, limits, half_width)

        pieces, _, _ = gather_chips(both[:, cut:], project_last, (context16,))
        up16 = assemble(pieces, chip, chip_rows).reshape(width, hidden_half)
        inner_part = dot(context16, output16)
        other_context16 = partner(context16)
        inner_sum = tokens16.astype(f32) + (inner_part + partner(inner_part)) + bias_rows[2]
        after_attend, norm_one, recip_one = layer_norm(inner_sum, gain_rows[0], bias_rows[3])
        after_attend16 = after_attend.astype(bf16)
        upstream16 = to_sequences(cotangent, (), (inner_part,))
        pre_act = dot(after_attend16, up16) + hidden_row
        activated16 = gelu_exact(pre_act).astype(bf16)
        pieces, _, _ = gather_chips(down_weight.astype(bf16), (packed,), (context16,))
        down16 = assemble(pieces, chip, down_weight.shape[0]).reshape(hidden_half, width)
        outer_part = dot(activated16, down16)
        outer_sum = after_attend + (outer_part + partner(outer_part)) + bias_rows[4]
        final, norm_two, recip_two = layer_norm(outer_sum, gain_rows[1], bias_rows[5])

        upstream = upstream16.astype(f32)
        grad_outer = norm_back(upstream, norm_two, recip_two, gain_rows[1])
        grad_outer16 = grad_outer.astype(bf16)
        down_term = contract_first(activated16, grad_outer16).astype(bf16)
        grad_pre = contract_last(grad_outer16, down16) * gelu_slope(pre_act)
        grad_pre16 = grad_pre.astype(bf16)
        middle_part = contract_last(grad_pre16, up16)
        grad_middle = grad_outer + (middle_part + partner(middle_part))
        up_term = contract_first(after_attend16, grad_pre16).astype(bf16)
        grad_inner = norm_back(grad_middle, norm_one, recip_one, gain_rows[0])
        grad_inner16 = grad_inner.astype(bf16)
        grad_context16 = contract_last(grad_inner16, output16).astype(bf16)
        block_output = from_sequences(final.astype(bf16), (grad_context16,))
        down_blocks = down_term.reshape(chips, planes, -1, width)
        down_sides = scatter_chips(
            (down_blocks[..., :half_width], down_blocks[..., half_width:]), chip, ((), (up_term,))
        )
        down_total = reduce_line(down_sides, plane, (grad_context16,))
        context_full = jnp.concatenate(
            [by_core(context16, other_context16), by_core(other_context16, context16)], axis=1
        )
        grad_half = by_core(grad_inner16[:, :half_width], grad_inner16[:, half_width:])
        output_term = contract_first(context_full, grad_half).astype(bf16)
        packed_grad = attend_backward(
            packed, context16, log_total, grad_context16, limits, half_width
        )
        up_blocks = up_term.reshape(chips, planes, -1, hidden_half)
        up_sides = scatter_chips(
            (up_blocks[..., : hidden_half // 2], up_blocks[..., hidden_half // 2 :]),
            chip,
            ((), (packed_grad,)),
        )
        up_total = reduce_line(up_sides, plane)
        project_term = contract_first(tokens16, packed_grad).astype(bf16)
        input_part = contract_last(packed_grad, project16)
        other_part = partner(input_part)
        input_sum = (grad_inner + (input_part + other_part)).astype(bf16)
        input_gradient = from_sequences(input_sum)

        packed_sum = jnp.sum(packed_grad.astype(f32), axis=0)
        edge = jnp.stack([packed_sum[:half_width], packed_sum[2 * half_width :]])
        blank = jnp.zeros_like(edge)
        edge = by_core(
            jnp.concatenate([edge, blank], axis=1), jnp.concatenate([blank, edge], axis=1)
        )
        wide_terms = jnp.stack(
            [
                jnp.sum(grad_middle * norm_one, axis=0),
                jnp.sum(upstream * norm_two, axis=0),
                jnp.sum(grad_inner, axis=0),
                jnp.sum(grad_middle, axis=0),
                jnp.sum(grad_outer, axis=0),
                jnp.sum(upstream, axis=0),
            ]
        )
        hidden_term = jnp.sum(grad_pre, axis=0).reshape(-1, width)
        small_terms = jnp.concatenate([edge, wide_terms, hidden_term], axis=0).astype(bf16)
        small_rows = round_up(small_terms.shape[0], 16)
        small_terms = jnp.pad(small_terms, ((0, small_rows - small_terms.shape[0]), (0, 0)))
        small_terms = jnp.concatenate(
            [small_terms[None], jnp.zeros((planes - 1, small_rows, width), bf16)], axis=0
        )
        small_terms = jnp.broadcast_to(small_terms[None], (chips,) + small_terms.shape)
        project_blocks = project_term.reshape(chips, planes, -1, 3 * half_width)
        output_blocks = output_term.reshape(chips, planes, -1, half_width)
        attend_sides = scatter_chips(
            (
                jnp.concatenate([project_blocks[..., :width], small_terms], axis=2),
                jnp.concatenate([project_blocks[..., width:], output_blocks], axis=3),
            ),
            chip,
        )
        attend_whole = reduce_planes(attend_sides, plane)

        def rows_of(whole, start, count):
            return whole[:, start : start + count].reshape(planes * count, -1)

        def swap_halves(term, extra):
            parts = term.reshape(2, own_rows, -1)
            sent = pick(parts, 1 - core)
            if extra is not None:
                sent = jnp.concatenate([sent, extra], axis=0)
            other = partner(sent)
            kept = pick(parts, core)
            rest = other[own_rows:]
            other = other[:own_rows]
            return by_core(kept, other), by_core(other, kept), rest

        down_total = down_total.astype(f32)
        low, high, _ = swap_halves(up_total, None)
        up_total = join_columns(low, high, hidden_block).astype(f32)
        quarter = (attend_whole.shape[1] - small_rows) // 2
        attend_term = jnp.concatenate(
            [
                rows_of(attend_whole, 0, quarter),
                rows_of(attend_whole, quarter + small_rows, quarter),
            ],
            axis=1,
        )
        own_small = attend_whole[0, quarter : quarter + small_rows]
        low, high, other_small = swap_halves(
            attend_term, jnp.pad(own_small, ((0, 0), (0, cut - width)))
        )
        project_total = join_columns(
            low[:, : 3 * half_width], high[:, : 3 * half_width], half_width
        ).astype(f32)
        output_total = jnp.concatenate(
            [low[:, 3 * half_width :], high[:, 3 * half_width :]], axis=1
        ).astype(f32)
        own_small = own_small.astype(f32)
        table_total = jnp.concatenate(
            [own_small[:2] + other_small[:2, :width].astype(f32), own_small[2:8]], axis=0
        )
        own_table = lax.dynamic_slice(table_total, (0, member * own_rows), (8, own_rows))
        hidden_total = lax.dynamic_slice(
            own_small[8 : 8 + hidden_half // width].reshape(-1),
            (chip * hidden_block,),
            (hidden_block,),
        )
        gains_total = own_table[2:4]
        biases_total = jnp.concatenate([own_table[:2], own_table[4:]], axis=0)
        totals = (
            project_total,
            output_total,
            up_total,
            down_total,
            gains_total,
            biases_total,
            hidden_total,
        )
        decay_flags = (True, True, True, True, False, False, False)
        results = []
        for n in range(7):
            results.append(adam_step(masters[n], firsts[n], seconds[n], totals[n], decay_flags[n]))
        return (
            (block_output, input_gradient)
            + totals
            + tuple(outcome[0] for outcome in results)
            + tuple(outcome[1] for outcome in results)
            + tuple(outcome[2] for outcome in results)
        )

    return shards


def solution(mesh):
    tokens = P("fsdp", "seq", None)
    rows = P("fsdp", None)
    columns = P(None, "fsdp")
    flat = P("fsdp")
    params = (rows, rows, rows, rows, columns, columns, flat)
    shards = make_shards(mesh.shape["seq"], mesh.shape["fsdp"])

    return jax.shard_map(
        shards,
        mesh=mesh,
        in_specs=(tokens, tokens, flat) + params * 3,
        out_specs=(tokens, tokens) + params * 4,
        check_vma=False,
    )
```

```python
import jax
import jax.numpy as jnp
from jax import lax
from jax.experimental import pallas as pl
from jax.experimental.pallas import tpu as pltpu
from jax.sharding import PartitionSpec as P


HD = 64
ADAM_STEP = 3


beta_one = 0.9
beta_two = 0.999
learn_rate = 0.01
decay_rate = 0.01
adam_eps = 1e-08
norm_eps = 1e-05
half_root = 0.7071067811865476
gauss_peak = 0.3989422804014327

bf16 = jnp.bfloat16
f32 = jnp.float32


def layer_norm(summed, gain, shift):
    centred = summed - jnp.mean(summed, axis=-1, keepdims=True)
    spread = jnp.mean(centred * centred, axis=-1, keepdims=True)
    recip = lax.rsqrt(spread + norm_eps)
    normed = centred * recip
    return (normed * gain + shift, normed, recip)


def norm_back(upstream, normed, recip, gain):
    scaled = upstream * gain
    return recip * (
        scaled
        - jnp.mean(scaled, axis=-1, keepdims=True)
        - normed * jnp.mean(scaled * normed, axis=-1, keepdims=True)
    )


def gelu_exact(pre_act):
    return 0.5 * pre_act * (1.0 + lax.erf(pre_act * half_root))


def gelu_slope(pre_act):
    return (
        0.5 * (1.0 + lax.erf(pre_act * half_root))
        + pre_act * jnp.exp(-0.5 * pre_act * pre_act) * gauss_peak
    )


def dot(left, right):
    return jnp.dot(left, right, preferred_element_type=f32)


def contract_last(left, right):
    return lax.dot_general(left, right, (((1,), (1,)), ((), ())), preferred_element_type=f32)


def contract_first(left, right):
    return lax.dot_general(left, right, (((0,), (0,)), ((), ())), preferred_element_type=f32)


def pick(array, index, axis=0):
    return lax.dynamic_index_in_dim(array, index, axis, keepdims=False)


def after(value, *others):
    return lax.optimization_barrier((value,) + others)[0] if others else value


def round_up(value, unit):
    return -(-value // unit) * unit


def adam_step(master, first, second, gradient, with_decay):
    first_new = beta_one * first + (1.0 - beta_one) * gradient
    second_new = beta_two * second + (1.0 - beta_two) * gradient * gradient
    first_hat = first_new / (1.0 - beta_one**ADAM_STEP)
    second_hat = second_new / (1.0 - beta_two**ADAM_STEP)
    change = first_hat / (jnp.sqrt(second_hat) + adam_eps)
    if with_decay:
        change = change + decay_rate * master
    return (master - learn_rate * change, first_new, second_new)


LANES = 128


def keep_rows(limits_ref, group_at, planes, slice_len):
    rows = lax.broadcasted_iota(jnp.int32, (slice_len, 1), 0)
    return jnp.concatenate(
        [rows < limits_ref[group_at, step] for step in range(planes)], axis=0
    )


def head_mask(shape, place):
    lane = lax.broadcasted_iota(jnp.int32, shape, 1)
    return (lane >= place * HD) & (lane < (place + 1) * HD)


def forward_kernel(limits_ref, query_ref, key_ref, value_ref, context_ref, log_ref):
    planes = limits_ref.shape[1]
    length = query_ref.shape[0]
    keep = keep_rows(limits_ref, pl.program_id(0), planes, length // planes)
    query = query_ref[...] * jnp.asarray(HD**-0.5, bf16)
    key = key_ref[...]
    value = value_ref[...]
    total = None
    for place in range(LANES // HD):
        own = head_mask(query.shape, place)
        zero = jnp.zeros_like(query)
        scores = contract_last(key, jnp.where(own, query, zero))
        scores = jnp.where(keep, scores, -jnp.inf)
        row_max = jnp.max(scores, axis=0, keepdims=True)
        lifted = jnp.exp(scores - row_max)
        row_total = jnp.sum(lifted, axis=0, keepdims=True)
        weights16 = (lifted * (1.0 / row_total)).astype(bf16)
        part = contract_first(jnp.where(own, value, zero), weights16)
        total = part if total is None else total + part
        log_ref[0, place : place + 1, :] = row_max + jnp.log(row_total)
    context_ref[...] = jnp.transpose(total).astype(bf16)


def backward_kernel(
    limits_ref,
    query_ref,
    key_ref,
    value_ref,
    context_ref,
    log_ref,
    upstream_ref,
    grads_ref,
):
    planes = limits_ref.shape[1]
    length = query_ref.shape[0]
    keep = keep_rows(limits_ref, pl.program_id(0), planes, length // planes)
    scale = HD**-0.5
    query = query_ref[...] * jnp.asarray(scale, bf16)
    key = key_ref[...]
    value = value_ref[...]
    upstream = upstream_ref[...]
    offsets = jnp.transpose(upstream.astype(f32) * context_ref[...].astype(f32))
    zero = jnp.zeros_like(query)
    query_grad, key_grad, value_grad = None, None, None
    for place in range(LANES // HD):
        own = head_mask(query.shape, place)
        own_query = jnp.where(own, query, zero)
        own_upstream = jnp.where(own, upstream, zero)
        scores = contract_last(key, own_query)
        attention = jnp.exp(scores - log_ref[0, place : place + 1, :])
        attention = jnp.where(keep, attention, 0.0)
        part = dot(attention.astype(bf16), own_upstream)
        value_grad = part if value_grad is None else value_grad + part
        prob_grad = contract_last(value, own_upstream)
        offset = jnp.sum(offsets[place * HD : (place + 1) * HD], axis=0, keepdims=True)
        score16 = (attention * (prob_grad - offset) * scale).astype(bf16)
        part = dot(score16, own_query)
        key_grad = part if key_grad is None else key_grad + part
        part = contract_first(jnp.where(own, key, zero), score16)
        query_grad = part if query_grad is None else query_grad + part
    width = grads_ref.shape[1] // 3
    start = pl.multiple_of(pl.program_id(1) * LANES, LANES)
    grads_ref[:, pl.ds(start, LANES)] = jnp.transpose(query_grad).astype(bf16)
    grads_ref[:, pl.ds(width + start, LANES)] = (key_grad * (1.0 / scale)).astype(bf16)
    grads_ref[:, pl.ds(2 * width + start, LANES)] = value_grad.astype(bf16)


def attend_forward(packed, limits, width):
    group, _ = limits.shape
    length = packed.shape[0] // group
    pairs = width // LANES
    places = LANES // HD

    def block(offset):
        return pl.BlockSpec((length, LANES), lambda g, j, limits: (g, offset + j))

    return pl.pallas_call(
        forward_kernel,
        out_shape=(
            jax.ShapeDtypeStruct((packed.shape[0], width), bf16),
            jax.ShapeDtypeStruct((group * pairs, places, length), f32),
        ),
        grid_spec=pltpu.PrefetchScalarGridSpec(
            num_scalar_prefetch=1,
            grid=(group, pairs),
            in_specs=[block(0), block(pairs), block(2 * pairs)],
            out_specs=[
                block(0),
                pl.BlockSpec((1, places, length), lambda g, j, limits: (g * pairs + j, 0, 0)),
            ],
        ),
        cost_estimate=pl.CostEstimate(
            flops=4 * packed.shape[0] * length * width,
            bytes_accessed=packed.size * 3,
            transcendentals=packed.shape[0] * length * width // HD,
        ),
        name="attend_forward",
    )(limits, packed, packed, packed)


def attend_backward(packed, context16, log_total, upstream16, limits, width):
    group, _ = limits.shape
    length = packed.shape[0] // group
    pairs = width // LANES
    places = LANES // HD

    def block(offset):
        return pl.BlockSpec((length, LANES), lambda g, j, limits: (g, offset + j))

    return pl.pallas_call(
        backward_kernel,
        out_shape=jax.ShapeDtypeStruct(packed.shape, bf16),
        grid_spec=pltpu.PrefetchScalarGridSpec(
            num_scalar_prefetch=1,
            grid=(group, pairs),
            in_specs=[
                block(0),
                block(pairs),
                block(2 * pairs),
                block(0),
                pl.BlockSpec((1, places, length), lambda g, j, limits: (g * pairs + j, 0, 0)),
                block(0),
            ],
            out_specs=pl.BlockSpec((length, packed.shape[1]), lambda g, j, limits: (g, 0)),
        ),
        cost_estimate=pl.CostEstimate(
            flops=10 * packed.shape[0] * length * width,
            bytes_accessed=packed.size * 6,
            transcendentals=packed.shape[0] * length * width // HD,
        ),
        name="attend_backward",
    )(limits, packed, packed, packed, context16, log_total, upstream16)


def block_sums(place, outputs):
    arrays, specs, layouts = [], [], []
    for shape, cells in outputs:
        layout = []
        for row, col, rows, width, terms in cells:
            layout.append((row, col, rows, width, len(terms)))
            for array, column, choose in terms:
                arrays.append(array)
                specs.append(
                    pl.BlockSpec(
                        (1, rows, width),
                        lambda i, at, choose=choose, column=column: (choose(at), 0, column),
                    )
                )
        layouts.append(layout)

    def kernel(place_ref, *refs):
        sources, targets = list(refs[: len(arrays)]), refs[len(arrays) :]
        for target, layout in zip(targets, layouts):
            for row, col, rows, width, count in layout:
                total = None
                for _ in range(count):
                    value = sources.pop(0)[0].astype(f32)
                    total = value if total is None else total + value
                target[row : row + rows, col : col + width] = total.astype(bf16)

    moved = sum(spec.block_shape[1] * spec.block_shape[2] for spec in specs)
    return pl.pallas_call(
        kernel,
        out_shape=[jax.ShapeDtypeStruct(shape, bf16) for shape, _ in outputs],
        grid_spec=pltpu.PrefetchScalarGridSpec(
            num_scalar_prefetch=1,
            grid=(1,),
            in_specs=specs,
            out_specs=[pl.BlockSpec(shape, lambda i, at: (0, 0)) for shape, _ in outputs],
        ),
        cost_estimate=pl.CostEstimate(flops=moved, bytes_accessed=4 * moved, transcendentals=0),
    )(place, *arrays)


def make_shards(planes, members):
    chips = members // 2
    bits = [1 << bit for bit in range(chips.bit_length() - 1)]
    axes = ("seq", "fsdp")

    def swap(value, mask):
        return lax.ppermute(value, "fsdp", [(i, i ^ mask) for i in range(members)])

    def partner(value):
        return swap(value, 1)

    def along(value, step):
        return lax.ppermute(value, "seq", [(i, (i + step) % planes) for i in range(planes)])

    def gather_chips(own, first=(), later=()):
        rows = own.shape[0]
        half = max(rows // 32 * 16, 1)
        direct = {}
        sent = after(own, *first)
        for bit in bits:
            direct[bit] = swap(sent, 2 * bit)
        pieces = [(0, 0, own)] + [(bit, 0, direct[bit]) for bit in bits]
        last = ()
        for lower, upper, order in ((0, half, bits), (half, rows, bits[::-1])):
            held = {0: own[lower:upper]}
            for bit in order:
                far = [rel for rel in held if rel]
                fresh = {bit: direct[bit][lower:upper]}
                if far:
                    batch = held[far[0]] if len(far) == 1 else jnp.concatenate([held[r] for r in far])
                    batch = after(batch, *later)
                    moved = swap(batch, 2 * bit)
                    size = upper - lower
                    for place, rel in enumerate(far):
                        fresh[rel | bit] = moved[place * size : (place + 1) * size]
                        pieces.append((rel | bit, lower, fresh[rel | bit]))
                        last += (fresh[rel | bit],)
                held.update(fresh)
        return pieces, tuple(direct.values()), last

    def assemble(pieces, chip, rows):
        width = pieces[0][2].shape[1]
        whole = jnp.zeros((chips, rows, width), pieces[0][2].dtype)
        for rel, lower, piece in pieces:
            used = min(piece.shape[0], rows - lower)
            if used > 0:
                whole = lax.dynamic_update_slice(
                    whole, piece[None, :used], (chip ^ rel, lower, 0)
                )
        return whole

    def total_of(terms):
        whole = terms[0].astype(f32)
        for term in terms[1:]:
            whole = whole + term.astype(f32)
        return whole

    def read(term, more=()):
        array, fixed = term
        fixed = {**fixed, **dict(more)}
        starts = [fixed.get(axis, 0) for axis in range(array.ndim)]
        sizes = [1 if axis in fixed else size for axis, size in enumerate(array.shape)]
        part = lax.dynamic_slice(array, starts, sizes)
        return part.reshape([size for axis, size in enumerate(array.shape) if axis not in fixed])

    def scatter_chips(sides, chip, holds=()):
        outs = []
        for block, order in zip(sides, (bits[::-1], bits)):
            left = bits[::-1]
            terms = [(block.reshape((2,) * len(bits) + block.shape[1:]), {}, left)]
            for turn, bit in enumerate(order):
                mine = (chip // bit) % 2
                sent = total_of(
                    [
                        read((array, fixed), {names.index(bit): 1 - mine})
                        for array, fixed, names in terms
                    ]
                ).astype(bf16)
                if turn < len(holds):
                    sent = after(sent, *holds[turn])
                terms = [
                    (array, {**fixed, names.index(bit): mine}, names)
                    for array, fixed, names in terms
                ]
                left = [other for other in left if other != bit]
                terms.append((swap(sent, 2 * bit), {}, left))
            outs.append([(array, fixed) for array, fixed, _ in terms])
        return outs

    def chooser(names, known=None, flipped=None):
        def choose(at):
            index = 0
            for bit in names:
                if known is not None and bit in known:
                    value = known[bit]
                else:
                    value = (at[1] // bit) % 2
                    value = 1 - value if bit == flipped else value
                index = index * 2 + value
            return index

        return choose

    def scatter_blocks(term, place, holds=()):
        _, rows, width = term.shape
        half = width // 2
        names = bits[::-1]
        sides = [[(term, 0, names)], [(term, 1, names)]]
        lefts = [names, names]
        orders = (names, bits)
        for turn in range(len(bits)):
            outputs = []
            for side in (0, 1):
                bit = orders[side][turn]
                lefts[side] = [other for other in lefts[side] if other != bit]
                cells = []
                for number in range(1 << len(lefts[side])):
                    known = {
                        other: (number >> (len(lefts[side]) - 1 - at)) & 1
                        for at, other in enumerate(lefts[side])
                    }
                    terms = [
                        (array, column, chooser(own, known, bit))
                        for array, column, own in sides[side]
                    ]
                    cells.append((number * rows, 0, rows, half, terms))
                outputs.append(((rows << len(lefts[side]), half), cells))
            sent = block_sums(place, outputs)
            for side in (0, 1):
                value = after(sent[side], *holds[turn]) if turn < len(holds) else sent[side]
                value = swap(value, 2 * orders[side][turn])
                sides[side] = sides[side] + [(value.reshape(-1, rows, half), 0, lefts[side])]
        return sides

    def reduce_planes(sides, plane, hold=()):
        def quarter(index):
            return jnp.concatenate(
                [
                    total_of([read(term, {term[0].ndim - 3: index}) for term in terms])
                    for terms in sides
                ],
                axis=0,
            )

        arrived = []
        for step in range(1, planes):
            sent = quarter((plane + step) % planes).astype(bf16)
            arrived.append(along(after(sent, *hold), step))
        total = total_of([quarter(plane)] + arrived).astype(bf16)
        whole = jnp.zeros((planes,) + total.shape, bf16)
        whole = lax.dynamic_update_slice(whole, total[None], (plane, 0, 0))
        for step in range(1, planes):
            moved = along(total, step)
            whole = lax.dynamic_update_slice(whole, moved[None], ((plane - step) % planes, 0, 0))
        return whole

    def reduce_line(sides, plane, place, hold=()):
        rows, half = sides[0][-1][0].shape[1:]
        cells = [
            (0, side * half, rows, half, [(a, column, chooser(names)) for a, column, names in terms])
            for side, terms in enumerate(sides)
        ]
        own = block_sums(place, [((rows, 2 * half), cells)])[0]
        if planes != 4:
            blocks = own.reshape(planes, rows // planes, 2 * half)
            return reduce_planes([[(blocks, {})]], plane, hold).reshape(rows, -1)

        def line(value, pairs):
            return lax.ppermute(value, "seq", pairs)

        own = after(own, *hold)
        own = total_of([own, line(own, [(0, 1), (3, 2)])]).astype(bf16)
        own = total_of([own, line(own, [(1, 2), (2, 1)])]).astype(bf16)
        other = line(own, [(1, 0), (2, 3)])
        return jnp.where((plane == 1) | (plane == 2), own, other)

    def shards(
        layer_input,
        cotangent,
        lengths,
        project_weight,
        output_weight,
        up_weight,
        down_weight,
        norm_gains,
        biases,
        hidden_bias,
        *moments,
    ):
        masters = (
            project_weight,
            output_weight,
            up_weight,
            down_weight,
            norm_gains,
            biases,
            hidden_bias,
        )
        firsts, seconds = moments[:7], moments[7:]
        seqs_here, slice_len, width = layer_input.shape
        own_rows = project_weight.shape[0]
        hidden_width = up_weight.shape[1]
        hidden_half = hidden_width // 2
        hidden_block = hidden_width // members
        half_width = width // 2
        group = 2 * seqs_here // planes
        turns = seqs_here // group
        plane = lax.axis_index("seq")
        member = lax.axis_index("fsdp")
        chip, core = member // 2, member % 2
        home = plane * group // seqs_here

        def home_of(plane_at):
            return plane_at * group // seqs_here

        def to_sequences(array, first=(), later=()):
            array = after(array, *first)
            blocks = []
            for step in range(planes):
                target = (plane + step) % planes
                block = lax.dynamic_slice_in_dim(array, (target * group) % seqs_here, group, 0)
                if step:
                    pairs = []
                    for source in range(planes):
                        there = (source + step) % planes
                        for one in range(chips):
                            at = 2 * one + home_of(there)
                            pairs.append((source * members + at, there * members + at))
                    block = lax.ppermute(block, axes, pairs)
                blocks.append(block)
            mine = jnp.stack(blocks, axis=1).reshape(group * planes * slice_len, width)
            return jnp.where(core == home, mine, partner(after(mine, *later)))

        def from_sequences(array, hold=()):
            blocks = after(array, *hold).reshape(group, planes, slice_len, width)
            arrived = [blocks[:, 0]]
            for step in range(1, planes):
                pairs = []
                for source in range(planes):
                    there = (source - step) % planes
                    for one in range(chips):
                        at = 2 * one + home_of(source)
                        pairs.append((source * members + at, there * members + at))
                arrived.append(lax.ppermute(blocks[:, step], axes, pairs))
            slots = []
            for turn in range(turns):
                step_at = (core * turns + turn - plane) % planes
                value = arrived[0]
                for step in range(1, planes):
                    value = jnp.where(step_at == step, arrived[step], value)
                slots.append(value)
            return jnp.concatenate(slots, axis=0)

        def by_core(low, high):
            return jnp.where(core == 0, low, high)

        def split_columns(array, block):
            pieces = [
                array[:, start : start + block] for start in range(0, array.shape[1], block)
            ]
            return jnp.concatenate(pieces[::2], axis=1), jnp.concatenate(pieces[1::2], axis=1)

        def join_columns(low, high, block):
            pieces = []
            for start in range(0, low.shape[1], block):
                pieces += [low[:, start : start + block], high[:, start : start + block]]
            return jnp.concatenate(pieces, axis=1)

        tokens16 = to_sequences(layer_input)
        project_low, project_high = split_columns(project_weight, half_width)
        up_low, up_high = split_columns(up_weight, hidden_block)
        output_low, output_high = split_columns(output_weight, half_width)
        low_cols = jnp.concatenate([project_low, output_low, up_low], axis=1).astype(bf16)
        high_cols = jnp.concatenate([project_high, output_high, up_high], axis=1).astype(bf16)
        table = jnp.concatenate([norm_gains, biases], axis=0).astype(bf16)
        tables = table.shape[0]
        table = lax.dynamic_update_slice(
            jnp.zeros((tables, width), bf16), table, (0, member * own_rows)
        )
        kept_cols = by_core(low_cols, high_cols)
        cut = 4 * half_width
        spare = jnp.pad(table, ((0, 16 - tables), (0, low_cols.shape[1] - width)))
        swapped = partner(jnp.concatenate([by_core(high_cols, low_cols), spare], axis=0))
        other_table = swapped[own_rows : own_rows + tables, :width]
        swapped = swapped[:own_rows]
        both = jnp.concatenate([by_core(kept_cols, swapped), by_core(swapped, kept_cols)], axis=0)
        hidden_small = lax.dynamic_update_slice(
            jnp.zeros((hidden_half,), bf16), hidden_bias.astype(bf16), (chip * hidden_block,)
        ).reshape(-1, width)
        small = jnp.concatenate([table + other_table, hidden_small], axis=0)
        chip_rows = 2 * own_rows
        fill = round_up(chip_rows + small.shape[0], 16) - chip_rows - small.shape[0]
        small = jnp.pad(small, ((0, fill), (0, cut - width)))
        pieces, _, project_last = gather_chips(jnp.concatenate([both[:, :cut], small], axis=0))
        attend16 = assemble(pieces, chip, chip_rows).reshape(width, cut)
        project16 = attend16[:, : 3 * half_width]
        output_own = attend16[:, 3 * half_width :]
        output_other = partner(output_own)
        output16 = jnp.concatenate(
            [by_core(output_own, output_other), by_core(output_other, output_own)], axis=1
        )
        output16 = lax.dynamic_slice_in_dim(output16, core * half_width, half_width, 0)
        smalls = 0.0
        for _, lower, piece in pieces:
            if lower + piece.shape[0] > chip_rows:
                smalls = smalls + piece[max(chip_rows - lower, 0) :, :width].astype(f32)
        gain_rows, bias_rows = smalls[:2], smalls[2:tables]
        hidden_row = smalls[tables : tables + hidden_half // width].reshape(-1)

        home_lengths = jnp.where(core == home, lengths, partner(lengths))
        length = lax.dynamic_slice_in_dim(home_lengths, (plane * group) % seqs_here, group, 0)
        starts = (plane - jnp.arange(planes)) % planes * slice_len
        limits = length[:, None] - starts[None, :]

        own_bias = by_core(bias_rows[:2, :half_width], bias_rows[:2, half_width:])
        shift = jnp.concatenate([own_bias[0], jnp.zeros_like(own_bias[0]), own_bias[1]])
        packed = (dot(tokens16, project16) + shift).astype(bf16)
        context16, log_total = attend_forward(packed, limits, half_width)

        pieces, _, _ = gather_chips(both[:, cut:], project_last, (context16,))
        up16 = assemble(pieces, chip, chip_rows).reshape(width, hidden_half)
        inner_part = dot(context16, output16)
        other_context16 = partner(context16)
        inner_sum = tokens16.astype(f32) + (inner_part + partner(inner_part)) + bias_rows[2]
        after_attend, norm_one, recip_one = layer_norm(inner_sum, gain_rows[0], bias_rows[3])
        after_attend16 = after_attend.astype(bf16)
        upstream16 = to_sequences(cotangent, (), (inner_part,))
        pre_act = dot(after_attend16, up16) + hidden_row
        activated16 = gelu_exact(pre_act).astype(bf16)
        pieces, _, _ = gather_chips(down_weight.astype(bf16), (packed,), (context16,))
        down16 = assemble(pieces, chip, down_weight.shape[0]).reshape(hidden_half, width)
        outer_part = dot(activated16, down16)
        outer_sum = after_attend + (outer_part + partner(outer_part)) + bias_rows[4]
        final, norm_two, recip_two = layer_norm(outer_sum, gain_rows[1], bias_rows[5])

        upstream = upstream16.astype(f32)
        grad_outer = norm_back(upstream, norm_two, recip_two, gain_rows[1])
        grad_outer16 = grad_outer.astype(bf16)
        down_term = contract_first(activated16, grad_outer16).astype(bf16)
        grad_pre = contract_last(grad_outer16, down16) * gelu_slope(pre_act)
        grad_pre16 = grad_pre.astype(bf16)
        middle_part = contract_last(grad_pre16, up16)
        grad_middle = grad_outer + (middle_part + partner(middle_part))
        up_term = contract_first(after_attend16, grad_pre16).astype(bf16)
        grad_inner = norm_back(grad_middle, norm_one, recip_one, gain_rows[0])
        grad_inner16 = grad_inner.astype(bf16)
        grad_context16 = contract_last(grad_inner16, output16).astype(bf16)
        block_output = from_sequences(final.astype(bf16), (grad_context16,))
        place = jnp.stack([plane, chip]).astype(jnp.int32)
        down_sides = scatter_blocks(down_term.reshape(chips, -1, width), place, ((), (up_term,)))
        down_total = reduce_line(down_sides, plane, place, (grad_context16,))
        context_full = jnp.concatenate(
            [by_core(context16, other_context16), by_core(other_context16, context16)], axis=1
        )
        grad_half = by_core(grad_inner16[:, :half_width], grad_inner16[:, half_width:])
        output_term = contract_first(context_full, grad_half).astype(bf16)
        packed_grad = attend_backward(
            packed, context16, log_total, grad_context16, limits, half_width
        )
        up_sides = scatter_blocks(
            up_term.reshape(chips, -1, hidden_half), place, ((), (packed_grad,))
        )
        up_total = reduce_line(up_sides, plane, place)
        project_term = contract_first(tokens16, packed_grad).astype(bf16)
        input_part = contract_last(packed_grad, project16)
        other_part = partner(input_part)
        input_sum = (grad_inner + (input_part + other_part)).astype(bf16)
        input_gradient = from_sequences(input_sum)

        packed_sum = jnp.sum(packed_grad.astype(f32), axis=0)
        edge = jnp.stack([packed_sum[:half_width], packed_sum[2 * half_width :]])
        blank = jnp.zeros_like(edge)
        edge = by_core(
            jnp.concatenate([edge, blank], axis=1), jnp.concatenate([blank, edge], axis=1)
        )
        wide_terms = jnp.stack(
            [
                jnp.sum(grad_middle * norm_one, axis=0),
                jnp.sum(upstream * norm_two, axis=0),
                jnp.sum(grad_inner, axis=0),
                jnp.sum(grad_middle, axis=0),
                jnp.sum(grad_outer, axis=0),
                jnp.sum(upstream, axis=0),
            ]
        )
        hidden_term = jnp.sum(grad_pre, axis=0).reshape(-1, width)
        small_terms = jnp.concatenate([edge, wide_terms, hidden_term], axis=0).astype(bf16)
        small_rows = round_up(small_terms.shape[0], 16)
        small_terms = jnp.pad(small_terms, ((0, small_rows - small_terms.shape[0]), (0, 0)))
        small_terms = jnp.concatenate(
            [small_terms[None], jnp.zeros((planes - 1, small_rows, width), bf16)], axis=0
        )
        small_terms = jnp.broadcast_to(small_terms[None], (chips,) + small_terms.shape)
        project_blocks = project_term.reshape(chips, planes, -1, 3 * half_width)
        output_blocks = output_term.reshape(chips, planes, -1, half_width)
        attend_sides = scatter_chips(
            (
                jnp.concatenate([project_blocks[..., :width], small_terms], axis=2),
                jnp.concatenate([project_blocks[..., width:], output_blocks], axis=3),
            ),
            chip,
        )
        attend_whole = reduce_planes(attend_sides, plane)

        def rows_of(whole, start, count):
            return whole[:, start : start + count].reshape(planes * count, -1)

        def swap_halves(term, extra):
            parts = term.reshape(2, own_rows, -1)
            sent = pick(parts, 1 - core)
            if extra is not None:
                sent = jnp.concatenate([sent, extra], axis=0)
            other = partner(sent)
            kept = pick(parts, core)
            rest = other[own_rows:]
            other = other[:own_rows]
            return by_core(kept, other), by_core(other, kept), rest

        down_total = down_total.astype(f32)
        low, high, _ = swap_halves(up_total, None)
        up_total = join_columns(low, high, hidden_block).astype(f32)
        quarter = (attend_whole.shape[1] - small_rows) // 2
        attend_term = jnp.concatenate(
            [
                rows_of(attend_whole, 0, quarter),
                rows_of(attend_whole, quarter + small_rows, quarter),
            ],
            axis=1,
        )
        own_small = attend_whole[0, quarter : quarter + small_rows]
        low, high, other_small = swap_halves(
            attend_term, jnp.pad(own_small, ((0, 0), (0, cut - width)))
        )
        project_total = join_columns(
            low[:, : 3 * half_width], high[:, : 3 * half_width], half_width
        ).astype(f32)
        output_total = jnp.concatenate(
            [low[:, 3 * half_width :], high[:, 3 * half_width :]], axis=1
        ).astype(f32)
        own_small = own_small.astype(f32)
        table_total = jnp.concatenate(
            [own_small[:2] + other_small[:2, :width].astype(f32), own_small[2:8]], axis=0
        )
        own_table = lax.dynamic_slice(table_total, (0, member * own_rows), (8, own_rows))
        hidden_total = lax.dynamic_slice(
            own_small[8 : 8 + hidden_half // width].reshape(-1),
            (chip * hidden_block,),
            (hidden_block,),
        )
        gains_total = own_table[2:4]
        biases_total = jnp.concatenate([own_table[:2], own_table[4:]], axis=0)
        totals = (
            project_total,
            output_total,
            up_total,
            down_total,
            gains_total,
            biases_total,
            hidden_total,
        )
        decay_flags = (True, True, True, True, False, False, False)
        results = []
        for n in range(7):
            results.append(adam_step(masters[n], firsts[n], seconds[n], totals[n], decay_flags[n]))
        return (
            (block_output, input_gradient)
            + totals
            + tuple(outcome[0] for outcome in results)
            + tuple(outcome[1] for outcome in results)
            + tuple(outcome[2] for outcome in results)
        )

    return shards


def solution(mesh):
    tokens = P("fsdp", "seq", None)
    rows = P("fsdp", None)
    columns = P(None, "fsdp")
    flat = P("fsdp")
    params = (rows, rows, rows, rows, columns, columns, flat)
    shards = make_shards(mesh.shape["seq"], mesh.shape["fsdp"])

    return jax.shard_map(
        shards,
        mesh=mesh,
        in_specs=(tokens, tokens, flat) + params * 3,
        out_specs=(tokens, tokens) + params * 4,
        check_vma=False,
    )
```

```python
import jax
import jax.numpy as jnp
from jax import lax
from jax.experimental import pallas as pl
from jax.experimental.pallas import tpu as pltpu
from jax.sharding import PartitionSpec as P


HD = 64
ADAM_STEP = 3


beta_one = 0.9
beta_two = 0.999
learn_rate = 0.01
decay_rate = 0.01
adam_eps = 1e-08
norm_eps = 1e-05
half_root = 0.7071067811865476
gauss_peak = 0.3989422804014327

bf16 = jnp.bfloat16
f32 = jnp.float32


def layer_norm(summed, gain, shift):
    centred = summed - jnp.mean(summed, axis=-1, keepdims=True)
    spread = jnp.mean(centred * centred, axis=-1, keepdims=True)
    recip = lax.rsqrt(spread + norm_eps)
    normed = centred * recip
    return (normed * gain + shift, normed, recip)


def norm_back(upstream, normed, recip, gain):
    scaled = upstream * gain
    return recip * (
        scaled
        - jnp.mean(scaled, axis=-1, keepdims=True)
        - normed * jnp.mean(scaled * normed, axis=-1, keepdims=True)
    )


def gelu_exact(pre_act):
    return 0.5 * pre_act * (1.0 + lax.erf(pre_act * half_root))


def gelu_slope(pre_act):
    return (
        0.5 * (1.0 + lax.erf(pre_act * half_root))
        + pre_act * jnp.exp(-0.5 * pre_act * pre_act) * gauss_peak
    )


def dot(left, right):
    return jnp.dot(left, right, preferred_element_type=f32)


def contract_last(left, right):
    return lax.dot_general(left, right, (((1,), (1,)), ((), ())), preferred_element_type=f32)


def contract_first(left, right):
    return lax.dot_general(left, right, (((0,), (0,)), ((), ())), preferred_element_type=f32)


def pick(array, index, axis=0):
    return lax.dynamic_index_in_dim(array, index, axis, keepdims=False)


def after(value, *others):
    return lax.optimization_barrier((value,) + others)[0] if others else value


def round_up(value, unit):
    return -(-value // unit) * unit


def adam_step(master, first, second, gradient, with_decay):
    first_new = beta_one * first + (1.0 - beta_one) * gradient
    second_new = beta_two * second + (1.0 - beta_two) * gradient * gradient
    first_hat = first_new / (1.0 - beta_one**ADAM_STEP)
    second_hat = second_new / (1.0 - beta_two**ADAM_STEP)
    change = first_hat / (jnp.sqrt(second_hat) + adam_eps)
    if with_decay:
        change = change + decay_rate * master
    return (master - learn_rate * change, first_new, second_new)


LANES = 128


def keep_rows(limits_ref, group_at, planes, slice_len):
    rows = lax.broadcasted_iota(jnp.int32, (slice_len, 1), 0)
    return jnp.concatenate(
        [rows < limits_ref[group_at, step] for step in range(planes)], axis=0
    )


def head_mask(shape, place):
    lane = lax.broadcasted_iota(jnp.int32, shape, 1)
    return (lane >= place * HD) & (lane < (place + 1) * HD)


def forward_kernel(limits_ref, query_ref, key_ref, value_ref, context_ref, log_ref):
    planes = limits_ref.shape[1]
    length = query_ref.shape[0]
    keep = keep_rows(limits_ref, pl.program_id(0), planes, length // planes)
    query = query_ref[...] * jnp.asarray(HD**-0.5, bf16)
    key = key_ref[...]
    value = value_ref[...]
    total = None
    for place in range(LANES // HD):
        own = head_mask(query.shape, place)
        zero = jnp.zeros_like(query)
        scores = contract_last(key, jnp.where(own, query, zero))
        scores = jnp.where(keep, scores, -jnp.inf)
        row_max = jnp.max(scores, axis=0, keepdims=True)
        lifted = jnp.exp(scores - row_max)
        row_total = jnp.sum(lifted, axis=0, keepdims=True)
        weights16 = (lifted * (1.0 / row_total)).astype(bf16)
        part = contract_first(jnp.where(own, value, zero), weights16)
        total = part if total is None else total + part
        log_ref[0, place : place + 1, :] = row_max + jnp.log(row_total)
    context_ref[...] = jnp.transpose(total).astype(bf16)


def backward_kernel(
    limits_ref,
    query_ref,
    key_ref,
    value_ref,
    context_ref,
    log_ref,
    upstream_ref,
    grads_ref,
):
    planes = limits_ref.shape[1]
    length = query_ref.shape[0]
    keep = keep_rows(limits_ref, pl.program_id(0), planes, length // planes)
    scale = HD**-0.5
    query = query_ref[...] * jnp.asarray(scale, bf16)
    key = key_ref[...]
    value = value_ref[...]
    upstream = upstream_ref[...]
    offsets = jnp.transpose(upstream.astype(f32) * context_ref[...].astype(f32))
    zero = jnp.zeros_like(query)
    query_grad, key_grad, value_grad = None, None, None
    for place in range(LANES // HD):
        own = head_mask(query.shape, place)
        own_query = jnp.where(own, query, zero)
        own_upstream = jnp.where(own, upstream, zero)
        scores = contract_last(key, own_query)
        attention = jnp.exp(scores - log_ref[0, place : place + 1, :])
        attention = jnp.where(keep, attention, 0.0)
        part = dot(attention.astype(bf16), own_upstream)
        value_grad = part if value_grad is None else value_grad + part
        prob_grad = contract_last(value, own_upstream)
        offset = jnp.sum(offsets[place * HD : (place + 1) * HD], axis=0, keepdims=True)
        score16 = (attention * (prob_grad - offset) * scale).astype(bf16)
        part = dot(score16, own_query)
        key_grad = part if key_grad is None else key_grad + part
        part = contract_first(jnp.where(own, key, zero), score16)
        query_grad = part if query_grad is None else query_grad + part
    width = grads_ref.shape[1] // 3
    start = pl.multiple_of(pl.program_id(1) * LANES, LANES)
    grads_ref[:, pl.ds(start, LANES)] = jnp.transpose(query_grad).astype(bf16)
    grads_ref[:, pl.ds(width + start, LANES)] = (key_grad * (1.0 / scale)).astype(bf16)
    grads_ref[:, pl.ds(2 * width + start, LANES)] = value_grad.astype(bf16)


def attend_forward(packed, limits, width):
    group, _ = limits.shape
    length = packed.shape[0] // group
    pairs = width // LANES
    places = LANES // HD

    def block(offset):
        return pl.BlockSpec((length, LANES), lambda g, j, limits: (g, offset + j))

    return pl.pallas_call(
        forward_kernel,
        out_shape=(
            jax.ShapeDtypeStruct((packed.shape[0], width), bf16),
            jax.ShapeDtypeStruct((group * pairs, places, length), f32),
        ),
        grid_spec=pltpu.PrefetchScalarGridSpec(
            num_scalar_prefetch=1,
            grid=(group, pairs),
            in_specs=[block(0), block(pairs), block(2 * pairs)],
            out_specs=[
                block(0),
                pl.BlockSpec((1, places, length), lambda g, j, limits: (g * pairs + j, 0, 0)),
            ],
        ),
        cost_estimate=pl.CostEstimate(
            flops=4 * packed.shape[0] * length * width,
            bytes_accessed=packed.size * 3,
            transcendentals=packed.shape[0] * length * width // HD,
        ),
        name="attend_forward",
    )(limits, packed, packed, packed)


def attend_backward(packed, context16, log_total, upstream16, limits, width):
    group, _ = limits.shape
    length = packed.shape[0] // group
    pairs = width // LANES
    places = LANES // HD

    def block(offset):
        return pl.BlockSpec((length, LANES), lambda g, j, limits: (g, offset + j))

    return pl.pallas_call(
        backward_kernel,
        out_shape=jax.ShapeDtypeStruct(packed.shape, bf16),
        grid_spec=pltpu.PrefetchScalarGridSpec(
            num_scalar_prefetch=1,
            grid=(group, pairs),
            in_specs=[
                block(0),
                block(pairs),
                block(2 * pairs),
                block(0),
                pl.BlockSpec((1, places, length), lambda g, j, limits: (g * pairs + j, 0, 0)),
                block(0),
            ],
            out_specs=pl.BlockSpec((length, packed.shape[1]), lambda g, j, limits: (g, 0)),
        ),
        cost_estimate=pl.CostEstimate(
            flops=10 * packed.shape[0] * length * width,
            bytes_accessed=packed.size * 6,
            transcendentals=packed.shape[0] * length * width // HD,
        ),
        name="attend_backward",
    )(limits, packed, packed, packed, context16, log_total, upstream16)


def make_shards(planes, members):
    chips = members // 2
    bits = [1 << bit for bit in range(chips.bit_length() - 1)]
    axes = ("seq", "fsdp")

    def swap(value, mask):
        return lax.ppermute(value, "fsdp", [(i, i ^ mask) for i in range(members)])

    def partner(value):
        return swap(value, 1)

    def along(value, step):
        return lax.ppermute(value, "seq", [(i, (i + step) % planes) for i in range(planes)])

    def gather_chips(own, first=(), later=()):
        rows = own.shape[0]
        half = max(rows // 32 * 16, 1)
        direct = {}
        sent = after(own, *first)
        for bit in bits:
            direct[bit] = swap(sent, 2 * bit)
        pieces = [(0, 0, own)] + [(bit, 0, direct[bit]) for bit in bits]
        last = ()
        for lower, upper, order in ((0, half, bits), (half, rows, bits[::-1])):
            held = {0: own[lower:upper]}
            for bit in order:
                far = [rel for rel in held if rel]
                fresh = {bit: direct[bit][lower:upper]}
                if far:
                    batch = held[far[0]] if len(far) == 1 else jnp.concatenate([held[r] for r in far])
                    moved = swap(after(batch, *later), 2 * bit)
                    size = upper - lower
                    for place, rel in enumerate(far):
                        fresh[rel | bit] = moved[place * size : (place + 1) * size]
                        pieces.append((rel | bit, lower, fresh[rel | bit]))
                        last += (fresh[rel | bit],)
                held.update(fresh)
        return pieces, tuple(direct.values()), last

    def assemble(pieces, chip, rows):
        width = pieces[0][2].shape[1]
        whole = jnp.zeros((chips, rows, width), pieces[0][2].dtype)
        for rel, lower, piece in pieces:
            used = min(piece.shape[0], rows - lower)
            if used <= 0:
                continue
            whole = lax.dynamic_update_slice(
                whole, piece[None, :used], (chip ^ rel, lower, 0)
            )
        return whole

    def total_of(terms):
        whole = terms[0].astype(f32)
        for term in terms[1:]:
            whole = whole + term.astype(f32)
        return whole

    def read(term, more=()):
        array, fixed = term
        fixed = {**fixed, **dict(more)}
        starts = [fixed.get(axis, 0) for axis in range(array.ndim)]
        sizes = [1 if axis in fixed else size for axis, size in enumerate(array.shape)]
        part = lax.dynamic_slice(array, starts, sizes)
        return part.reshape([size for axis, size in enumerate(array.shape) if axis not in fixed])

    def scatter_chips(sides, chip, holds=()):
        outs = []
        for block, order in zip(sides, (bits[::-1], bits)):
            left = bits[::-1]
            terms = [(block.reshape((2,) * len(bits) + block.shape[1:]), {}, left)]
            for turn, bit in enumerate(order):
                mine = (chip // bit) % 2
                sent = total_of(
                    [
                        read((array, fixed), {names.index(bit): 1 - mine})
                        for array, fixed, names in terms
                    ]
                ).astype(bf16)
                if turn < len(holds):
                    sent = after(sent, *holds[turn])
                terms = [
                    (array, {**fixed, names.index(bit): mine}, names)
                    for array, fixed, names in terms
                ]
                left = [other for other in left if other != bit]
                terms.append((swap(sent, 2 * bit), {}, left))
            outs.append([(array, fixed) for array, fixed, _ in terms])
        return outs

    def reduce_planes(sides, plane, hold=()):
        def quarter(index):
            return jnp.concatenate(
                [
                    total_of([read(term, {term[0].ndim - 3: index}) for term in terms])
                    for terms in sides
                ],
                axis=0,
            )

        arrived = []
        for step in range(1, planes):
            sent = quarter((plane + step) % planes).astype(bf16)
            arrived.append(along(after(sent, *hold), step))
        total = total_of([quarter(plane)] + arrived).astype(bf16)
        whole = jnp.zeros((planes,) + total.shape, bf16)
        whole = lax.dynamic_update_slice(whole, total[None], (plane, 0, 0))
        for step in range(1, planes):
            moved = along(total, step)
            whole = lax.dynamic_update_slice(whole, moved[None], ((plane - step) % planes, 0, 0))
        return whole

    def reduce_line(sides, plane, hold=()):
        if planes != 4:
            whole = reduce_planes(sides, plane, hold)
            count = whole.shape[1] // len(sides)
            return jnp.concatenate(
                [
                    whole[:, start : start + count].reshape(planes * count, -1)
                    for start in range(0, whole.shape[1], count)
                ],
                axis=1,
            )

        def line(value, pairs):
            return lax.ppermute(value, "seq", pairs)

        def flat(terms):
            return total_of([read(term).reshape(-1, term[0].shape[-1]) for term in terms])

        own = jnp.concatenate([flat(terms) for terms in sides], axis=1).astype(bf16)
        own = after(own, *hold)
        own = total_of([own, line(own, [(0, 1), (3, 2)])]).astype(bf16)
        own = total_of([own, line(own, [(1, 2), (2, 1)])]).astype(bf16)
        other = line(own, [(1, 0), (2, 3)])
        return jnp.where((plane == 1) | (plane == 2), own, other)

    def shards(
        layer_input,
        cotangent,
        lengths,
        project_weight,
        output_weight,
        up_weight,
        down_weight,
        norm_gains,
        biases,
        hidden_bias,
        *moments,
    ):
        masters = (
            project_weight,
            output_weight,
            up_weight,
            down_weight,
            norm_gains,
            biases,
            hidden_bias,
        )
        firsts, seconds = moments[:7], moments[7:]
        seqs_here, slice_len, width = layer_input.shape
        own_rows = project_weight.shape[0]
        hidden_width = up_weight.shape[1]
        hidden_half = hidden_width // 2
        hidden_block = hidden_width // members
        half_width = width // 2
        group = 2 * seqs_here // planes
        turns = seqs_here // group
        plane = lax.axis_index("seq")
        member = lax.axis_index("fsdp")
        chip, core = member // 2, member % 2
        home = plane * group // seqs_here

        def home_of(plane_at):
            return plane_at * group // seqs_here

        def to_sequences(array, first=(), later=()):
            array = after(array, *first)
            blocks = []
            for step in range(planes):
                target = (plane + step) % planes
                block = lax.dynamic_slice_in_dim(array, (target * group) % seqs_here, group, 0)
                if step:
                    pairs = []
                    for source in range(planes):
                        there = (source + step) % planes
                        for one in range(chips):
                            at = 2 * one + home_of(there)
                            pairs.append((source * members + at, there * members + at))
                    block = lax.ppermute(block, axes, pairs)
                blocks.append(block)
            mine = jnp.stack(blocks, axis=1).reshape(group * planes * slice_len, width)
            return jnp.where(core == home, mine, partner(after(mine, *later)))

        def from_sequences(array, hold=()):
            blocks = after(array, *hold).reshape(group, planes, slice_len, width)
            arrived = [blocks[:, 0]]
            for step in range(1, planes):
                pairs = []
                for source in range(planes):
                    there = (source - step) % planes
                    for one in range(chips):
                        at = 2 * one + home_of(source)
                        pairs.append((source * members + at, there * members + at))
                arrived.append(lax.ppermute(blocks[:, step], axes, pairs))
            slots = []
            for turn in range(turns):
                step_at = (core * turns + turn - plane) % planes
                value = arrived[0]
                for step in range(1, planes):
                    value = jnp.where(step_at == step, arrived[step], value)
                slots.append(value)
            return jnp.concatenate(slots, axis=0)

        def by_core(low, high):
            return jnp.where(core == 0, low, high)

        def split_columns(array, block):
            pieces = [
                array[:, start : start + block] for start in range(0, array.shape[1], block)
            ]
            return jnp.concatenate(pieces[::2], axis=1), jnp.concatenate(pieces[1::2], axis=1)

        def join_columns(low, high, block):
            pieces = []
            for start in range(0, low.shape[1], block):
                pieces += [low[:, start : start + block], high[:, start : start + block]]
            return jnp.concatenate(pieces, axis=1)

        tokens16 = to_sequences(layer_input)
        project_low, project_high = split_columns(project_weight, half_width)
        up_low, up_high = split_columns(up_weight, hidden_block)
        output_low, output_high = split_columns(output_weight, half_width)
        low_cols = jnp.concatenate([project_low, output_low, up_low], axis=1).astype(bf16)
        high_cols = jnp.concatenate([project_high, output_high, up_high], axis=1).astype(bf16)
        table = jnp.concatenate([norm_gains, biases], axis=0).astype(bf16)
        tables = table.shape[0]
        table = lax.dynamic_update_slice(
            jnp.zeros((tables, width), bf16), table, (0, member * own_rows)
        )
        kept_cols = by_core(low_cols, high_cols)
        cut = 4 * half_width
        spare = jnp.pad(table, ((0, 16 - tables), (0, low_cols.shape[1] - width)))
        swapped = partner(jnp.concatenate([by_core(high_cols, low_cols), spare], axis=0))
        other_table = swapped[own_rows : own_rows + tables, :width]
        swapped = swapped[:own_rows]
        both = jnp.concatenate([by_core(kept_cols, swapped), by_core(swapped, kept_cols)], axis=0)
        hidden_small = lax.dynamic_update_slice(
            jnp.zeros((hidden_half,), bf16), hidden_bias.astype(bf16), (chip * hidden_block,)
        ).reshape(-1, width)
        small = jnp.concatenate([table + other_table, hidden_small], axis=0)
        chip_rows = 2 * own_rows
        fill = round_up(chip_rows + small.shape[0], 16) - chip_rows - small.shape[0]
        small = jnp.pad(small, ((0, fill), (0, cut - width)))
        pieces, _, project_last = gather_chips(jnp.concatenate([both[:, :cut], small], axis=0))
        attend16 = assemble(pieces, chip, chip_rows).reshape(width, cut)
        project16 = attend16[:, : 3 * half_width]
        output_own = attend16[:, 3 * half_width :]
        output_other = partner(output_own)
        output16 = jnp.concatenate(
            [by_core(output_own, output_other), by_core(output_other, output_own)], axis=1
        )
        output16 = lax.dynamic_slice_in_dim(output16, core * half_width, half_width, 0)
        smalls = 0.0
        for _, lower, piece in pieces:
            if lower + piece.shape[0] > chip_rows:
                smalls = smalls + piece[max(chip_rows - lower, 0) :, :width].astype(f32)
        gain_rows, bias_rows = smalls[:2], smalls[2:tables]
        hidden_row = smalls[tables : tables + hidden_half // width].reshape(-1)

        home_lengths = jnp.where(core == home, lengths, partner(lengths))
        length = lax.dynamic_slice_in_dim(home_lengths, (plane * group) % seqs_here, group, 0)
        starts = (plane - jnp.arange(planes)) % planes * slice_len
        limits = length[:, None] - starts[None, :]

        own_bias = by_core(bias_rows[:2, :half_width], bias_rows[:2, half_width:])
        shift = jnp.concatenate([own_bias[0], jnp.zeros_like(own_bias[0]), own_bias[1]])
        packed = (dot(tokens16, project16) + shift).astype(bf16)
        context16, log_total = attend_forward(packed, limits, half_width)

        pieces, _, _ = gather_chips(both[:, cut:], project_last, (context16,))
        up16 = assemble(pieces, chip, chip_rows).reshape(width, hidden_half)
        inner_part = dot(context16, output16)
        other_context16 = partner(context16)
        inner_sum = tokens16.astype(f32) + (inner_part + partner(inner_part)) + bias_rows[2]
        after_attend, norm_one, recip_one = layer_norm(inner_sum, gain_rows[0], bias_rows[3])
        after_attend16 = after_attend.astype(bf16)
        upstream16 = to_sequences(cotangent, (), (inner_part,))
        pre_act = dot(after_attend16, up16) + hidden_row
        activated16 = gelu_exact(pre_act).astype(bf16)
        pieces, _, _ = gather_chips(down_weight.astype(bf16), (packed,), (context16,))
        down16 = assemble(pieces, chip, down_weight.shape[0]).reshape(hidden_half, width)
        outer_part = dot(activated16, down16)
        outer_sum = after_attend + (outer_part + partner(outer_part)) + bias_rows[4]
        final, norm_two, recip_two = layer_norm(outer_sum, gain_rows[1], bias_rows[5])

        upstream = upstream16.astype(f32)
        grad_outer = norm_back(upstream, norm_two, recip_two, gain_rows[1])
        grad_outer16 = grad_outer.astype(bf16)
        down_term = contract_first(activated16, grad_outer16).astype(bf16)
        grad_pre = contract_last(grad_outer16, down16) * gelu_slope(pre_act)
        grad_pre16 = grad_pre.astype(bf16)
        middle_part = contract_last(grad_pre16, up16)
        grad_middle = grad_outer + (middle_part + partner(middle_part))
        up_term = contract_first(after_attend16, grad_pre16).astype(bf16)
        grad_inner = norm_back(grad_middle, norm_one, recip_one, gain_rows[0])
        grad_inner16 = grad_inner.astype(bf16)
        grad_context16 = contract_last(grad_inner16, output16).astype(bf16)
        block_output = from_sequences(final.astype(bf16), (grad_context16,))
        down_blocks = down_term.reshape(chips, planes, -1, width)
        down_sides = scatter_chips(
            (down_blocks[..., :half_width], down_blocks[..., half_width:]), chip, ((), (up_term,))
        )
        down_total = reduce_line(down_sides, plane, (grad_context16,))
        context_full = jnp.concatenate(
            [by_core(context16, other_context16), by_core(other_context16, context16)], axis=1
        )
        grad_half = by_core(grad_inner16[:, :half_width], grad_inner16[:, half_width:])
        output_term = contract_first(context_full, grad_half).astype(bf16)
        packed_grad = attend_backward(
            packed, context16, log_total, grad_context16, limits, half_width
        )
        up_blocks = up_term.reshape(chips, planes, -1, hidden_half)
        up_sides = scatter_chips(
            (up_blocks[..., : hidden_half // 2], up_blocks[..., hidden_half // 2 :]),
            chip,
            ((), (packed_grad,)),
        )
        up_total = reduce_line(up_sides, plane)
        project_term = contract_first(tokens16, packed_grad).astype(bf16)
        input_part = contract_last(packed_grad, project16)
        other_part = partner(input_part)
        input_sum = (grad_inner + (input_part + other_part)).astype(bf16)
        input_gradient = from_sequences(input_sum)

        packed_sum = jnp.sum(packed_grad.astype(f32), axis=0)
        edge = jnp.stack([packed_sum[:half_width], packed_sum[2 * half_width :]])
        blank = jnp.zeros_like(edge)
        edge = by_core(
            jnp.concatenate([edge, blank], axis=1), jnp.concatenate([blank, edge], axis=1)
        )
        wide_terms = jnp.stack(
            [
                jnp.sum(grad_middle * norm_one, axis=0),
                jnp.sum(upstream * norm_two, axis=0),
                jnp.sum(grad_inner, axis=0),
                jnp.sum(grad_middle, axis=0),
                jnp.sum(grad_outer, axis=0),
                jnp.sum(upstream, axis=0),
            ]
        )
        hidden_term = jnp.sum(grad_pre, axis=0).reshape(-1, width)
        small_terms = jnp.concatenate([edge, wide_terms, hidden_term], axis=0).astype(bf16)
        small_rows = round_up(small_terms.shape[0], 16)
        small_terms = jnp.pad(small_terms, ((0, small_rows - small_terms.shape[0]), (0, 0)))
        small_terms = jnp.concatenate(
            [small_terms[None], jnp.zeros((planes - 1, small_rows, width), bf16)], axis=0
        )
        small_terms = jnp.broadcast_to(small_terms[None], (chips,) + small_terms.shape)
        project_blocks = project_term.reshape(chips, planes, -1, 3 * half_width)
        output_blocks = output_term.reshape(chips, planes, -1, half_width)
        attend_sides = scatter_chips(
            (
                jnp.concatenate([project_blocks[..., :width], small_terms], axis=2),
                jnp.concatenate([project_blocks[..., width:], output_blocks], axis=3),
            ),
            chip,
        )
        attend_whole = reduce_planes(attend_sides, plane)

        def rows_of(whole, start, count):
            return whole[:, start : start + count].reshape(planes * count, -1)

        def swap_halves(term, extra):
            parts = term.reshape(2, own_rows, -1)
            sent = pick(parts, 1 - core)
            if extra is not None:
                sent = jnp.concatenate([sent, extra], axis=0)
            other = partner(sent)
            kept = pick(parts, core)
            rest = other[own_rows:]
            other = other[:own_rows]
            return by_core(kept, other), by_core(other, kept), rest

        down_total = down_total.astype(f32)
        low, high, _ = swap_halves(up_total, None)
        up_total = join_columns(low, high, hidden_block).astype(f32)
        quarter = (attend_whole.shape[1] - small_rows) // 2
        attend_term = jnp.concatenate(
            [
                rows_of(attend_whole, 0, quarter),
                rows_of(attend_whole, quarter + small_rows, quarter),
            ],
            axis=1,
        )
        own_small = attend_whole[0, quarter : quarter + small_rows]
        low, high, other_small = swap_halves(
            attend_term, jnp.pad(own_small, ((0, 0), (0, cut - width)))
        )
        project_total = join_columns(
            low[:, : 3 * half_width], high[:, : 3 * half_width], half_width
        ).astype(f32)
        output_total = jnp.concatenate(
            [low[:, 3 * half_width :], high[:, 3 * half_width :]], axis=1
        ).astype(f32)
        own_small = own_small.astype(f32)
        table_total = jnp.concatenate(
            [own_small[:2] + other_small[:2, :width].astype(f32), own_small[2:8]], axis=0
        )
        own_table = lax.dynamic_slice(table_total, (0, member * own_rows), (8, own_rows))
        hidden_total = lax.dynamic_slice(
            own_small[8 : 8 + hidden_half // width].reshape(-1),
            (chip * hidden_block,),
            (hidden_block,),
        )
        gains_total = own_table[2:4]
        biases_total = jnp.concatenate([own_table[:2], own_table[4:]], axis=0)
        totals = (
            project_total,
            output_total,
            up_total,
            down_total,
            gains_total,
            biases_total,
            hidden_total,
        )
        decay_flags = (True, True, True, True, False, False, False)
        results = []
        for n in range(7):
            results.append(adam_step(masters[n], firsts[n], seconds[n], totals[n], decay_flags[n]))
        return (
            (block_output, input_gradient)
            + totals
            + tuple(outcome[0] for outcome in results)
            + tuple(outcome[1] for outcome in results)
            + tuple(outcome[2] for outcome in results)
        )

    return shards


def solution(mesh):
    tokens = P("fsdp", "seq", None)
    rows = P("fsdp", None)
    columns = P(None, "fsdp")
    flat = P("fsdp")
    params = (rows, rows, rows, rows, columns, columns, flat)
    shards = make_shards(mesh.shape["seq"], mesh.shape["fsdp"])

    return jax.shard_map(
        shards,
        mesh=mesh,
        in_specs=(tokens, tokens, flat) + params * 3,
        out_specs=(tokens, tokens) + params * 4,
        check_vma=False,
    )
```

```python
import jax
import jax.numpy as jnp
from jax import lax
from jax.experimental import pallas as pl
from jax.experimental.pallas import tpu as pltpu
from jax.sharding import PartitionSpec as P


HD = 64
ADAM_STEP = 3


beta_one = 0.9
beta_two = 0.999
learn_rate = 0.01
decay_rate = 0.01
adam_eps = 1e-08
norm_eps = 1e-05
half_root = 0.7071067811865476
gauss_peak = 0.3989422804014327

bf16 = jnp.bfloat16
f32 = jnp.float32


def layer_norm(summed, gain, shift):
    centred = summed - jnp.mean(summed, axis=-1, keepdims=True)
    spread = jnp.mean(centred * centred, axis=-1, keepdims=True)
    recip = lax.rsqrt(spread + norm_eps)
    normed = centred * recip
    return (normed * gain + shift, normed, recip)


def norm_back(upstream, normed, recip, gain):
    scaled = upstream * gain
    return recip * (
        scaled
        - jnp.mean(scaled, axis=-1, keepdims=True)
        - normed * jnp.mean(scaled * normed, axis=-1, keepdims=True)
    )


def gelu_exact(pre_act):
    return 0.5 * pre_act * (1.0 + lax.erf(pre_act * half_root))


def gelu_slope(pre_act):
    return (
        0.5 * (1.0 + lax.erf(pre_act * half_root))
        + pre_act * jnp.exp(-0.5 * pre_act * pre_act) * gauss_peak
    )


def dot(left, right):
    return jnp.dot(left, right, preferred_element_type=f32)


def contract_last(left, right):
    return lax.dot_general(left, right, (((1,), (1,)), ((), ())), preferred_element_type=f32)


def contract_first(left, right):
    return lax.dot_general(left, right, (((0,), (0,)), ((), ())), preferred_element_type=f32)


def pick(array, index, axis=0):
    return lax.dynamic_index_in_dim(array, index, axis, keepdims=False)


def after(value, *others):
    return lax.optimization_barrier((value,) + others)[0] if others else value


def round_up(value, unit):
    return -(-value // unit) * unit


def adam_step(master, first, second, gradient, with_decay):
    first_new = beta_one * first + (1.0 - beta_one) * gradient
    second_new = beta_two * second + (1.0 - beta_two) * gradient * gradient
    first_hat = first_new / (1.0 - beta_one**ADAM_STEP)
    second_hat = second_new / (1.0 - beta_two**ADAM_STEP)
    change = first_hat / (jnp.sqrt(second_hat) + adam_eps)
    if with_decay:
        change = change + decay_rate * master
    return (master - learn_rate * change, first_new, second_new)


LANES = 128


def keep_rows(limits_ref, group_at, planes, slice_len):
    rows = lax.broadcasted_iota(jnp.int32, (slice_len, 1), 0)
    return jnp.concatenate(
        [rows < limits_ref[group_at, step] for step in range(planes)], axis=0
    )


def head_mask(shape, place):
    lane = lax.broadcasted_iota(jnp.int32, shape, 1)
    return (lane >= place * HD) & (lane < (place + 1) * HD)


def forward_kernel(limits_ref, query_ref, key_ref, value_ref, context_ref, log_ref):
    planes = limits_ref.shape[1]
    length = query_ref.shape[0]
    keep = keep_rows(limits_ref, pl.program_id(0), planes, length // planes)
    query = query_ref[...] * jnp.asarray(HD**-0.5, bf16)
    key = key_ref[...]
    value = value_ref[...]
    total = None
    for place in range(LANES // HD):
        own = head_mask(query.shape, place)
        zero = jnp.zeros_like(query)
        scores = contract_last(key, jnp.where(own, query, zero))
        scores = jnp.where(keep, scores, -jnp.inf)
        row_max = jnp.max(scores, axis=0, keepdims=True)
        lifted = jnp.exp(scores - row_max)
        row_total = jnp.sum(lifted, axis=0, keepdims=True)
        weights16 = (lifted * (1.0 / row_total)).astype(bf16)
        part = contract_first(jnp.where(own, value, zero), weights16)
        total = part if total is None else total + part
        log_ref[0, place : place + 1, :] = row_max + jnp.log(row_total)
    context_ref[...] = jnp.transpose(total).astype(bf16)


def backward_kernel(
    limits_ref,
    query_ref,
    key_ref,
    value_ref,
    context_ref,
    log_ref,
    upstream_ref,
    grads_ref,
):
    planes = limits_ref.shape[1]
    length = query_ref.shape[0]
    keep = keep_rows(limits_ref, pl.program_id(0), planes, length // planes)
    scale = HD**-0.5
    query = query_ref[...] * jnp.asarray(scale, bf16)
    key = key_ref[...]
    value = value_ref[...]
    upstream = upstream_ref[...]
    offsets = jnp.transpose(upstream.astype(f32) * context_ref[...].astype(f32))
    zero = jnp.zeros_like(query)
    query_grad, key_grad, value_grad = None, None, None
    for place in range(LANES // HD):
        own = head_mask(query.shape, place)
        own_query = jnp.where(own, query, zero)
        own_upstream = jnp.where(own, upstream, zero)
        scores = contract_last(key, own_query)
        attention = jnp.exp(scores - log_ref[0, place : place + 1, :])
        attention = jnp.where(keep, attention, 0.0)
        part = dot(attention.astype(bf16), own_upstream)
        value_grad = part if value_grad is None else value_grad + part
        prob_grad = contract_last(value, own_upstream)
        offset = jnp.sum(offsets[place * HD : (place + 1) * HD], axis=0, keepdims=True)
        score16 = (attention * (prob_grad - offset) * scale).astype(bf16)
        part = dot(score16, own_query)
        key_grad = part if key_grad is None else key_grad + part
        part = contract_first(jnp.where(own, key, zero), score16)
        query_grad = part if query_grad is None else query_grad + part
    width = grads_ref.shape[1] // 3
    start = pl.multiple_of(pl.program_id(1) * LANES, LANES)
    grads_ref[:, pl.ds(start, LANES)] = jnp.transpose(query_grad).astype(bf16)
    grads_ref[:, pl.ds(width + start, LANES)] = (key_grad * (1.0 / scale)).astype(bf16)
    grads_ref[:, pl.ds(2 * width + start, LANES)] = value_grad.astype(bf16)


def attend_forward(packed, limits, width):
    group, _ = limits.shape
    length = packed.shape[0] // group
    pairs = width // LANES
    places = LANES // HD

    def block(offset):
        return pl.BlockSpec((length, LANES), lambda g, j, limits: (g, offset + j))

    return pl.pallas_call(
        forward_kernel,
        out_shape=(
            jax.ShapeDtypeStruct((packed.shape[0], width), bf16),
            jax.ShapeDtypeStruct((group * pairs, places, length), f32),
        ),
        grid_spec=pltpu.PrefetchScalarGridSpec(
            num_scalar_prefetch=1,
            grid=(group, pairs),
            in_specs=[block(0), block(pairs), block(2 * pairs)],
            out_specs=[
                block(0),
                pl.BlockSpec((1, places, length), lambda g, j, limits: (g * pairs + j, 0, 0)),
            ],
        ),
        cost_estimate=pl.CostEstimate(
            flops=4 * packed.shape[0] * length * width,
            bytes_accessed=packed.size * 3,
            transcendentals=packed.shape[0] * length * width // HD,
        ),
        name="attend_forward",
    )(limits, packed, packed, packed)


def attend_backward(packed, context16, log_total, upstream16, limits, width):
    group, _ = limits.shape
    length = packed.shape[0] // group
    pairs = width // LANES
    places = LANES // HD

    def block(offset):
        return pl.BlockSpec((length, LANES), lambda g, j, limits: (g, offset + j))

    return pl.pallas_call(
        backward_kernel,
        out_shape=jax.ShapeDtypeStruct(packed.shape, bf16),
        grid_spec=pltpu.PrefetchScalarGridSpec(
            num_scalar_prefetch=1,
            grid=(group, pairs),
            in_specs=[
                block(0),
                block(pairs),
                block(2 * pairs),
                block(0),
                pl.BlockSpec((1, places, length), lambda g, j, limits: (g * pairs + j, 0, 0)),
                block(0),
            ],
            out_specs=pl.BlockSpec((length, packed.shape[1]), lambda g, j, limits: (g, 0)),
        ),
        cost_estimate=pl.CostEstimate(
            flops=10 * packed.shape[0] * length * width,
            bytes_accessed=packed.size * 6,
            transcendentals=packed.shape[0] * length * width // HD,
        ),
        name="attend_backward",
    )(limits, packed, packed, packed, context16, log_total, upstream16)


def make_shards(planes, members):
    chips = members // 2
    bits = [1 << bit for bit in range(chips.bit_length() - 1)]
    axes = ("seq", "fsdp")

    def swap(value, mask):
        return lax.ppermute(value, "fsdp", [(i, i ^ mask) for i in range(members)])

    def partner(value):
        return swap(value, 1)

    def along(value, step):
        return lax.ppermute(value, "seq", [(i, (i + step) % planes) for i in range(planes)])

    def gather_chips(own, first=(), later=()):
        rows = own.shape[0]
        half = max(rows // 32 * 16, 1)
        direct = {}
        sent = after(own, *first)
        for bit in bits:
            direct[bit] = swap(sent, 2 * bit)
        pieces = [(0, 0, own)] + [(bit, 0, direct[bit]) for bit in bits]
        last = ()
        for lower, upper, order in ((0, half, bits), (half, rows, bits[::-1])):
            held = {0: own[lower:upper]}
            for bit in order:
                far = [rel for rel in held if rel]
                fresh = {bit: direct[bit][lower:upper]}
                if far:
                    batch = held[far[0]] if len(far) == 1 else jnp.concatenate([held[r] for r in far])
                    moved = swap(after(batch, *later), 2 * bit)
                    size = upper - lower
                    for place, rel in enumerate(far):
                        fresh[rel | bit] = moved[place * size : (place + 1) * size]
                        pieces.append((rel | bit, lower, fresh[rel | bit]))
                        last += (fresh[rel | bit],)
                held.update(fresh)
        return pieces, tuple(direct.values()), last

    def assemble(pieces, chip, rows):
        width = pieces[0][2].shape[1]
        whole = jnp.zeros((chips, rows, width), pieces[0][2].dtype)
        for rel, lower, piece in pieces:
            used = min(piece.shape[0], rows - lower)
            if used <= 0:
                continue
            whole = lax.dynamic_update_slice(
                whole, piece[None, :used], (chip ^ rel, lower, 0)
            )
        return whole

    def total_of(terms):
        whole = terms[0].astype(f32)
        for term in terms[1:]:
            whole = whole + term.astype(f32)
        return whole

    def read(term, more=()):
        array, fixed = term
        fixed = {**fixed, **dict(more)}
        starts = [fixed.get(axis, 0) for axis in range(array.ndim)]
        sizes = [1 if axis in fixed else size for axis, size in enumerate(array.shape)]
        part = lax.dynamic_slice(array, starts, sizes)
        return part.reshape([size for axis, size in enumerate(array.shape) if axis not in fixed])

    def scatter_chips(sides, chip, holds=()):
        outs = []
        for block, order in zip(sides, (bits[::-1], bits)):
            left = bits[::-1]
            terms = [(block.reshape((2,) * len(bits) + block.shape[1:]), {}, left)]
            for turn, bit in enumerate(order):
                mine = (chip // bit) % 2
                sent = total_of(
                    [
                        read((array, fixed), {names.index(bit): 1 - mine})
                        for array, fixed, names in terms
                    ]
                ).astype(bf16)
                if turn < len(holds):
                    sent = after(sent, *holds[turn])
                terms = [
                    (array, {**fixed, names.index(bit): mine}, names)
                    for array, fixed, names in terms
                ]
                left = [other for other in left if other != bit]
                terms.append((swap(sent, 2 * bit), {}, left))
            outs.append([(array, fixed) for array, fixed, _ in terms])
        return outs

    def reduce_planes(sides, plane, hold=()):
        def quarter(index):
            return jnp.concatenate(
                [
                    total_of([read(term, {term[0].ndim - 3: index}) for term in terms])
                    for terms in sides
                ],
                axis=0,
            )

        arrived = []
        for step in range(1, planes):
            sent = quarter((plane + step) % planes).astype(bf16)
            arrived.append(along(after(sent, *hold), step))
        total = total_of([quarter(plane)] + arrived).astype(bf16)
        whole = jnp.zeros((planes,) + total.shape, bf16)
        whole = lax.dynamic_update_slice(whole, total[None], (plane, 0, 0))
        for step in range(1, planes):
            moved = along(total, step)
            whole = lax.dynamic_update_slice(whole, moved[None], ((plane - step) % planes, 0, 0))
        return whole

    def along_line(own, plane):
        if planes != 4:
            blocks = own.reshape(planes, own.shape[0] // planes, own.shape[1])
            return reduce_planes([[(blocks, {})]], plane).reshape(own.shape)

        def line(value, pairs):
            return lax.ppermute(value, "seq", pairs)

        own = total_of([own, line(own, [(0, 1), (3, 2)])]).astype(bf16)
        own = total_of([own, line(own, [(1, 2), (2, 1)])]).astype(bf16)
        other = line(own, [(1, 0), (2, 3)])
        return jnp.where((plane == 1) | (plane == 2), own, other)

    def flat(terms):
        return total_of([read(term).reshape(-1, term[0].shape[-1]) for term in terms])

    def reduce_line(sides, plane, hold=()):
        own = jnp.concatenate([flat(terms) for terms in sides], axis=1).astype(bf16)
        return along_line(after(own, *hold), plane)

    def shards(
        layer_input,
        cotangent,
        lengths,
        project_weight,
        output_weight,
        up_weight,
        down_weight,
        norm_gains,
        biases,
        hidden_bias,
        *moments,
    ):
        masters = (
            project_weight,
            output_weight,
            up_weight,
            down_weight,
            norm_gains,
            biases,
            hidden_bias,
        )
        firsts, seconds = moments[:7], moments[7:]
        seqs_here, slice_len, width = layer_input.shape
        own_rows = project_weight.shape[0]
        hidden_width = up_weight.shape[1]
        hidden_half = hidden_width // 2
        hidden_block = hidden_width // members
        half_width = width // 2
        group = 2 * seqs_here // planes
        turns = seqs_here // group
        plane = lax.axis_index("seq")
        member = lax.axis_index("fsdp")
        chip, core = member // 2, member % 2
        home = plane * group // seqs_here

        def home_of(plane_at):
            return plane_at * group // seqs_here

        def to_sequences(array, first=(), later=()):
            array = after(array, *first)
            blocks = []
            for step in range(planes):
                target = (plane + step) % planes
                block = lax.dynamic_slice_in_dim(array, (target * group) % seqs_here, group, 0)
                if step:
                    pairs = []
                    for source in range(planes):
                        there = (source + step) % planes
                        for one in range(chips):
                            at = 2 * one + home_of(there)
                            pairs.append((source * members + at, there * members + at))
                    block = lax.ppermute(block, axes, pairs)
                blocks.append(block)
            mine = jnp.stack(blocks, axis=1).reshape(group * planes * slice_len, width)
            return jnp.where(core == home, mine, partner(after(mine, *later)))

        def from_sequences(array, hold=()):
            blocks = after(array, *hold).reshape(group, planes, slice_len, width)
            arrived = [blocks[:, 0]]
            for step in range(1, planes):
                pairs = []
                for source in range(planes):
                    there = (source - step) % planes
                    for one in range(chips):
                        at = 2 * one + home_of(source)
                        pairs.append((source * members + at, there * members + at))
                arrived.append(lax.ppermute(blocks[:, step], axes, pairs))
            slots = []
            for turn in range(turns):
                step_at = (core * turns + turn - plane) % planes
                value = arrived[0]
                for step in range(1, planes):
                    value = jnp.where(step_at == step, arrived[step], value)
                slots.append(value)
            return jnp.concatenate(slots, axis=0)

        def by_core(low, high):
            return jnp.where(core == 0, low, high)

        def split_columns(array, block):
            pieces = [
                array[:, start : start + block] for start in range(0, array.shape[1], block)
            ]
            return jnp.concatenate(pieces[::2], axis=1), jnp.concatenate(pieces[1::2], axis=1)

        def join_columns(low, high, block):
            pieces = []
            for start in range(0, low.shape[1], block):
                pieces += [low[:, start : start + block], high[:, start : start + block]]
            return jnp.concatenate(pieces, axis=1)

        tokens16 = to_sequences(layer_input)
        project_low, project_high = split_columns(project_weight, half_width)
        up_low, up_high = split_columns(up_weight, hidden_block)
        output_low, output_high = split_columns(output_weight, half_width)
        low_cols = jnp.concatenate([project_low, output_low, up_low], axis=1).astype(bf16)
        high_cols = jnp.concatenate([project_high, output_high, up_high], axis=1).astype(bf16)
        table = jnp.concatenate([norm_gains, biases], axis=0).astype(bf16)
        tables = table.shape[0]
        table = lax.dynamic_update_slice(
            jnp.zeros((tables, width), bf16), table, (0, member * own_rows)
        )
        kept_cols = by_core(low_cols, high_cols)
        cut = 4 * half_width
        spare = jnp.pad(table, ((0, 16 - tables), (0, low_cols.shape[1] - width)))
        swapped = partner(jnp.concatenate([by_core(high_cols, low_cols), spare], axis=0))
        other_table = swapped[own_rows : own_rows + tables, :width]
        swapped = swapped[:own_rows]
        both = jnp.concatenate([by_core(kept_cols, swapped), by_core(swapped, kept_cols)], axis=0)
        hidden_small = lax.dynamic_update_slice(
            jnp.zeros((hidden_half,), bf16), hidden_bias.astype(bf16), (chip * hidden_block,)
        ).reshape(-1, width)
        small = jnp.concatenate([table + other_table, hidden_small], axis=0)
        chip_rows = 2 * own_rows
        fill = round_up(chip_rows + small.shape[0], 16) - chip_rows - small.shape[0]
        small = jnp.pad(small, ((0, fill), (0, cut - width)))
        pieces, _, project_last = gather_chips(jnp.concatenate([both[:, :cut], small], axis=0))
        attend16 = assemble(pieces, chip, chip_rows).reshape(width, cut)
        project16 = attend16[:, : 3 * half_width]
        output_own = attend16[:, 3 * half_width :]
        output_other = partner(output_own)
        output16 = jnp.concatenate(
            [by_core(output_own, output_other), by_core(output_other, output_own)], axis=1
        )
        output16 = lax.dynamic_slice_in_dim(output16, core * half_width, half_width, 0)
        smalls = 0.0
        for _, lower, piece in pieces:
            if lower + piece.shape[0] > chip_rows:
                smalls = smalls + piece[max(chip_rows - lower, 0) :, :width].astype(f32)
        gain_rows, bias_rows = smalls[:2], smalls[2:tables]
        hidden_row = smalls[tables : tables + hidden_half // width].reshape(-1)

        home_lengths = jnp.where(core == home, lengths, partner(lengths))
        length = lax.dynamic_slice_in_dim(home_lengths, (plane * group) % seqs_here, group, 0)
        starts = (plane - jnp.arange(planes)) % planes * slice_len
        limits = length[:, None] - starts[None, :]

        own_bias = by_core(bias_rows[:2, :half_width], bias_rows[:2, half_width:])
        shift = jnp.concatenate([own_bias[0], jnp.zeros_like(own_bias[0]), own_bias[1]])
        packed = (dot(tokens16, project16) + shift).astype(bf16)
        context16, log_total = attend_forward(packed, limits, half_width)

        pieces, _, _ = gather_chips(both[:, cut:], project_last, (context16,))
        up16 = assemble(pieces, chip, chip_rows).reshape(width, hidden_half)
        inner_part = dot(context16, output16)
        other_context16 = partner(context16)
        inner_sum = tokens16.astype(f32) + (inner_part + partner(inner_part)) + bias_rows[2]
        after_attend, norm_one, recip_one = layer_norm(inner_sum, gain_rows[0], bias_rows[3])
        after_attend16 = after_attend.astype(bf16)
        upstream16 = to_sequences(cotangent, (), (inner_part,))
        pre_act = dot(after_attend16, up16) + hidden_row
        activated16 = gelu_exact(pre_act).astype(bf16)
        pieces, _, _ = gather_chips(down_weight.astype(bf16), (packed,), (context16,))
        down16 = assemble(pieces, chip, down_weight.shape[0]).reshape(hidden_half, width)
        outer_part = dot(activated16, down16)
        outer_sum = after_attend + (outer_part + partner(outer_part)) + bias_rows[4]
        final, norm_two, recip_two = layer_norm(outer_sum, gain_rows[1], bias_rows[5])

        upstream = upstream16.astype(f32)
        grad_outer = norm_back(upstream, norm_two, recip_two, gain_rows[1])
        grad_outer16 = grad_outer.astype(bf16)
        down_term = contract_first(activated16, grad_outer16).astype(bf16)
        grad_pre = contract_last(grad_outer16, down16) * gelu_slope(pre_act)
        grad_pre16 = grad_pre.astype(bf16)
        middle_part = contract_last(grad_pre16, up16)
        grad_middle = grad_outer + (middle_part + partner(middle_part))
        up_term = contract_first(after_attend16, grad_pre16).astype(bf16)
        grad_inner = norm_back(grad_middle, norm_one, recip_one, gain_rows[0])
        grad_inner16 = grad_inner.astype(bf16)
        grad_context16 = contract_last(grad_inner16, output16).astype(bf16)
        block_output = from_sequences(final.astype(bf16), (grad_context16,))
        down_blocks = down_term.reshape(chips, planes, -1, width)
        down_sides = scatter_chips(
            (down_blocks[..., :half_width], down_blocks[..., half_width:]), chip, ((), (up_term,))
        )
        down_total = reduce_line(down_sides, plane, (grad_context16,))
        context_full = jnp.concatenate(
            [by_core(context16, other_context16), by_core(other_context16, context16)], axis=1
        )
        grad_half = by_core(grad_inner16[:, :half_width], grad_inner16[:, half_width:])
        output_term = contract_first(context_full, grad_half).astype(bf16)
        packed_grad = attend_backward(
            packed, context16, log_total, grad_context16, limits, half_width
        )
        up_blocks = up_term.reshape(chips, planes, -1, hidden_half)
        up_sides = scatter_chips(
            (up_blocks[..., : hidden_half // 2], up_blocks[..., hidden_half // 2 :]),
            chip,
            ((), (packed_grad,)),
        )
        up_total = reduce_line(up_sides, plane)
        project_term = contract_first(tokens16, packed_grad).astype(bf16)
        input_part = contract_last(packed_grad, project16)
        other_part = partner(input_part)
        input_sum = (grad_inner + (input_part + other_part)).astype(bf16)
        input_gradient = from_sequences(input_sum)

        packed_sum = jnp.sum(packed_grad.astype(f32), axis=0)
        edge = jnp.stack([packed_sum[:half_width], packed_sum[2 * half_width :]])
        blank = jnp.zeros_like(edge)
        edge = by_core(
            jnp.concatenate([edge, blank], axis=1), jnp.concatenate([blank, edge], axis=1)
        )
        wide_terms = jnp.stack(
            [
                jnp.sum(grad_middle * norm_one, axis=0),
                jnp.sum(upstream * norm_two, axis=0),
                jnp.sum(grad_inner, axis=0),
                jnp.sum(grad_middle, axis=0),
                jnp.sum(grad_outer, axis=0),
                jnp.sum(upstream, axis=0),
            ]
        )
        hidden_term = jnp.sum(grad_pre, axis=0).reshape(-1, width)
        small_terms = jnp.concatenate([edge, wide_terms, hidden_term], axis=0).astype(bf16)
        small_rows = round_up(small_terms.shape[0], 16)
        small_terms = jnp.pad(small_terms, ((0, small_rows - small_terms.shape[0]), (0, 0)))
        small_terms = jnp.broadcast_to(small_terms[None], (chips,) + small_terms.shape)
        project_blocks = project_term.reshape(chips, -1, 3 * half_width)
        output_blocks = output_term.reshape(chips, -1, half_width)
        attend_sides = scatter_chips(
            (
                jnp.concatenate([project_blocks[..., :width], small_terms], axis=1),
                jnp.concatenate([project_blocks[..., width:], output_blocks], axis=2),
            ),
            chip,
        )
        attend_sums = [flat(terms).astype(bf16) for terms in attend_sides]
        attend_totals = [along_line(own, plane) for own in attend_sums]

        def swap_halves(term, extra):
            parts = term.reshape(2, own_rows, -1)
            sent = pick(parts, 1 - core)
            if extra is not None:
                sent = jnp.concatenate([sent, extra], axis=0)
            other = partner(sent)
            kept = pick(parts, core)
            rest = other[own_rows:]
            other = other[:own_rows]
            return by_core(kept, other), by_core(other, kept), rest

        down_total = down_total.astype(f32)
        low, high, _ = swap_halves(up_total, None)
        up_total = join_columns(low, high, hidden_block).astype(f32)
        attend_term = jnp.concatenate([attend_totals[0][:chip_rows], attend_totals[1]], axis=1)
        own_small = attend_totals[0][chip_rows:]
        low, high, other_small = swap_halves(
            attend_term, jnp.pad(own_small, ((0, 0), (0, cut - width)))
        )
        project_total = join_columns(
            low[:, : 3 * half_width], high[:, : 3 * half_width], half_width
        ).astype(f32)
        output_total = jnp.concatenate(
            [low[:, 3 * half_width :], high[:, 3 * half_width :]], axis=1
        ).astype(f32)
        own_small = own_small.astype(f32)
        table_total = jnp.concatenate(
            [own_small[:2] + other_small[:2, :width].astype(f32), own_small[2:8]], axis=0
        )
        own_table = lax.dynamic_slice(table_total, (0, member * own_rows), (8, own_rows))
        hidden_total = lax.dynamic_slice(
            own_small[8 : 8 + hidden_half // width].reshape(-1),
            (chip * hidden_block,),
            (hidden_block,),
        )
        gains_total = own_table[2:4]
        biases_total = jnp.concatenate([own_table[:2], own_table[4:]], axis=0)
        totals = (
            project_total,
            output_total,
            up_total,
            down_total,
            gains_total,
            biases_total,
            hidden_total,
        )
        decay_flags = (True, True, True, True, False, False, False)
        results = []
        for n in range(7):
            results.append(adam_step(masters[n], firsts[n], seconds[n], totals[n], decay_flags[n]))
        return (
            (block_output, input_gradient)
            + totals
            + tuple(outcome[0] for outcome in results)
            + tuple(outcome[1] for outcome in results)
            + tuple(outcome[2] for outcome in results)
        )

    return shards


def solution(mesh):
    tokens = P("fsdp", "seq", None)
    rows = P("fsdp", None)
    columns = P(None, "fsdp")
    flat = P("fsdp")
    params = (rows, rows, rows, rows, columns, columns, flat)
    shards = make_shards(mesh.shape["seq"], mesh.shape["fsdp"])

    return jax.shard_map(
        shards,
        mesh=mesh,
        in_specs=(tokens, tokens, flat) + params * 3,
        out_specs=(tokens, tokens) + params * 4,
        check_vma=False,
    )
```
